128 devices in a mesh: fsdp: 64 (over x, y, z_lo, core), tp: 2 (over z_hi).
Axes of the slice: x: 4, y: 4, z: 4 (z_hi: 2, z_lo: 2; z = z_hi * 2 + z_lo), core: 2. Of those that a mesh axis runs over, the one named last changes fastest.
Arguments:
- inputs: float32 [25600, 768], P(('fsdp', 'tp')), may hold values from -6 to 6
- routes: int32 [25600, 2], P('fsdp'), may hold values from 0 to 15, all different within a row; in each aligned block of 400 rows (0 to 399, 400 to 799, ...) at most 63 rows name the same one
- attention_norm_gain: bfloat16 [768], P('fsdp'), may hold values from 0.099609375 to 1.8984375
- attention_norm_shift: bfloat16 [768], P('fsdp'), may hold values from -3 to 3
- qkv_weight: bfloat16 [3, 768, 768], P(None, 'fsdp', 'tp'), may hold values from -0.21875 to 0.21875
- proj_weight: bfloat16 [768, 768], P('tp', 'fsdp'), may hold values from -0.875 to 0.875
- expert_norm_gain: bfloat16 [768], P('fsdp'), may hold values from 0.099609375 to 1.8984375
- expert_norm_shift: bfloat16 [768], P('fsdp'), may hold values from -3 to 3
- router_weight: bfloat16 [768, 16], P('fsdp'), may hold values from -0.109375 to 0.109375
- expert_in: bfloat16 [768, 16, 3072], P('fsdp', None, 'tp'), may hold values from -0.21875 to 0.21875
- expert_out: bfloat16 [768, 16, 3072], P('fsdp', None, 'tp'), may hold values from -0.4375 to 0.4375
- cotangent: float32 [25600, 768], P(('fsdp', 'tp')), may hold values from -6 to 6
Outputs:
- outputs: float32 [25600, 768], P(('fsdp', 'tp'))
- input_grad: float32 [25600, 768], P(('fsdp', 'tp'))
- attn_gain_grad: float32 [768], P('fsdp')
- attn_shift_grad: float32 [768], P('fsdp')
- qkv_grad: float32 [3, 768, 768], P(None, 'fsdp', 'tp')
- proj_grad: float32 [768, 768], P('tp', 'fsdp')
- moe_gain_grad: float32 [768], P('fsdp')
- moe_shift_grad: float32 [768], P('fsdp')
- router_grad: float32 [768, 16], P('fsdp')
- expert_in_grad: float32 [768, 16, 3072], P('fsdp', None, 'tp')
- expert_out_grad: float32 [768, 16, 3072], P('fsdp', None, 'tp')
The draws below stay inside these ranges and needn't reach their ends.
Inputs may be any that keep to these rules, and one draw needn't show every extreme that they name: `routes`: in each aligned block of 400 rows (one routing group) the two experts of a row differ and no expert is named by more than 63 rows; some expert is named by exactly 63 rows of some block.
All inputs are finite; a program needn't handle non-finite values.
Results may differ from the reference program's by a relative error of at most 0.01.
Values may be sent and summed in bfloat16 or wider, within the bound.
A program may use at most 192 MiB of HBM per device.

```python
import math
import jax
import jax.numpy as jnp
import numpy as np
from jax import lax

D = 768
HEAD_DIM = 64
FF = 3072
EXPERTS = 16
SEQ = 200
REAL_TOK = 197
IMG_DEV = 2
TOK_FS = 400
CAP = 63
TOKENS = 25600


def block_scale(own_key, shape, cuts, smallest, top_value):
    factor_of = 1.0
    for axis_at, shards_of in cuts:
        steps = jax.random.uniform(jax.random.fold_in(jax.random.fold_in(own_key, 6), axis_at), (shards_of,), jnp.float32, smallest / len(cuts), top_value / len(cuts))
        factor_of = factor_of * jnp.repeat(jnp.exp(steps), shape[axis_at] // shards_of).reshape((-1,) + (1,) * (len(shape) - 1 - axis_at))
    return factor_of


def routed_block(stream_key, own, number, rows, number_of, top, reach, slope):
    sequence = jax.random.permutation(stream_key, number_of)
    packed, usual = load_shares(number_of, rows * top, reach, slope, True), load_shares(number_of, rows * top, reach, slope, False)
    places = jnp.arange(number_of)

    def named(lengths, turn):
        used = int((lengths > 0).sum())
        fixed = max(1, used // 4)
        passed = fixed + (places - fixed + turn * (used - fixed)) % max(1, number_of - fixed)
        return jnp.zeros((number_of,), jnp.int32).at[sequence[jnp.where(places < fixed, places, passed)]].set(jnp.asarray(lengths, jnp.int32))

    lengths = jnp.where(number % 4 == 0, named(packed, number // 4), named(usual, number - number // 4 - 1))
    mixed = jax.random.permutation(jax.random.fold_in(own, 3), number_of)
    donor, taker = mixed[0:number_of // 2 * 2:2], mixed[1:number_of // 2 * 2:2]
    margin = jnp.minimum(lengths[donor] - 1, reach - lengths[taker]) // 2
    margin = jnp.where((donor == sequence[0]) | (taker == sequence[0]) | (lengths[taker] == 0), 0, jnp.maximum(margin, 0))
    passed = jax.random.randint(jax.random.fold_in(own, 4), (number_of // 2,), 0, 1 << 20) % (margin + 1)
    lengths = lengths.at[donor].add(-passed).at[taker].add(passed)
    items = jnp.searchsorted(jnp.cumsum(lengths), jnp.arange(rows * top), side="right").astype(jnp.int32)
    listing = items.reshape(top, rows).T
    listing = listing[jax.random.permutation(jax.random.fold_in(own, 1), rows)]
    turn = jax.random.randint(jax.random.fold_in(own, 2), (rows, 1), 0, top)
    return jnp.take_along_axis(listing, (jnp.arange(top)[None, :] + turn) % top, axis=1)


def load_shares(count, total, bound, slope, full):
    loads = [(1 << 20) // math.isqrt(standing ** slope) + 1 for standing in range(1, count + 1)]
    largest = bound if full else min(bound, max(-(-total // count), total * loads[0] // sum(loads)))
    least = 1 if total - largest >= count - 1 else 0
    counts, surplus = [largest] + [least] * (count - 1), total - largest - least * (count - 1)
    while surplus > 0:
        movable = [i for i in range(1, count) if counts[i] < largest] or [i for i in range(1, count) if counts[i] < bound]
        mass, left = sum([loads[i] for i in movable]), surplus
        for i in movable:
            more = min(bound - counts[i], max(1, left * loads[i] // mass), surplus)
            counts[i] = counts[i] + more
            surplus = surplus - more
    return np.array(counts)


def scatter_about(key, extent, scale, bound, split=(), held_as=jnp.bfloat16):
    array = jax.random.normal(key, extent, jnp.float32) * scale
    if len(split) > 0:
        array = block_scale(key, extent, split, -0.22, 0.18) * array
    return jnp.clip(array, min=-bound, max=bound).astype(held_as)


def setup_inputs(seed: int = 0) -> dict:
    key_list = jax.random.split(jax.random.key(seed), 13)
    inputs = scatter_about(key_list[0], (TOKENS, D), 1.0, 6.0, ((0, 128),), jnp.float32)
    routes_keys = jax.random.split(jax.random.fold_in(key_list[1], 1), TOKENS // TOK_FS)
    routes_turns = jax.random.permutation(jax.random.fold_in(key_list[1], 3), TOKENS // TOK_FS)
    routes = jax.vmap(lambda own, number: routed_block(jax.random.fold_in(key_list[1], 2), own, number, TOK_FS, EXPERTS, 2, CAP, 2))(routes_keys, routes_turns).reshape((TOKENS, 2))
    attention_norm_gain = jnp.clip(1.0 + 0.18 * jax.random.normal(key_list[2], (D,), jnp.float32), 0.099609375, 1.8984375).astype(jnp.bfloat16)
    attention_norm_shift = scatter_about(key_list[3], (D,), 0.5, 3.0, ((0, 64),))
    qkv_weight = scatter_about(key_list[4], (3, D, D), D ** -0.5, 0.21875, ((1, 64), (2, 2)))
    proj_weight = scatter_about(key_list[5], (D, D), (D // 16) ** -0.5, 0.875, ((0, 2), (1, 64)))
    expert_norm_gain = jnp.clip(1.0 + 0.18 * jax.random.normal(key_list[6], (D,), jnp.float32), 0.099609375, 1.8984375).astype(jnp.bfloat16)
    expert_norm_shift = scatter_about(key_list[7], (D,), 0.5, 3.0, ((0, 64),))
    router_weight = scatter_about(key_list[8], (D, EXPERTS), (4 * D) ** -0.5, 0.109375, ((0, 64),))
    expert_in = scatter_about(key_list[9], (D, EXPERTS, FF), D ** -0.5, 0.21875, ((0, 64), (2, 2)))
    expert_out = scatter_about(key_list[10], (D, EXPERTS, FF), (FF // 16) ** -0.5, 0.4375, ((0, 64), (2, 2)))
    cotangent = scatter_about(key_list[11], (TOKENS, D), 1.0, 6.0, ((0, 128),), jnp.float32)
    return {"inputs": inputs, "routes": routes, "attention_norm_gain": attention_norm_gain, "attention_norm_shift": attention_norm_shift, "qkv_weight": qkv_weight, "proj_weight": proj_weight, "expert_norm_gain": expert_norm_gain, "expert_norm_shift": expert_norm_shift, "router_weight": router_weight, "expert_in": expert_in, "expert_out": expert_out, "cotangent": cotangent}


EPS = 1e-06
TOP = lax.Precision.HIGHEST

def widen(value):
    return lax.optimization_barrier(value).astype(jnp.float32)

def gelu_exact(value):
    return jax.nn.gelu(value, approximate=False)

def normalize_rows(value, norm_gain, norm_shift):
    row_mean = lax.optimization_barrier(jnp.mean(value, axis=-1, keepdims=True))
    centered_rows = value - row_mean
    inverse_deviation = lax.rsqrt(lax.optimization_barrier(jnp.mean(centered_rows * centered_rows, axis=-1, keepdims=True)) + EPS)
    standardized_rows = centered_rows * inverse_deviation
    normed_rows = (standardized_rows * norm_gain.astype(jnp.float32) + norm_shift.astype(jnp.float32)).astype(jnp.bfloat16)
    return (normed_rows, standardized_rows, inverse_deviation)

def norm_backward(incoming_gradient, standardized_rows, inverse_deviation, norm_gain):
    scaled_gradient = incoming_gradient * norm_gain.astype(jnp.float32)
    inner_product = scaled_gradient - lax.optimization_barrier(jnp.mean(scaled_gradient, axis=-1, keepdims=True)) - standardized_rows * lax.optimization_barrier(jnp.mean(scaled_gradient * standardized_rows, axis=-1, keepdims=True))
    return (inverse_deviation * inner_product, lax.optimization_barrier(jnp.sum(incoming_gradient * standardized_rows, axis=0)), lax.optimization_barrier(jnp.sum(incoming_gradient, axis=0)))

def slot_table(routes, experts, capacity):
    picked = (routes[:, :, None] == jnp.arange(experts, dtype=jnp.int32)[None, None, :]).astype(jnp.int32)
    flat = picked.reshape(-1, experts)
    before = (jnp.cumsum(flat, axis=0) - flat).astype(jnp.int32)
    number = lax.optimization_barrier(jnp.sum(before * flat, axis=-1)).astype(jnp.int32)
    slot = (routes.reshape(-1).astype(jnp.int32) * capacity + number).astype(jnp.int32)
    owner = jnp.arange(flat.shape[0], dtype=jnp.int32) // 2
    token_of_slot = jnp.zeros((experts * capacity,), jnp.int32).at[slot].set(owner)
    filled = jnp.zeros((experts * capacity,), jnp.int32).at[slot].set(1)
    return (picked, slot, token_of_slot, filled)

def split_heads(value, images):
    input_rows, width = value.shape
    return value.reshape(images, input_rows // images, width // HEAD_DIM, HEAD_DIM)

def live_keys(length):
    return (jnp.arange(length) < REAL_TOK)[None, None, None, :]

def attend(query, key, value, images):
    query_h = widen(split_heads(query, images))
    key_h = widen(split_heads(key, images))
    value_h = widen(split_heads(value, images))
    scores = jnp.einsum('ishd,ithd->ihst', query_h, key_h) * HEAD_DIM ** (-0.5)
    live = live_keys(scores.shape[-1])
    lse = jnp.log(lax.optimization_barrier(jnp.sum(jnp.where(live, jnp.exp(scores), 0.0), axis=-1, keepdims=True)))
    probs = jnp.where(live, jnp.exp(scores - lse), 0.0).astype(jnp.bfloat16)
    context = jnp.einsum('ihst,ithd->ishd', widen(probs), value_h).astype(jnp.bfloat16)
    return (context.reshape(query.shape), lse)

def attend_back(query, key, value, lse, context_grad, images):
    query_h = widen(split_heads(query, images))
    key_h = widen(split_heads(key, images))
    value_h = widen(split_heads(value, images))
    grad_h = widen(split_heads(context_grad, images))
    scores = jnp.einsum('ishd,ithd->ihst', query_h, key_h) * HEAD_DIM ** (-0.5)
    live = live_keys(scores.shape[-1])
    probs = jnp.where(live, jnp.exp(scores - lse), 0.0)
    value_grad = jnp.einsum('ihst,ishd->ithd', widen(probs.astype(jnp.bfloat16)), grad_h).astype(jnp.bfloat16)
    inner_product = jnp.einsum('ishd,ithd->ihst', grad_h, value_h)
    score_grad = (probs * (inner_product - lax.optimization_barrier(jnp.sum(probs * inner_product, axis=-1, keepdims=True))) * HEAD_DIM ** (-0.5)).astype(jnp.bfloat16)
    query_grad = jnp.einsum('ihst,ithd->ishd', widen(score_grad), key_h).astype(jnp.bfloat16)
    key_grad = jnp.einsum('ihst,ishd->ithd', widen(score_grad), query_h).astype(jnp.bfloat16)
    shape = query.shape
    return (query_grad.reshape(shape), key_grad.reshape(shape), value_grad.reshape(shape))

def reference(inputs, routes, attention_norm_gain, attention_norm_shift, qkv_weight, proj_weight, expert_norm_gain, expert_norm_shift, router_weight, expert_in, expert_out, cotangent):
    f32 = jnp.float32
    bf16 = jnp.bfloat16
    group = IMG_DEV * SEQ
    qkv_f = qkv_weight.astype(f32)
    proj_f = proj_weight.astype(f32)
    router_f = router_weight.astype(f32)
    in_f = expert_in.astype(f32)
    out_f = expert_out.astype(f32)

    def one_group(totals, pieces):
        input_rows, cot, picks = pieces
        attention_normed, attention_standardized, attention_inverse_deviation = normalize_rows(input_rows, attention_norm_gain, attention_norm_shift)
        proj = jnp.einsum('td,idh->ith', widen(attention_normed), qkv_f).astype(bf16)
        context, lse = attend(proj[0], proj[1], proj[2], IMG_DEV)
        residual_middle = input_rows + jnp.einsum('th,hd->td', widen(context), proj_f)
        expert_normed, expert_standardized, expert_inverse_deviation = normalize_rows(residual_middle, expert_norm_gain, expert_norm_shift)
        logits = jnp.einsum('td,de->te', widen(expert_normed), router_f)
        raised = jnp.exp(logits)
        probs = raised / lax.optimization_barrier(jnp.sum(raised, axis=-1, keepdims=True))
        picked, slot, token_of_slot, filled = slot_table(picks, EXPERTS, CAP)
        gates = lax.optimization_barrier(jnp.sum(picked.astype(f32) * probs[:, None, :], axis=-1))
        slotted = jnp.where(filled[:, None] > 0, expert_normed[token_of_slot], jnp.zeros((), bf16)).reshape(EXPERTS, CAP, D)
        hidden_pre = jnp.einsum('ecd,def->ecf', widen(slotted), in_f)
        hidden = gelu_exact(hidden_pre).astype(bf16)
        expert_res = jnp.einsum('ecf,def->ecd', widen(hidden), out_f)
        routed = expert_res.reshape(EXPERTS * CAP, D)[slot].reshape(group, 2, D)
        outputs = residual_middle + lax.optimization_barrier(jnp.sum(gates[:, :, None] * routed, axis=1))
        dout = cot.astype(bf16)
        dout_f = widen(dout)
        gate_of_slot = jnp.zeros((EXPERTS * CAP,), f32).at[slot].set(gates.reshape(-1))
        slot_grad = jnp.where(filled[:, None] > 0, gate_of_slot[:, None] * dout_f[token_of_slot], 0.0).astype(bf16).reshape(EXPERTS, CAP, D)
        gate_grad = lax.optimization_barrier(jnp.sum(dout_f[:, None, :] * routed, axis=-1))
        hidden_grad = jnp.einsum('ecd,def->ecf', widen(slot_grad), out_f)
        pre_grad = jax.vjp(gelu_exact, hidden_pre)[1](hidden_grad)[0].astype(bf16)
        slot_in_grad = jnp.einsum('ecf,def->ecd', widen(pre_grad), in_f)
        in_term = jnp.einsum('ecd,ecf->def', widen(slotted), widen(pre_grad))
        out_term = jnp.einsum('ecd,ecf->def', widen(slot_grad), widen(hidden))
        choice_grad = lax.optimization_barrier(jnp.sum(picked.astype(f32) * gate_grad[:, :, None], axis=1))
        logit_grad = probs * (choice_grad - lax.optimization_barrier(jnp.sum(probs * choice_grad, axis=-1, keepdims=True)))
        router_term = jnp.einsum('td,te->de', widen(expert_normed), logit_grad, precision=TOP)
        routed_in = slot_in_grad.reshape(EXPERTS * CAP, D)[slot].reshape(group, 2, D)
        expert_input_gradient = lax.optimization_barrier(jnp.sum(routed_in, axis=1)) + jnp.einsum('te,de->td', logit_grad, router_f, precision=TOP)
        expert_norm_backward, expert_gain_piece, expert_shift_piece = norm_backward(expert_input_gradient, expert_standardized, expert_inverse_deviation, expert_norm_gain)
        middle_grad = cot + expert_norm_backward
        mid_b = middle_grad.astype(bf16)
        proj_term = jnp.einsum('th,td->hd', widen(context), widen(mid_b))
        context_grad = jnp.einsum('td,hd->th', widen(mid_b), proj_f).astype(bf16)
        query_grad, key_grad, value_grad = attend_back(proj[0], proj[1], proj[2], lse, context_grad, IMG_DEV)
        stacked = jnp.stack([query_grad, key_grad, value_grad])
        qkv_term = jnp.einsum('td,ith->idh', widen(attention_normed), widen(stacked))
        attention_input_gradient = jnp.einsum('ith,idh->td', widen(stacked), qkv_f)
        attention_norm_backward, attention_gain_piece, attention_shift_piece = norm_backward(attention_input_gradient, attention_standardized, attention_inverse_deviation, attention_norm_gain)
        input_grad = middle_grad + attention_norm_backward
        terms = (attention_gain_piece, attention_shift_piece, qkv_term, proj_term, expert_gain_piece, expert_shift_piece, router_term, in_term, out_term)
        totals = jax.tree.map(lambda left, right: left + right, totals, terms)
        return (totals, (outputs, input_grad))
    count = inputs.shape[0] // group
    pieces = (inputs.reshape(count, group, D), cotangent.reshape(count, group, D), routes.reshape(count, group, 2))
    start = (jnp.zeros((D,), f32), jnp.zeros((D,), f32), jnp.zeros((3, D, D), f32), jnp.zeros((D, D), f32), jnp.zeros((D,), f32), jnp.zeros((D,), f32), jnp.zeros((D, EXPERTS), f32), jnp.zeros((D, EXPERTS, FF), f32), jnp.zeros((D, EXPERTS, FF), f32))
    totals, (outs, grads) = lax.scan(one_group, start, pieces)
    return (outs.reshape(-1, D), grads.reshape(-1, D), totals[0], totals[1], totals[2], totals[3], totals[4], totals[5], totals[6], totals[7], totals[8])
```

```python
import jax
import jax.numpy as jnp
from jax import lax
from jax.sharding import PartitionSpec as P

HEAD_DIM = 64
SEQ = 200
REAL_TOK = 197
CAP = 63


EPS = 1e-06
TOP = lax.Precision.HIGHEST


def gelu_exact(value):
    return jax.nn.gelu(value, approximate=False)


def normalize_rows(value, norm_gain, norm_shift):
    row_mean = jnp.mean(value, axis=-1, keepdims=True)
    centered_rows = value - row_mean
    inverse_deviation = lax.rsqrt(
        jnp.mean(centered_rows * centered_rows, axis=-1, keepdims=True) + EPS
    )
    standardized_rows = centered_rows * inverse_deviation
    normed_rows = (
        standardized_rows * norm_gain.astype(jnp.float32) + norm_shift.astype(jnp.float32)
    ).astype(jnp.bfloat16)
    return (normed_rows, standardized_rows, inverse_deviation)


def norm_backward(incoming_gradient, standardized_rows, inverse_deviation, norm_gain):
    scaled_gradient = incoming_gradient * norm_gain.astype(jnp.float32)
    inner_product = (
        scaled_gradient
        - jnp.mean(scaled_gradient, axis=-1, keepdims=True)
        - standardized_rows * jnp.mean(scaled_gradient * standardized_rows, axis=-1, keepdims=True)
    )
    return (
        inverse_deviation * inner_product,
        jnp.sum(incoming_gradient * standardized_rows, axis=0),
        jnp.sum(incoming_gradient, axis=0),
    )


def slot_table(routes, experts, capacity):
    picked = (routes[:, :, None] == jnp.arange(experts, dtype=jnp.int32)[None, None, :]).astype(
        jnp.int32
    )
    flat = picked.reshape(-1, experts)
    before = jnp.cumsum(flat, axis=0) - flat
    number = jnp.sum(before * flat, axis=-1)
    slot = routes.reshape(-1) * capacity + number
    owner = jnp.arange(flat.shape[0], dtype=jnp.int32) // 2
    token_of_slot = jnp.zeros((experts * capacity,), jnp.int32).at[slot].set(owner)
    filled = jnp.zeros((experts * capacity,), jnp.int32).at[slot].set(1)
    return (picked, slot, token_of_slot, filled)


def split_heads(value, images):
    input_rows, width = value.shape
    return value.reshape(images, input_rows // images, width // HEAD_DIM, HEAD_DIM)


def live_keys(length):
    return (jnp.arange(length) < REAL_TOK)[None, None, None, :]


def attend(query, key, value, images):
    query_h = split_heads(query, images)
    key_h = split_heads(key, images)
    value_h = split_heads(value, images)
    scores = jnp.einsum(
        "ishd,ithd->ihst", query_h, key_h, preferred_element_type=jnp.float32
    ) * HEAD_DIM ** (-0.5)
    live = live_keys(scores.shape[-1])
    lse = jnp.log(jnp.sum(jnp.where(live, jnp.exp(scores), 0.0), axis=-1, keepdims=True))
    probs = jnp.where(live, jnp.exp(scores - lse), 0.0).astype(jnp.bfloat16)
    context = jnp.einsum(
        "ihst,ithd->ishd", probs, value_h, preferred_element_type=jnp.float32
    ).astype(jnp.bfloat16)
    return (context.reshape(query.shape), lse)


def attend_back(query, key, value, lse, context_grad, images):
    query_h = split_heads(query, images)
    key_h = split_heads(key, images)
    value_h = split_heads(value, images)
    grad_h = split_heads(context_grad, images)
    scores = jnp.einsum(
        "ishd,ithd->ihst", query_h, key_h, preferred_element_type=jnp.float32
    ) * HEAD_DIM ** (-0.5)
    live = live_keys(scores.shape[-1])
    probs = jnp.where(live, jnp.exp(scores - lse), 0.0)
    value_grad = jnp.einsum(
        "ihst,ishd->ithd", probs.astype(jnp.bfloat16), grad_h, preferred_element_type=jnp.float32
    ).astype(jnp.bfloat16)
    inner_product = jnp.einsum(
        "ishd,ithd->ihst", grad_h, value_h, preferred_element_type=jnp.float32
    )
    score_grad = (
        probs
        * (inner_product - jnp.sum(probs * inner_product, axis=-1, keepdims=True))
        * HEAD_DIM ** (-0.5)
    ).astype(jnp.bfloat16)
    query_grad = jnp.einsum(
        "ihst,ithd->ishd", score_grad, key_h, preferred_element_type=jnp.float32
    ).astype(jnp.bfloat16)
    key_grad = jnp.einsum(
        "ihst,ishd->ithd", score_grad, query_h, preferred_element_type=jnp.float32
    ).astype(jnp.bfloat16)
    shape = query.shape
    return (query_grad.reshape(shape), key_grad.reshape(shape), value_grad.reshape(shape))


def gather_dense(
    qkv_weight,
    proj_weight,
    router_weight,
    attention_norm_gain,
    attention_norm_shift,
    expert_norm_gain,
    expert_norm_shift,
):
    rows = qkv_weight.shape[1]
    heads_width = qkv_weight.shape[2]
    experts = router_weight.shape[1]
    packed = jnp.concatenate(
        [
            jnp.transpose(qkv_weight, (1, 0, 2)).reshape(rows, -1),
            proj_weight.T,
            router_weight,
            jnp.stack(
                [attention_norm_gain, attention_norm_shift, expert_norm_gain, expert_norm_shift],
                axis=1,
            ),
        ],
        axis=1,
    )
    full = lax.all_gather(packed, "fsdp", axis=0, tiled=True)
    width = full.shape[0]
    at = 3 * heads_width
    qkv_full = jnp.transpose(full[:, :at].reshape(width, 3, heads_width), (1, 0, 2))
    proj_full = full[:, at : at + heads_width].T
    at += heads_width
    router_full = full[:, at : at + experts]
    at += experts
    norms = full[:, at : at + 4]
    return (qkv_full, proj_full, router_full, norms[:, 0], norms[:, 1], norms[:, 2], norms[:, 3])


def reduce_dense(qkv_part, proj_part, router_part, norm_parts):
    width = qkv_part.shape[1]
    heads_width = qkv_part.shape[2]
    experts = router_part.shape[1]
    packed = jnp.concatenate(
        [
            jnp.transpose(qkv_part, (1, 0, 2)).reshape(width, -1),
            proj_part.T,
            router_part,
            jnp.stack(norm_parts, axis=1),
        ],
        axis=1,
    )
    part = lax.psum_scatter(packed, "fsdp", scatter_dimension=0, tiled=True)
    rows = part.shape[0]
    at = 3 * heads_width
    qkv_grad = jnp.transpose(part[:, :at].reshape(rows, 3, heads_width), (1, 0, 2))
    proj_grad = part[:, at : at + heads_width].T
    at += heads_width
    shared = lax.psum(part[:, at:], "tp")
    router_grad = shared[:, :experts]
    norm_grads = [shared[:, experts + i] for i in range(len(norm_parts))]
    return qkv_grad, proj_grad, router_grad, norm_grads


def group_rows(value):
    return lax.all_gather(value, "tp", axis=0, tiled=True)


def owned_rows(value):
    return lax.psum_scatter(value, "tp", scatter_dimension=0, tiled=True)


def to_owners(slots, holders):
    experts, capacity, width = slots.shape
    spread = jnp.broadcast_to(slots[:, None], (experts, holders, capacity, width)).reshape(
        experts * holders, capacity, width
    )
    moved = lax.all_to_all(spread, "fsdp", split_axis=0, concat_axis=0, tiled=True)
    return moved.reshape(-1, width)


def to_groups(partial_value, experts, holders, capacity):
    width = partial_value.shape[1]
    pieces = partial_value.reshape(experts * holders, capacity, width)
    moved = lax.all_to_all(pieces, "fsdp", split_axis=0, concat_axis=0, tiled=True)
    return jnp.sum(moved.reshape(experts, holders, capacity, width), axis=1)


def per_device(
    inputs,
    routes,
    attention_norm_gain,
    attention_norm_shift,
    qkv_weight,
    proj_weight,
    expert_norm_gain,
    expert_norm_shift,
    router_weight,
    expert_in,
    expert_out,
    cotangent,
):
    f32 = jnp.float32
    bf16 = jnp.bfloat16
    dense = gather_dense(
        qkv_weight,
        proj_weight,
        router_weight,
        attention_norm_gain,
        attention_norm_shift,
        expert_norm_gain,
        expert_norm_shift,
    )
    qkv_full, proj_full, router_full, attention_gain, attention_shift, expert_gain, expert_shift = (
        dense
    )
    group = routes.shape[0]
    images = group // SEQ
    experts = router_full.shape[1]
    width = qkv_full.shape[1]
    units = expert_in.shape[2]
    local_rows = expert_in.shape[0]
    holders = lax.axis_size("fsdp") // experts
    block_units = units // holders
    attention_normed, attention_standardized, attention_inverse_deviation = normalize_rows(
        inputs, attention_gain, attention_shift
    )
    tokens_a = group_rows(attention_normed)
    proj = jnp.einsum("td,idh->ith", tokens_a, qkv_full, preferred_element_type=f32).astype(bf16)
    context, lse = attend(proj[0], proj[1], proj[2], images)
    residual_middle = inputs + owned_rows(jnp.dot(context, proj_full, preferred_element_type=f32))
    expert_normed, expert_standardized, expert_inverse_deviation = normalize_rows(
        residual_middle, expert_gain, expert_shift
    )
    tokens_m = group_rows(expert_normed)
    logits = jnp.dot(tokens_m, router_full, preferred_element_type=f32)
    raised = jnp.exp(logits)
    probs = raised / jnp.sum(raised, axis=-1, keepdims=True)
    picked, slot, token_of_slot, filled = slot_table(routes, experts, CAP)
    gates = jnp.sum(picked.astype(f32) * probs[:, None, :], axis=-1)
    slotted = jnp.where(filled[:, None] > 0, tokens_m[token_of_slot], jnp.zeros((), bf16)).reshape(
        experts, CAP, width
    )
    regroup_in = expert_in.reshape(local_rows, experts * holders, block_units)
    regroup_out = expert_out.reshape(local_rows, experts * holders, block_units)
    own_in, own_out = (
        lax.all_to_all(regroup_in, "fsdp", split_axis=1, concat_axis=0, tiled=True),
        lax.all_to_all(regroup_out, "fsdp", split_axis=1, concat_axis=0, tiled=True),
    )
    own_in = own_in.reshape(width, block_units)
    own_out = own_out.reshape(width, block_units)
    owner_x = to_owners(slotted, holders)
    owner_pre = jnp.dot(owner_x, own_in, preferred_element_type=f32)
    owner_hidden = gelu_exact(owner_pre).astype(bf16)
    owner_res = jnp.einsum("cf,df->cd", owner_hidden, own_out, preferred_element_type=f32)
    expert_res = to_groups(owner_res, experts, holders, CAP)
    routed = expert_res.reshape(experts * CAP, width)[slot].reshape(group, 2, width)
    outputs = residual_middle + owned_rows(jnp.sum(gates[:, :, None] * routed, axis=1))
    qkv_back, proj_back, router_back = qkv_full, proj_full, router_full
    attention_gain_gradient, expert_gain_gradient = attention_gain, expert_gain
    dout = group_rows(cotangent.astype(bf16))
    dout_f = dout.astype(f32)
    gate_of_slot = jnp.zeros((experts * CAP,), f32).at[slot].set(gates.reshape(-1))
    slot_grad = (
        jnp.where(filled[:, None] > 0, gate_of_slot[:, None] * dout_f[token_of_slot], 0.0)
        .astype(bf16)
        .reshape(experts, CAP, width)
    )
    gate_grad = jnp.sum(dout_f[:, None, :] * routed, axis=-1)
    owner_g = to_owners(slot_grad, holders)
    owner_hgrad = jnp.dot(owner_g, own_out, preferred_element_type=f32)
    owner_pgrad = jax.vjp(gelu_exact, owner_pre)[1](owner_hgrad)[0].astype(bf16)
    owner_back = jnp.einsum("cf,df->cd", owner_pgrad, own_in, preferred_element_type=f32)
    slot_in_grad = to_groups(owner_back, experts, holders, CAP)
    in_local = jnp.einsum("cd,cf->df", owner_x, owner_pgrad, preferred_element_type=f32)
    out_local = jnp.einsum("cd,cf->df", owner_g, owner_hidden, preferred_element_type=f32)
    in_home, out_home = (
        lax.all_to_all(
            in_local.reshape(width, 1, block_units).astype(jnp.bfloat16),
            "fsdp",
            split_axis=0,
            concat_axis=1,
            tiled=True,
        ).astype(jnp.float32),
        lax.all_to_all(
            out_local.reshape(width, 1, block_units).astype(jnp.bfloat16),
            "fsdp",
            split_axis=0,
            concat_axis=1,
            tiled=True,
        ).astype(jnp.float32),
    )
    in_grad = in_home.reshape(local_rows, experts, units)
    out_grad = out_home.reshape(local_rows, experts, units)
    choice_grad = jnp.sum(picked.astype(f32) * gate_grad[:, :, None], axis=1)
    logit_grad = probs * (choice_grad - jnp.sum(probs * choice_grad, axis=-1, keepdims=True))
    router_part = jnp.einsum("td,te->de", tokens_m.astype(f32), logit_grad, precision=TOP)
    routed_in = slot_in_grad.reshape(experts * CAP, width)[slot].reshape(group, 2, width)
    token_gradient = jnp.sum(routed_in, axis=1) + jnp.einsum(
        "te,de->td", logit_grad, router_back.astype(f32), precision=TOP
    )
    expert_norm_backward, expert_gain_partial, expert_shift_partial = norm_backward(
        owned_rows(token_gradient),
        expert_standardized,
        expert_inverse_deviation,
        expert_gain_gradient,
    )
    middle_grad = cotangent + expert_norm_backward
    mid_rows = group_rows(middle_grad.astype(bf16))
    proj_part = jnp.einsum("th,td->hd", context, mid_rows, preferred_element_type=f32)
    context_grad = jnp.einsum("td,hd->th", mid_rows, proj_back, preferred_element_type=f32).astype(
        bf16
    )
    query_grad, key_grad, value_grad = attend_back(
        proj[0], proj[1], proj[2], lse, context_grad, images
    )
    stacked = jnp.stack([query_grad, key_grad, value_grad])
    qkv_part = jnp.einsum("td,ith->idh", tokens_a, stacked, preferred_element_type=f32)
    attention_input_gradient = owned_rows(
        jnp.einsum("ith,idh->td", stacked, qkv_back, preferred_element_type=f32)
    )
    attention_norm_backward, attention_gain_partial, attention_shift_partial = norm_backward(
        attention_input_gradient,
        attention_standardized,
        attention_inverse_deviation,
        attention_gain_gradient,
    )
    input_grad = middle_grad + attention_norm_backward
    qkv_grad, proj_grad, router_grad, norm_grads = reduce_dense(
        qkv_part,
        proj_part,
        router_part,
        [attention_gain_partial, attention_shift_partial, expert_gain_partial, expert_shift_partial],
    )
    return (
        outputs,
        input_grad,
        norm_grads[0],
        norm_grads[1],
        qkv_grad,
        proj_grad,
        norm_grads[2],
        norm_grads[3],
        router_grad,
        in_grad,
        out_grad,
    )


def solution(mesh):
    return jax.shard_map(
        per_device,
        mesh=mesh,
        in_specs=(
            P(("fsdp", "tp"), None),
            P("fsdp", None),
            P("fsdp"),
            P("fsdp"),
            P(None, "fsdp", "tp"),
            P("tp", "fsdp"),
            P("fsdp"),
            P("fsdp"),
            P("fsdp", None),
            P("fsdp", None, "tp"),
            P("fsdp", None, "tp"),
            P(("fsdp", "tp"), None),
        ),
        out_specs=(
            P(("fsdp", "tp"), None),
            P(("fsdp", "tp"), None),
            P("fsdp"),
            P("fsdp"),
            P(None, "fsdp", "tp"),
            P("tp", "fsdp"),
            P("fsdp"),
            P("fsdp"),
            P("fsdp", None),
            P("fsdp", None, "tp"),
            P("fsdp", None, "tp"),
        ),
        check_vma=False,
    )
```

```python
import jax
import jax.numpy as jnp
from jax import lax
from jax.sharding import PartitionSpec as P

HEAD_DIM = 64
SEQ = 200
REAL_TOK = 197
CAP = 63


EPS = 1e-06
TOP = lax.Precision.HIGHEST


def gelu_exact(value):
    return jax.nn.gelu(value, approximate=False)


def normalize_rows(value, norm_gain, norm_shift):
    row_mean = jnp.mean(value, axis=-1, keepdims=True)
    centered_rows = value - row_mean
    inverse_deviation = lax.rsqrt(
        jnp.mean(centered_rows * centered_rows, axis=-1, keepdims=True) + EPS
    )
    standardized_rows = centered_rows * inverse_deviation
    normed_rows = (
        standardized_rows * norm_gain.astype(jnp.float32) + norm_shift.astype(jnp.float32)
    ).astype(jnp.bfloat16)
    return (normed_rows, standardized_rows, inverse_deviation)


def norm_backward(incoming_gradient, standardized_rows, inverse_deviation, norm_gain):
    scaled_gradient = incoming_gradient * norm_gain.astype(jnp.float32)
    inner_product = (
        scaled_gradient
        - jnp.mean(scaled_gradient, axis=-1, keepdims=True)
        - standardized_rows * jnp.mean(scaled_gradient * standardized_rows, axis=-1, keepdims=True)
    )
    return (
        inverse_deviation * inner_product,
        jnp.sum(incoming_gradient * standardized_rows, axis=0),
        jnp.sum(incoming_gradient, axis=0),
    )


def slot_table(routes, experts, capacity):
    picked = (routes[:, :, None] == jnp.arange(experts, dtype=jnp.int32)[None, None, :]).astype(
        jnp.int32
    )
    flat = picked.reshape(-1, experts)
    before = jnp.cumsum(flat, axis=0) - flat
    number = jnp.sum(before * flat, axis=-1)
    slot = routes.reshape(-1) * capacity + number
    owner = jnp.arange(flat.shape[0], dtype=jnp.int32) // 2
    token_of_slot = jnp.zeros((experts * capacity,), jnp.int32).at[slot].set(owner)
    filled = jnp.zeros((experts * capacity,), jnp.int32).at[slot].set(1)
    return (picked, slot, token_of_slot, filled)


def split_heads(value, images):
    input_rows, width = value.shape
    return value.reshape(images, input_rows // images, width // HEAD_DIM, HEAD_DIM)


def live_keys(length):
    return (jnp.arange(length) < REAL_TOK)[None, None, None, :]


def attend(query, key, value, images):
    query_h = split_heads(query, images)
    key_h = split_heads(key, images)
    value_h = split_heads(value, images)
    scores = jnp.einsum(
        "ishd,ithd->ihst", query_h, key_h, preferred_element_type=jnp.float32
    ) * HEAD_DIM ** (-0.5)
    live = live_keys(scores.shape[-1])
    lse = jnp.log(jnp.sum(jnp.where(live, jnp.exp(scores), 0.0), axis=-1, keepdims=True))
    probs = jnp.where(live, jnp.exp(scores - lse), 0.0).astype(jnp.bfloat16)
    context = jnp.einsum(
        "ihst,ithd->ishd", probs, value_h, preferred_element_type=jnp.float32
    ).astype(jnp.bfloat16)
    return (context.reshape(query.shape), lse)


def attend_back(query, key, value, lse, context_grad, images):
    query_h = split_heads(query, images)
    key_h = split_heads(key, images)
    value_h = split_heads(value, images)
    grad_h = split_heads(context_grad, images)
    scores = jnp.einsum(
        "ishd,ithd->ihst", query_h, key_h, preferred_element_type=jnp.float32
    ) * HEAD_DIM ** (-0.5)
    live = live_keys(scores.shape[-1])
    probs = jnp.where(live, jnp.exp(scores - lse), 0.0)
    value_grad = jnp.einsum(
        "ihst,ishd->ithd", probs.astype(jnp.bfloat16), grad_h, preferred_element_type=jnp.float32
    ).astype(jnp.bfloat16)
    inner_product = jnp.einsum(
        "ishd,ithd->ihst", grad_h, value_h, preferred_element_type=jnp.float32
    )
    score_grad = (
        probs
        * (inner_product - jnp.sum(probs * inner_product, axis=-1, keepdims=True))
        * HEAD_DIM ** (-0.5)
    ).astype(jnp.bfloat16)
    query_grad = jnp.einsum(
        "ihst,ithd->ishd", score_grad, key_h, preferred_element_type=jnp.float32
    ).astype(jnp.bfloat16)
    key_grad = jnp.einsum(
        "ihst,ishd->ithd", score_grad, query_h, preferred_element_type=jnp.float32
    ).astype(jnp.bfloat16)
    shape = query.shape
    return (query_grad.reshape(shape), key_grad.reshape(shape), value_grad.reshape(shape))


def gather_dense(
    qkv_weight,
    proj_weight,
    router_weight,
    attention_norm_gain,
    attention_norm_shift,
    expert_norm_gain,
    expert_norm_shift,
):
    rows = qkv_weight.shape[1]
    heads_width = qkv_weight.shape[2]
    experts = router_weight.shape[1]
    packed = jnp.concatenate(
        [
            jnp.transpose(qkv_weight, (1, 0, 2)).reshape(rows, -1),
            proj_weight.T,
            router_weight,
            jnp.stack(
                [attention_norm_gain, attention_norm_shift, expert_norm_gain, expert_norm_shift],
                axis=1,
            ),
        ],
        axis=1,
    )
    full = lax.all_gather(packed, "fsdp", axis=0, tiled=True)
    width = full.shape[0]
    at = 3 * heads_width
    qkv_full = jnp.transpose(full[:, :at].reshape(width, 3, heads_width), (1, 0, 2))
    proj_full = full[:, at : at + heads_width].T
    at += heads_width
    router_full = full[:, at : at + experts]
    at += experts
    norms = full[:, at : at + 4]
    return (qkv_full, proj_full, router_full, norms[:, 0], norms[:, 1], norms[:, 2], norms[:, 3])


def reduce_dense(qkv_part, proj_part, router_part, norm_parts):
    width = qkv_part.shape[1]
    heads_width = qkv_part.shape[2]
    experts = router_part.shape[1]
    packed = jnp.concatenate(
        [
            jnp.transpose(qkv_part, (1, 0, 2)).reshape(width, -1),
            proj_part.T,
            router_part,
            jnp.stack(norm_parts, axis=1),
        ],
        axis=1,
    )
    holders = lax.axis_size("fsdp")
    rows = width // holders
    part = lax.psum_scatter(
        packed.reshape(holders, rows, packed.shape[1]), "fsdp", scatter_dimension=0, tiled=True
    ).reshape(rows, packed.shape[1])
    at = 3 * heads_width
    qkv_grad = jnp.transpose(part[:, :at].reshape(rows, 3, heads_width), (1, 0, 2))
    proj_grad = part[:, at : at + heads_width].T
    at += heads_width
    shared = lax.psum(part[:, at:], "tp")
    router_grad = shared[:, :experts]
    norm_grads = [shared[:, experts + i] for i in range(len(norm_parts))]
    return qkv_grad, proj_grad, router_grad, norm_grads


def group_rows(value):
    return lax.all_gather(value, "tp", axis=0, tiled=True)


def owned_rows(value):
    return lax.psum_scatter(value, "tp", scatter_dimension=0, tiled=True)


def to_owners(slots, holders):
    experts, capacity, width = slots.shape
    spread = jnp.broadcast_to(slots[:, None], (experts, holders, capacity, width)).reshape(
        experts * holders, capacity, width
    )
    moved = lax.all_to_all(spread, "fsdp", split_axis=0, concat_axis=0, tiled=True)
    return moved.reshape(-1, width)


def to_groups(partial_value, experts, holders, capacity):
    width = partial_value.shape[1]
    pieces = partial_value.astype(jnp.bfloat16).reshape(experts * holders, capacity, width)
    moved = lax.all_to_all(pieces, "fsdp", split_axis=0, concat_axis=0, tiled=True)
    return jnp.sum(moved.reshape(experts, holders, capacity, width).astype(jnp.float32), axis=1)


def per_device(
    inputs,
    routes,
    attention_norm_gain,
    attention_norm_shift,
    qkv_weight,
    proj_weight,
    expert_norm_gain,
    expert_norm_shift,
    router_weight,
    expert_in,
    expert_out,
    cotangent,
):
    f32 = jnp.float32
    bf16 = jnp.bfloat16
    dense = gather_dense(
        qkv_weight,
        proj_weight,
        router_weight,
        attention_norm_gain,
        attention_norm_shift,
        expert_norm_gain,
        expert_norm_shift,
    )
    qkv_full, proj_full, router_full, attention_gain, attention_shift, expert_gain, expert_shift = (
        dense
    )
    group = routes.shape[0]
    images = group // SEQ
    experts = router_full.shape[1]
    width = qkv_full.shape[1]
    units = expert_in.shape[2]
    local_rows = expert_in.shape[0]
    holders = lax.axis_size("fsdp") // experts
    block_units = units // holders
    attention_normed, attention_standardized, attention_inverse_deviation = normalize_rows(
        inputs, attention_gain, attention_shift
    )
    tokens_a = group_rows(attention_normed)
    proj = jnp.einsum("td,idh->ith", tokens_a, qkv_full, preferred_element_type=f32).astype(bf16)
    context, lse = attend(proj[0], proj[1], proj[2], images)
    residual_middle = inputs + owned_rows(jnp.dot(context, proj_full, preferred_element_type=f32))
    expert_normed, expert_standardized, expert_inverse_deviation = normalize_rows(
        residual_middle, expert_gain, expert_shift
    )
    tokens_m = group_rows(expert_normed)
    logits = jnp.dot(tokens_m, router_full, preferred_element_type=f32)
    raised = jnp.exp(logits)
    probs = raised / jnp.sum(raised, axis=-1, keepdims=True)
    picked, slot, token_of_slot, filled = slot_table(routes, experts, CAP)
    gates = jnp.sum(picked.astype(f32) * probs[:, None, :], axis=-1)
    slotted = jnp.where(filled[:, None] > 0, tokens_m[token_of_slot], jnp.zeros((), bf16)).reshape(
        experts, CAP, width
    )
    regroup_in = expert_in.reshape(local_rows, experts * holders, block_units)
    regroup_out = expert_out.reshape(local_rows, experts * holders, block_units)
    own_in, own_out = (
        lax.all_to_all(regroup_in, "fsdp", split_axis=1, concat_axis=0, tiled=True),
        lax.all_to_all(regroup_out, "fsdp", split_axis=1, concat_axis=0, tiled=True),
    )
    own_in = own_in.reshape(width, block_units)
    own_out = own_out.reshape(width, block_units)
    owner_x = to_owners(slotted, holders)
    owner_pre = jnp.dot(owner_x, own_in, preferred_element_type=f32)
    owner_hidden = gelu_exact(owner_pre).astype(bf16)
    owner_res = jnp.einsum("cf,df->cd", owner_hidden, own_out, preferred_element_type=f32)
    expert_res = to_groups(owner_res, experts, holders, CAP)
    routed = expert_res.reshape(experts * CAP, width)[slot].reshape(group, 2, width)
    outputs = residual_middle + owned_rows(jnp.sum(gates[:, :, None] * routed, axis=1))
    qkv_back, proj_back, router_back = qkv_full, proj_full, router_full
    attention_gain_gradient, expert_gain_gradient = attention_gain, expert_gain
    dout = group_rows(cotangent.astype(bf16))
    dout_f = dout.astype(f32)
    gate_of_slot = jnp.zeros((experts * CAP,), f32).at[slot].set(gates.reshape(-1))
    slot_grad = (
        jnp.where(filled[:, None] > 0, gate_of_slot[:, None] * dout_f[token_of_slot], 0.0)
        .astype(bf16)
        .reshape(experts, CAP, width)
    )
    gate_grad = jnp.sum(dout_f[:, None, :] * routed, axis=-1)
    owner_g = to_owners(slot_grad, holders)
    owner_hgrad = jnp.dot(owner_g, own_out, preferred_element_type=f32)
    owner_pgrad = jax.vjp(gelu_exact, owner_pre)[1](owner_hgrad)[0].astype(bf16)
    owner_back = jnp.einsum("cf,df->cd", owner_pgrad, own_in, preferred_element_type=f32)
    slot_in_grad = to_groups(owner_back, experts, holders, CAP)
    in_local = jnp.einsum("cd,cf->df", owner_x, owner_pgrad, preferred_element_type=f32)
    out_local = jnp.einsum("cd,cf->df", owner_g, owner_hidden, preferred_element_type=f32)
    in_home, out_home = (
        lax.all_to_all(
            in_local.reshape(width, 1, block_units).astype(jnp.bfloat16),
            "fsdp",
            split_axis=0,
            concat_axis=1,
            tiled=True,
        ).astype(jnp.float32),
        lax.all_to_all(
            out_local.reshape(width, 1, block_units).astype(jnp.bfloat16),
            "fsdp",
            split_axis=0,
            concat_axis=1,
            tiled=True,
        ).astype(jnp.float32),
    )
    in_grad = in_home.reshape(local_rows, experts, units)
    out_grad = out_home.reshape(local_rows, experts, units)
    choice_grad = jnp.sum(picked.astype(f32) * gate_grad[:, :, None], axis=1)
    logit_grad = probs * (choice_grad - jnp.sum(probs * choice_grad, axis=-1, keepdims=True))
    router_part = jnp.einsum("td,te->de", tokens_m.astype(f32), logit_grad, precision=TOP)
    routed_in = slot_in_grad.reshape(experts * CAP, width)[slot].reshape(group, 2, width)
    token_gradient = jnp.sum(routed_in, axis=1) + jnp.einsum(
        "te,de->td", logit_grad, router_back.astype(f32), precision=TOP
    )
    expert_norm_backward, expert_gain_partial, expert_shift_partial = norm_backward(
        owned_rows(token_gradient),
        expert_standardized,
        expert_inverse_deviation,
        expert_gain_gradient,
    )
    middle_grad = cotangent + expert_norm_backward
    mid_rows = group_rows(middle_grad.astype(bf16))
    proj_part = jnp.einsum("th,td->hd", context, mid_rows, preferred_element_type=f32)
    context_grad = jnp.einsum("td,hd->th", mid_rows, proj_back, preferred_element_type=f32).astype(
        bf16
    )
    query_grad, key_grad, value_grad = attend_back(
        proj[0], proj[1], proj[2], lse, context_grad, images
    )
    stacked = jnp.stack([query_grad, key_grad, value_grad])
    qkv_part = jnp.einsum("td,ith->idh", tokens_a, stacked, preferred_element_type=f32)
    attention_input_gradient = owned_rows(
        jnp.einsum("ith,idh->td", stacked, qkv_back, preferred_element_type=f32)
    )
    attention_norm_backward, attention_gain_partial, attention_shift_partial = norm_backward(
        attention_input_gradient,
        attention_standardized,
        attention_inverse_deviation,
        attention_gain_gradient,
    )
    input_grad = middle_grad + attention_norm_backward
    qkv_grad, proj_grad, router_grad, norm_grads = reduce_dense(
        qkv_part,
        proj_part,
        router_part,
        [attention_gain_partial, attention_shift_partial, expert_gain_partial, expert_shift_partial],
    )
    return (
        outputs,
        input_grad,
        norm_grads[0],
        norm_grads[1],
        qkv_grad,
        proj_grad,
        norm_grads[2],
        norm_grads[3],
        router_grad,
        in_grad,
        out_grad,
    )


def solution(mesh):
    return jax.shard_map(
        per_device,
        mesh=mesh,
        in_specs=(
            P(("fsdp", "tp"), None),
            P("fsdp", None),
            P("fsdp"),
            P("fsdp"),
            P(None, "fsdp", "tp"),
            P("tp", "fsdp"),
            P("fsdp"),
            P("fsdp"),
            P("fsdp", None),
            P("fsdp", None, "tp"),
            P("fsdp", None, "tp"),
            P(("fsdp", "tp"), None),
        ),
        out_specs=(
            P(("fsdp", "tp"), None),
            P(("fsdp", "tp"), None),
            P("fsdp"),
            P("fsdp"),
            P(None, "fsdp", "tp"),
            P("tp", "fsdp"),
            P("fsdp"),
            P("fsdp"),
            P("fsdp", None),
            P("fsdp", None, "tp"),
            P("fsdp", None, "tp"),
        ),
        check_vma=False,
    )
```

```python
import jax
import jax.numpy as jnp
from jax import lax
from jax.sharding import PartitionSpec as P

HEAD_DIM = 64
SEQ = 200
REAL_TOK = 197
CAP = 63


EPS = 1e-06
TOP = lax.Precision.HIGHEST


def gelu_exact(value):
    return jax.nn.gelu(value, approximate=False)


def normalize_rows(value, norm_gain, norm_shift):
    row_mean = jnp.mean(value, axis=-1, keepdims=True)
    centered_rows = value - row_mean
    inverse_deviation = lax.rsqrt(
        jnp.mean(centered_rows * centered_rows, axis=-1, keepdims=True) + EPS
    )
    standardized_rows = centered_rows * inverse_deviation
    normed_rows = (
        standardized_rows * norm_gain.astype(jnp.float32) + norm_shift.astype(jnp.float32)
    ).astype(jnp.bfloat16)
    return (normed_rows, standardized_rows, inverse_deviation)


def norm_backward(incoming_gradient, standardized_rows, inverse_deviation, norm_gain):
    scaled_gradient = incoming_gradient * norm_gain.astype(jnp.float32)
    inner_product = (
        scaled_gradient
        - jnp.mean(scaled_gradient, axis=-1, keepdims=True)
        - standardized_rows * jnp.mean(scaled_gradient * standardized_rows, axis=-1, keepdims=True)
    )
    return (
        inverse_deviation * inner_product,
        jnp.sum(incoming_gradient * standardized_rows, axis=0),
        jnp.sum(incoming_gradient, axis=0),
    )


def slot_table(routes, experts, capacity):
    picked = (routes[:, :, None] == jnp.arange(experts, dtype=jnp.int32)[None, None, :]).astype(
        jnp.int32
    )
    flat = picked.reshape(-1, experts)
    before = jnp.cumsum(flat, axis=0) - flat
    number = jnp.sum(before * flat, axis=-1)
    slot = routes.reshape(-1) * capacity + number
    owner = jnp.arange(flat.shape[0], dtype=jnp.int32) // 2
    token_of_slot = jnp.zeros((experts * capacity,), jnp.int32).at[slot].set(owner)
    filled = jnp.zeros((experts * capacity,), jnp.int32).at[slot].set(1)
    return (picked, slot, token_of_slot, filled)


def split_heads(value, images):
    input_rows, width = value.shape
    return value.reshape(images, input_rows // images, width // HEAD_DIM, HEAD_DIM)


def live_keys(length):
    return (jnp.arange(length) < REAL_TOK)[None, None, None, :]


def attend(query, key, value, images):
    query_h = split_heads(query, images)
    key_h = split_heads(key, images)
    value_h = split_heads(value, images)
    scores = jnp.einsum(
        "ishd,ithd->ihst", query_h, key_h, preferred_element_type=jnp.float32
    ) * HEAD_DIM ** (-0.5)
    live = live_keys(scores.shape[-1])
    lse = jnp.log(jnp.sum(jnp.where(live, jnp.exp(scores), 0.0), axis=-1, keepdims=True))
    probs = jnp.where(live, jnp.exp(scores - lse), 0.0).astype(jnp.bfloat16)
    context = jnp.einsum(
        "ihst,ithd->ishd", probs, value_h, preferred_element_type=jnp.float32
    ).astype(jnp.bfloat16)
    return (context.reshape(query.shape), lse)


def attend_back(query, key, value, lse, context_grad, images):
    query_h = split_heads(query, images)
    key_h = split_heads(key, images)
    value_h = split_heads(value, images)
    grad_h = split_heads(context_grad, images)
    scores = jnp.einsum(
        "ishd,ithd->ihst", query_h, key_h, preferred_element_type=jnp.float32
    ) * HEAD_DIM ** (-0.5)
    live = live_keys(scores.shape[-1])
    probs = jnp.where(live, jnp.exp(scores - lse), 0.0)
    value_grad = jnp.einsum(
        "ihst,ishd->ithd", probs.astype(jnp.bfloat16), grad_h, preferred_element_type=jnp.float32
    ).astype(jnp.bfloat16)
    inner_product = jnp.einsum(
        "ishd,ithd->ihst", grad_h, value_h, preferred_element_type=jnp.float32
    )
    score_grad = (
        probs
        * (inner_product - jnp.sum(probs * inner_product, axis=-1, keepdims=True))
        * HEAD_DIM ** (-0.5)
    ).astype(jnp.bfloat16)
    query_grad = jnp.einsum(
        "ihst,ithd->ishd", score_grad, key_h, preferred_element_type=jnp.float32
    ).astype(jnp.bfloat16)
    key_grad = jnp.einsum(
        "ihst,ishd->ithd", score_grad, query_h, preferred_element_type=jnp.float32
    ).astype(jnp.bfloat16)
    shape = query.shape
    return (query_grad.reshape(shape), key_grad.reshape(shape), value_grad.reshape(shape))


def gather_rows(pieces):
    rows = pieces[0].shape[0]
    packed = jnp.concatenate(pieces, axis=1)
    spare = -packed.shape[1] % 128
    if spare:
        packed = jnp.pad(packed, ((0, 0), (0, spare)))
    full = lax.all_gather(packed[None], "fsdp", axis=0, tiled=True)
    return full.reshape(lax.axis_size("fsdp") * rows, packed.shape[1])


def gather_dense(
    qkv_weight,
    proj_weight,
    router_weight,
    attention_norm_gain,
    attention_norm_shift,
    expert_norm_gain,
    expert_norm_shift,
):
    rows = qkv_weight.shape[1]
    heads_width = qkv_weight.shape[2]
    experts = router_weight.shape[1]
    full = gather_rows(
        [
            jnp.transpose(qkv_weight, (1, 0, 2)).reshape(rows, -1),
            proj_weight.T,
            router_weight,
            jnp.stack(
                [attention_norm_gain, attention_norm_shift, expert_norm_gain, expert_norm_shift],
                axis=1,
            ),
        ]
    )
    width = full.shape[0]
    at = 3 * heads_width
    qkv_full = jnp.transpose(full[:, :at].reshape(width, 3, heads_width), (1, 0, 2))
    proj_full = full[:, at : at + heads_width].T
    at += heads_width
    router_full = full[:, at : at + experts]
    at += experts
    return (qkv_full, proj_full, router_full) + tuple(full[:, at + i] for i in range(4))


def reduce_rows(pieces):
    packed = jnp.concatenate(pieces, axis=1)
    spare = -packed.shape[1] % 128
    if spare:
        packed = jnp.pad(packed, ((0, 0), (0, spare)))
    holders = lax.axis_size("fsdp")
    rows = packed.shape[0] // holders
    return lax.psum_scatter(
        packed.reshape(holders, rows, packed.shape[1]), "fsdp", scatter_dimension=0, tiled=True
    ).reshape(rows, packed.shape[1])


def group_rows(value):
    return lax.all_gather(value, "tp", axis=0, tiled=True)


def owned_rows(value):
    return lax.psum_scatter(value, "tp", scatter_dimension=0, tiled=True)


def to_owners(slots, holders):
    experts, capacity, width = slots.shape
    spread = jnp.broadcast_to(slots[:, None], (experts, holders, capacity, width)).reshape(
        experts * holders, capacity, width
    )
    moved = lax.all_to_all(spread, "fsdp", split_axis=0, concat_axis=0, tiled=True)
    return moved.reshape(-1, width)


def to_groups(partial_value, experts, holders, capacity):
    width = partial_value.shape[1]
    pieces = partial_value.astype(jnp.bfloat16).reshape(experts * holders, capacity, width)
    moved = lax.all_to_all(pieces, "fsdp", split_axis=0, concat_axis=0, tiled=True)
    return jnp.sum(moved.reshape(experts, holders, capacity, width).astype(jnp.float32), axis=1)


def per_device(
    inputs,
    routes,
    attention_norm_gain,
    attention_norm_shift,
    qkv_weight,
    proj_weight,
    expert_norm_gain,
    expert_norm_shift,
    router_weight,
    expert_in,
    expert_out,
    cotangent,
):
    f32 = jnp.float32
    bf16 = jnp.bfloat16
    dense = gather_dense(
        qkv_weight,
        proj_weight,
        router_weight,
        attention_norm_gain,
        attention_norm_shift,
        expert_norm_gain,
        expert_norm_shift,
    )
    qkv_full, proj_full, router_full, attention_gain, attention_shift, expert_gain, expert_shift = (
        dense
    )
    group = routes.shape[0]
    images = group // SEQ
    experts = router_full.shape[1]
    width = qkv_full.shape[1]
    units = expert_in.shape[2]
    local_rows = expert_in.shape[0]
    holders = lax.axis_size("fsdp") // experts
    block_units = units // holders
    attention_normed, attention_standardized, attention_inverse_deviation = normalize_rows(
        inputs, attention_gain, attention_shift
    )
    tokens_a = group_rows(attention_normed)
    proj = jnp.einsum("td,idh->ith", tokens_a, qkv_full, preferred_element_type=f32).astype(bf16)
    context, lse = attend(proj[0], proj[1], proj[2], images)
    residual_middle = inputs + owned_rows(jnp.dot(context, proj_full, preferred_element_type=f32))
    expert_normed, expert_standardized, expert_inverse_deviation = normalize_rows(
        residual_middle, expert_gain, expert_shift
    )
    tokens_m = group_rows(expert_normed)
    logits = jnp.dot(tokens_m, router_full, preferred_element_type=f32)
    raised = jnp.exp(logits)
    probs = raised / jnp.sum(raised, axis=-1, keepdims=True)
    picked, slot, token_of_slot, filled = slot_table(routes, experts, CAP)
    gates = jnp.sum(picked.astype(f32) * probs[:, None, :], axis=-1)
    slotted = jnp.where(filled[:, None] > 0, tokens_m[token_of_slot], jnp.zeros((), bf16)).reshape(
        experts, CAP, width
    )
    regroup_in = expert_in.reshape(local_rows, experts * holders, block_units)
    regroup_out = expert_out.reshape(local_rows, experts * holders, block_units)
    own_in, own_out = (
        lax.all_to_all(regroup_in, "fsdp", split_axis=1, concat_axis=0, tiled=True),
        lax.all_to_all(regroup_out, "fsdp", split_axis=1, concat_axis=0, tiled=True),
    )
    own_in = own_in.reshape(width, block_units)
    own_out = own_out.reshape(width, block_units)
    owner_x = to_owners(slotted, holders)
    owner_pre = jnp.dot(owner_x, own_in, preferred_element_type=f32)
    owner_hidden = gelu_exact(owner_pre).astype(bf16)
    owner_res = jnp.einsum("cf,df->cd", owner_hidden, own_out, preferred_element_type=f32)
    expert_res = to_groups(owner_res, experts, holders, CAP)
    routed = expert_res.reshape(experts * CAP, width)[slot].reshape(group, 2, width)
    outputs = residual_middle + owned_rows(jnp.sum(gates[:, :, None] * routed, axis=1))
    qkv_back, proj_back, router_back = qkv_full, proj_full, router_full
    attention_gain_gradient, expert_gain_gradient = attention_gain, expert_gain
    dout = group_rows(cotangent.astype(bf16))
    dout_f = dout.astype(f32)
    gate_of_slot = jnp.zeros((experts * CAP,), f32).at[slot].set(gates.reshape(-1))
    slot_grad = (
        jnp.where(filled[:, None] > 0, gate_of_slot[:, None] * dout_f[token_of_slot], 0.0)
        .astype(bf16)
        .reshape(experts, CAP, width)
    )
    gate_grad = jnp.sum(dout_f[:, None, :] * routed, axis=-1)
    owner_g = to_owners(slot_grad, holders)
    owner_hgrad = jnp.dot(owner_g, own_out, preferred_element_type=f32)
    owner_pgrad = jax.vjp(gelu_exact, owner_pre)[1](owner_hgrad)[0].astype(bf16)
    owner_back = jnp.einsum("cf,df->cd", owner_pgrad, own_in, preferred_element_type=f32)
    slot_in_grad = to_groups(owner_back, experts, holders, CAP)
    in_local = jnp.einsum("cd,cf->df", owner_x, owner_pgrad, preferred_element_type=f32)
    out_local = jnp.einsum("cd,cf->df", owner_g, owner_hidden, preferred_element_type=f32)
    in_home, out_home = (
        lax.all_to_all(
            in_local.reshape(width, 1, block_units).astype(jnp.bfloat16),
            "fsdp",
            split_axis=0,
            concat_axis=1,
            tiled=True,
        ).astype(jnp.float32),
        lax.all_to_all(
            out_local.reshape(width, 1, block_units).astype(jnp.bfloat16),
            "fsdp",
            split_axis=0,
            concat_axis=1,
            tiled=True,
        ).astype(jnp.float32),
    )
    in_grad = in_home.reshape(local_rows, experts, units)
    out_grad = out_home.reshape(local_rows, experts, units)
    choice_grad = jnp.sum(picked.astype(f32) * gate_grad[:, :, None], axis=1)
    logit_grad = probs * (choice_grad - jnp.sum(probs * choice_grad, axis=-1, keepdims=True))
    router_part = jnp.einsum("td,te->de", tokens_m.astype(f32), logit_grad, precision=TOP)
    routed_in = slot_in_grad.reshape(experts * CAP, width)[slot].reshape(group, 2, width)
    token_gradient = jnp.sum(routed_in, axis=1) + jnp.einsum(
        "te,de->td", logit_grad, router_back.astype(f32), precision=TOP
    )
    expert_norm_backward, expert_gain_partial, expert_shift_partial = norm_backward(
        owned_rows(token_gradient),
        expert_standardized,
        expert_inverse_deviation,
        expert_gain_gradient,
    )
    middle_grad = cotangent + expert_norm_backward
    mid_rows = group_rows(middle_grad.astype(bf16))
    proj_part = jnp.einsum("th,td->hd", context, mid_rows, preferred_element_type=f32)
    experts_w = router_part.shape[1]
    heads_w = proj_part.shape[0]
    early = reduce_rows(
        [proj_part.T, router_part, jnp.stack([expert_gain_partial, expert_shift_partial], axis=1)]
    )
    context_grad = jnp.einsum("td,hd->th", mid_rows, proj_back, preferred_element_type=f32).astype(
        bf16
    )
    query_grad, key_grad, value_grad = attend_back(
        proj[0], proj[1], proj[2], lse, context_grad, images
    )
    stacked = jnp.stack([query_grad, key_grad, value_grad])
    early, stacked = lax.optimization_barrier((early, stacked))
    qkv_part = jnp.einsum("td,ith->idh", tokens_a, stacked, preferred_element_type=f32)
    attention_input_gradient = owned_rows(
        jnp.einsum("ith,idh->td", stacked, qkv_back, preferred_element_type=f32)
    )
    attention_norm_backward, attention_gain_partial, attention_shift_partial = norm_backward(
        attention_input_gradient,
        attention_standardized,
        attention_inverse_deviation,
        attention_gain_gradient,
    )
    input_grad = middle_grad + attention_norm_backward
    late = reduce_rows(
        [
            jnp.transpose(qkv_part, (1, 0, 2)).reshape(qkv_part.shape[1], -1),
            jnp.stack([attention_gain_partial, attention_shift_partial], axis=1),
        ]
    )
    rows = late.shape[0]
    at = 3 * heads_w
    qkv_grad = jnp.transpose(late[:, :at].reshape(rows, 3, heads_w), (1, 0, 2))
    proj_grad = early[:, :heads_w].T
    shared = lax.psum(
        jnp.concatenate([early[:, heads_w : heads_w + experts_w + 2], late[:, at : at + 2]], axis=1),
        "tp",
    )
    router_grad = shared[:, :experts_w]
    return (
        outputs,
        input_grad,
        shared[:, experts_w + 2],
        shared[:, experts_w + 3],
        qkv_grad,
        proj_grad,
        shared[:, experts_w],
        shared[:, experts_w + 1],
        router_grad,
        in_grad,
        out_grad,
    )


def solution(mesh):
    return jax.shard_map(
        per_device,
        mesh=mesh,
        in_specs=(
            P(("fsdp", "tp"), None),
            P("fsdp", None),
            P("fsdp"),
            P("fsdp"),
            P(None, "fsdp", "tp"),
            P("tp", "fsdp"),
            P("fsdp"),
            P("fsdp"),
            P("fsdp", None),
            P("fsdp", None, "tp"),
            P("fsdp", None, "tp"),
            P(("fsdp", "tp"), None),
        ),
        out_specs=(
            P(("fsdp", "tp"), None),
            P(("fsdp", "tp"), None),
            P("fsdp"),
            P("fsdp"),
            P(None, "fsdp", "tp"),
            P("tp", "fsdp"),
            P("fsdp"),
            P("fsdp"),
            P("fsdp", None),
            P("fsdp", None, "tp"),
            P("fsdp", None, "tp"),
        ),
        check_vma=False,
    )
```

```python
import jax
import jax.numpy as jnp
from jax import lax
from jax.sharding import PartitionSpec as P

HEAD_DIM = 64
SEQ = 200
REAL_TOK = 197
CAP = 63


EPS = 1e-06
TOP = lax.Precision.HIGHEST


def gelu_exact(value):
    return jax.nn.gelu(value, approximate=False)


def normalize_rows(value, norm_gain, norm_shift):
    row_mean = jnp.mean(value, axis=-1, keepdims=True)
    centered_rows = value - row_mean
    inverse_deviation = lax.rsqrt(
        jnp.mean(centered_rows * centered_rows, axis=-1, keepdims=True) + EPS
    )
    standardized_rows = centered_rows * inverse_deviation
    normed_rows = (
        standardized_rows * norm_gain.astype(jnp.float32) + norm_shift.astype(jnp.float32)
    ).astype(jnp.bfloat16)
    return (normed_rows, standardized_rows, inverse_deviation)


def norm_backward(incoming_gradient, standardized_rows, inverse_deviation, norm_gain):
    scaled_gradient = incoming_gradient * norm_gain.astype(jnp.float32)
    inner_product = (
        scaled_gradient
        - jnp.mean(scaled_gradient, axis=-1, keepdims=True)
        - standardized_rows * jnp.mean(scaled_gradient * standardized_rows, axis=-1, keepdims=True)
    )
    return (
        inverse_deviation * inner_product,
        jnp.sum(incoming_gradient * standardized_rows, axis=0),
        jnp.sum(incoming_gradient, axis=0),
    )


def slot_table(routes, experts, capacity):
    picked = (routes[:, :, None] == jnp.arange(experts, dtype=jnp.int32)[None, None, :]).astype(
        jnp.int32
    )
    flat = picked.reshape(-1, experts)
    before = jnp.cumsum(flat, axis=0) - flat
    number = jnp.sum(before * flat, axis=-1)
    slot = routes.reshape(-1) * capacity + number
    owner = jnp.arange(flat.shape[0], dtype=jnp.int32) // 2
    token_of_slot = jnp.zeros((experts * capacity,), jnp.int32).at[slot].set(owner)
    filled = jnp.zeros((experts * capacity,), jnp.int32).at[slot].set(1)
    return (picked, slot, token_of_slot, filled)


def split_heads(value, images):
    input_rows, width = value.shape
    return value.reshape(images, input_rows // images, width // HEAD_DIM, HEAD_DIM)


def live_keys(length):
    return (jnp.arange(length) < REAL_TOK)[None, None, None, :]


def attend(query, key, value, images):
    query_h = split_heads(query, images)
    key_h = split_heads(key, images)
    value_h = split_heads(value, images)
    scores = jnp.einsum(
        "ishd,ithd->ihst", query_h, key_h, preferred_element_type=jnp.float32
    ) * HEAD_DIM ** (-0.5)
    live = live_keys(scores.shape[-1])
    lse = jnp.log(jnp.sum(jnp.where(live, jnp.exp(scores), 0.0), axis=-1, keepdims=True))
    probs = jnp.where(live, jnp.exp(scores - lse), 0.0).astype(jnp.bfloat16)
    context = jnp.einsum(
        "ihst,ithd->ishd", probs, value_h, preferred_element_type=jnp.float32
    ).astype(jnp.bfloat16)
    return (context.reshape(query.shape), lse)


def attend_back(query, key, value, lse, context_grad, images):
    query_h = split_heads(query, images)
    key_h = split_heads(key, images)
    value_h = split_heads(value, images)
    grad_h = split_heads(context_grad, images)
    scores = jnp.einsum(
        "ishd,ithd->ihst", query_h, key_h, preferred_element_type=jnp.float32
    ) * HEAD_DIM ** (-0.5)
    live = live_keys(scores.shape[-1])
    probs = jnp.where(live, jnp.exp(scores - lse), 0.0)
    value_grad = jnp.einsum(
        "ihst,ishd->ithd", probs.astype(jnp.bfloat16), grad_h, preferred_element_type=jnp.float32
    ).astype(jnp.bfloat16)
    inner_product = jnp.einsum(
        "ishd,ithd->ihst", grad_h, value_h, preferred_element_type=jnp.float32
    )
    score_grad = (
        probs
        * (inner_product - jnp.sum(probs * inner_product, axis=-1, keepdims=True))
        * HEAD_DIM ** (-0.5)
    ).astype(jnp.bfloat16)
    query_grad = jnp.einsum(
        "ihst,ithd->ishd", score_grad, key_h, preferred_element_type=jnp.float32
    ).astype(jnp.bfloat16)
    key_grad = jnp.einsum(
        "ihst,ishd->ithd", score_grad, query_h, preferred_element_type=jnp.float32
    ).astype(jnp.bfloat16)
    shape = query.shape
    return (query_grad.reshape(shape), key_grad.reshape(shape), value_grad.reshape(shape))


def gather_dense(
    qkv_weight,
    proj_weight,
    router_weight,
    attention_norm_gain,
    attention_norm_shift,
    expert_norm_gain,
    expert_norm_shift,
):
    rows = qkv_weight.shape[1]
    heads_width = qkv_weight.shape[2]
    experts = router_weight.shape[1]
    packed = jnp.concatenate(
        [
            jnp.transpose(qkv_weight, (1, 0, 2)).reshape(rows, -1),
            proj_weight.T,
            router_weight,
            jnp.stack(
                [attention_norm_gain, attention_norm_shift, expert_norm_gain, expert_norm_shift],
                axis=1,
            ),
        ],
        axis=1,
    )
    holders = lax.axis_size("fsdp")
    spread = jnp.broadcast_to(packed[None], (holders,) + packed.shape)
    full = lax.all_to_all(spread, "fsdp", split_axis=0, concat_axis=0, tiled=True)
    full = full.reshape(holders * rows, packed.shape[1])
    width = full.shape[0]
    at = 3 * heads_width
    qkv_full = jnp.transpose(full[:, :at].reshape(width, 3, heads_width), (1, 0, 2))
    proj_full = full[:, at : at + heads_width].T
    at += heads_width
    router_full = full[:, at : at + experts]
    at += experts
    norms = full[:, at : at + 4]
    return (qkv_full, proj_full, router_full, norms[:, 0], norms[:, 1], norms[:, 2], norms[:, 3])


def reduce_dense(qkv_part, proj_part, router_part, norm_parts):
    width = qkv_part.shape[1]
    heads_width = qkv_part.shape[2]
    experts = router_part.shape[1]
    packed = jnp.concatenate(
        [
            jnp.transpose(qkv_part, (1, 0, 2)).reshape(width, -1),
            proj_part.T,
            router_part,
            jnp.stack(norm_parts, axis=1),
        ],
        axis=1,
    )
    holders = lax.axis_size("fsdp")
    rows = width // holders
    moved = lax.all_to_all(
        packed.reshape(holders, rows, packed.shape[1]), "fsdp", split_axis=0, concat_axis=0, tiled=True
    )
    part = jnp.sum(moved, axis=0)
    at = 3 * heads_width
    qkv_grad = jnp.transpose(part[:, :at].reshape(rows, 3, heads_width), (1, 0, 2))
    proj_grad = part[:, at : at + heads_width].T
    at += heads_width
    shared = lax.psum(part[:, at:], "tp")
    router_grad = shared[:, :experts]
    norm_grads = [shared[:, experts + i] for i in range(len(norm_parts))]
    return qkv_grad, proj_grad, router_grad, norm_grads


def group_rows(value):
    return lax.all_gather(value, "tp", axis=0, tiled=True)


def owned_rows(value):
    return lax.psum_scatter(value, "tp", scatter_dimension=0, tiled=True)


def to_owners(slots, holders):
    experts, capacity, width = slots.shape
    spread = jnp.broadcast_to(slots[:, None], (experts, holders, capacity, width)).reshape(
        experts * holders, capacity, width
    )
    moved = lax.all_to_all(spread, "fsdp", split_axis=0, concat_axis=0, tiled=True)
    return moved.reshape(-1, width)


def to_groups(partial_value, experts, holders, capacity):
    width = partial_value.shape[1]
    pieces = partial_value.astype(jnp.bfloat16).reshape(experts * holders, capacity, width)
    moved = lax.all_to_all(pieces, "fsdp", split_axis=0, concat_axis=0, tiled=True)
    return jnp.sum(moved.reshape(experts, holders, capacity, width).astype(jnp.float32), axis=1)


def per_device(
    inputs,
    routes,
    attention_norm_gain,
    attention_norm_shift,
    qkv_weight,
    proj_weight,
    expert_norm_gain,
    expert_norm_shift,
    router_weight,
    expert_in,
    expert_out,
    cotangent,
):
    f32 = jnp.float32
    bf16 = jnp.bfloat16
    dense = gather_dense(
        qkv_weight,
        proj_weight,
        router_weight,
        attention_norm_gain,
        attention_norm_shift,
        expert_norm_gain,
        expert_norm_shift,
    )
    qkv_full, proj_full, router_full, attention_gain, attention_shift, expert_gain, expert_shift = (
        dense
    )
    group = routes.shape[0]
    images = group // SEQ
    experts = router_full.shape[1]
    width = qkv_full.shape[1]
    units = expert_in.shape[2]
    local_rows = expert_in.shape[0]
    holders = lax.axis_size("fsdp") // experts
    block_units = units // holders
    attention_normed, attention_standardized, attention_inverse_deviation = normalize_rows(
        inputs, attention_gain, attention_shift
    )
    tokens_a = group_rows(attention_normed)
    proj = jnp.einsum("td,idh->ith", tokens_a, qkv_full, preferred_element_type=f32).astype(bf16)
    context, lse = attend(proj[0], proj[1], proj[2], images)
    residual_middle = inputs + owned_rows(jnp.dot(context, proj_full, preferred_element_type=f32))
    expert_normed, expert_standardized, expert_inverse_deviation = normalize_rows(
        residual_middle, expert_gain, expert_shift
    )
    tokens_m = group_rows(expert_normed)
    logits = jnp.dot(tokens_m, router_full, preferred_element_type=f32)
    raised = jnp.exp(logits)
    probs = raised / jnp.sum(raised, axis=-1, keepdims=True)
    picked, slot, token_of_slot, filled = slot_table(routes, experts, CAP)
    gates = jnp.sum(picked.astype(f32) * probs[:, None, :], axis=-1)
    slotted = jnp.where(filled[:, None] > 0, tokens_m[token_of_slot], jnp.zeros((), bf16)).reshape(
        experts, CAP, width
    )
    regroup_in = expert_in.reshape(local_rows, experts * holders, block_units)
    regroup_out = expert_out.reshape(local_rows, experts * holders, block_units)
    own_in, own_out = (
        lax.all_to_all(regroup_in, "fsdp", split_axis=1, concat_axis=0, tiled=True),
        lax.all_to_all(regroup_out, "fsdp", split_axis=1, concat_axis=0, tiled=True),
    )
    own_in = own_in.reshape(width, block_units)
    own_out = own_out.reshape(width, block_units)
    owner_x = to_owners(slotted, holders)
    owner_pre = jnp.dot(owner_x, own_in, preferred_element_type=f32)
    owner_hidden = gelu_exact(owner_pre).astype(bf16)
    owner_res = jnp.einsum("cf,df->cd", owner_hidden, own_out, preferred_element_type=f32)
    expert_res = to_groups(owner_res, experts, holders, CAP)
    routed = expert_res.reshape(experts * CAP, width)[slot].reshape(group, 2, width)
    outputs = residual_middle + owned_rows(jnp.sum(gates[:, :, None] * routed, axis=1))
    qkv_back, proj_back, router_back = qkv_full, proj_full, router_full
    attention_gain_gradient, expert_gain_gradient = attention_gain, expert_gain
    dout = group_rows(cotangent.astype(bf16))
    dout_f = dout.astype(f32)
    gate_of_slot = jnp.zeros((experts * CAP,), f32).at[slot].set(gates.reshape(-1))
    slot_grad = (
        jnp.where(filled[:, None] > 0, gate_of_slot[:, None] * dout_f[token_of_slot], 0.0)
        .astype(bf16)
        .reshape(experts, CAP, width)
    )
    gate_grad = jnp.sum(dout_f[:, None, :] * routed, axis=-1)
    owner_g = to_owners(slot_grad, holders)
    owner_hgrad = jnp.dot(owner_g, own_out, preferred_element_type=f32)
    owner_pgrad = jax.vjp(gelu_exact, owner_pre)[1](owner_hgrad)[0].astype(bf16)
    owner_back = jnp.einsum("cf,df->cd", owner_pgrad, own_in, preferred_element_type=f32)
    slot_in_grad = to_groups(owner_back, experts, holders, CAP)
    in_local = jnp.einsum("cd,cf->df", owner_x, owner_pgrad, preferred_element_type=f32)
    out_local = jnp.einsum("cd,cf->df", owner_g, owner_hidden, preferred_element_type=f32)
    in_home, out_home = (
        lax.all_to_all(
            in_local.reshape(width, 1, block_units).astype(jnp.bfloat16),
            "fsdp",
            split_axis=0,
            concat_axis=1,
            tiled=True,
        ).astype(jnp.float32),
        lax.all_to_all(
            out_local.reshape(width, 1, block_units).astype(jnp.bfloat16),
            "fsdp",
            split_axis=0,
            concat_axis=1,
            tiled=True,
        ).astype(jnp.float32),
    )
    in_grad = in_home.reshape(local_rows, experts, units)
    out_grad = out_home.reshape(local_rows, experts, units)
    choice_grad = jnp.sum(picked.astype(f32) * gate_grad[:, :, None], axis=1)
    logit_grad = probs * (choice_grad - jnp.sum(probs * choice_grad, axis=-1, keepdims=True))
    router_part = jnp.einsum("td,te->de", tokens_m.astype(f32), logit_grad, precision=TOP)
    routed_in = slot_in_grad.reshape(experts * CAP, width)[slot].reshape(group, 2, width)
    token_gradient = jnp.sum(routed_in, axis=1) + jnp.einsum(
        "te,de->td", logit_grad, router_back.astype(f32), precision=TOP
    )
    expert_norm_backward, expert_gain_partial, expert_shift_partial = norm_backward(
        owned_rows(token_gradient),
        expert_standardized,
        expert_inverse_deviation,
        expert_gain_gradient,
    )
    middle_grad = cotangent + expert_norm_backward
    mid_rows = group_rows(middle_grad.astype(bf16))
    proj_part = jnp.einsum("th,td->hd", context, mid_rows, preferred_element_type=f32)
    context_grad = jnp.einsum("td,hd->th", mid_rows, proj_back, preferred_element_type=f32).astype(
        bf16
    )
    query_grad, key_grad, value_grad = attend_back(
        proj[0], proj[1], proj[2], lse, context_grad, images
    )
    stacked = jnp.stack([query_grad, key_grad, value_grad])
    qkv_part = jnp.einsum("td,ith->idh", tokens_a, stacked, preferred_element_type=f32)
    attention_input_gradient = owned_rows(
        jnp.einsum("ith,idh->td", stacked, qkv_back, preferred_element_type=f32)
    )
    attention_norm_backward, attention_gain_partial, attention_shift_partial = norm_backward(
        attention_input_gradient,
        attention_standardized,
        attention_inverse_deviation,
        attention_gain_gradient,
    )
    input_grad = middle_grad + attention_norm_backward
    qkv_grad, proj_grad, router_grad, norm_grads = reduce_dense(
        qkv_part,
        proj_part,
        router_part,
        [attention_gain_partial, attention_shift_partial, expert_gain_partial, expert_shift_partial],
    )
    return (
        outputs,
        input_grad,
        norm_grads[0],
        norm_grads[1],
        qkv_grad,
        proj_grad,
        norm_grads[2],
        norm_grads[3],
        router_grad,
        in_grad,
        out_grad,
    )


def solution(mesh):
    return jax.shard_map(
        per_device,
        mesh=mesh,
        in_specs=(
            P(("fsdp", "tp"), None),
            P("fsdp", None),
            P("fsdp"),
            P("fsdp"),
            P(None, "fsdp", "tp"),
            P("tp", "fsdp"),
            P("fsdp"),
            P("fsdp"),
            P("fsdp", None),
            P("fsdp", None, "tp"),
            P("fsdp", None, "tp"),
            P(("fsdp", "tp"), None),
        ),
        out_specs=(
            P(("fsdp", "tp"), None),
            P(("fsdp", "tp"), None),
            P("fsdp"),
            P("fsdp"),
            P(None, "fsdp", "tp"),
            P("tp", "fsdp"),
            P("fsdp"),
            P("fsdp"),
            P("fsdp", None),
            P("fsdp", None, "tp"),
            P("fsdp", None, "tp"),
        ),
        check_vma=False,
    )
```

```python
import jax
import jax.numpy as jnp
from jax import lax
from jax.sharding import PartitionSpec as P
from jax.experimental import pallas as pl
from jax.experimental.pallas import tpu as pltpu

MESH_IDS = pl.DeviceIdType.MESH


def _swap_kernel(x_ref, out_ref, held, send_sem, recv_sem):
    me = lax.axis_index("tp")
    other = 1 - me
    peer = (lax.axis_index("fsdp"), other)
    barrier = pltpu.get_barrier_semaphore()
    pl.semaphore_signal(barrier, inc=1, device_id=peer, device_id_type=MESH_IDS)
    pl.semaphore_wait(barrier, 1)
    copy = pltpu.make_async_remote_copy(
        src_ref=x_ref,
        dst_ref=held,
        send_sem=send_sem,
        recv_sem=recv_sem,
        device_id=peer,
        device_id_type=MESH_IDS,
    )
    copy.start()
    out_ref[me] = x_ref[...]
    copy.wait()
    out_ref[other] = held[...]


def tp_swap(x, call_id):
    rows, width = x.shape
    out = pl.pallas_call(
        _swap_kernel,
        out_shape=jax.ShapeDtypeStruct((2, rows, width), x.dtype),
        in_specs=[pl.BlockSpec(memory_space=pltpu.VMEM)],
        out_specs=pl.BlockSpec(memory_space=pltpu.VMEM),
        scratch_shapes=[
            pltpu.VMEM((rows, width), x.dtype),
            pltpu.SemaphoreType.DMA(()),
            pltpu.SemaphoreType.DMA(()),
        ],
        compiler_params=pltpu.CompilerParams(collective_id=call_id, has_side_effects=True),
    )(x)
    return out.reshape(2 * rows, width)

HEAD_DIM = 64
SEQ = 200
REAL_TOK = 197
CAP = 63


EPS = 1e-06
TOP = lax.Precision.HIGHEST


def gelu_exact(value):
    return jax.nn.gelu(value, approximate=False)


def normalize_rows(value, norm_gain, norm_shift):
    row_mean = jnp.mean(value, axis=-1, keepdims=True)
    centered_rows = value - row_mean
    inverse_deviation = lax.rsqrt(
        jnp.mean(centered_rows * centered_rows, axis=-1, keepdims=True) + EPS
    )
    standardized_rows = centered_rows * inverse_deviation
    normed_rows = (
        standardized_rows * norm_gain.astype(jnp.float32) + norm_shift.astype(jnp.float32)
    ).astype(jnp.bfloat16)
    return (normed_rows, standardized_rows, inverse_deviation)


def norm_backward(incoming_gradient, standardized_rows, inverse_deviation, norm_gain):
    scaled_gradient = incoming_gradient * norm_gain.astype(jnp.float32)
    inner_product = (
        scaled_gradient
        - jnp.mean(scaled_gradient, axis=-1, keepdims=True)
        - standardized_rows * jnp.mean(scaled_gradient * standardized_rows, axis=-1, keepdims=True)
    )
    return (
        inverse_deviation * inner_product,
        jnp.sum(incoming_gradient * standardized_rows, axis=0),
        jnp.sum(incoming_gradient, axis=0),
    )


def slot_table(routes, experts, capacity):
    picked = (routes[:, :, None] == jnp.arange(experts, dtype=jnp.int32)[None, None, :]).astype(
        jnp.int32
    )
    flat = picked.reshape(-1, experts)
    before = jnp.cumsum(flat, axis=0) - flat
    number = jnp.sum(before * flat, axis=-1)
    slot = routes.reshape(-1) * capacity + number
    owner = jnp.arange(flat.shape[0], dtype=jnp.int32) // 2
    token_of_slot = jnp.zeros((experts * capacity,), jnp.int32).at[slot].set(owner)
    filled = jnp.zeros((experts * capacity,), jnp.int32).at[slot].set(1)
    return (picked, slot, token_of_slot, filled)


def split_heads(value, images):
    input_rows, width = value.shape
    return value.reshape(images, input_rows // images, width // HEAD_DIM, HEAD_DIM)


def live_keys(length):
    return (jnp.arange(length) < REAL_TOK)[None, None, None, :]


def attend(query, key, value, images):
    query_h = split_heads(query, images)
    key_h = split_heads(key, images)
    value_h = split_heads(value, images)
    scores = jnp.einsum(
        "ishd,ithd->ihst", query_h, key_h, preferred_element_type=jnp.float32
    ) * HEAD_DIM ** (-0.5)
    live = live_keys(scores.shape[-1])
    lse = jnp.log(jnp.sum(jnp.where(live, jnp.exp(scores), 0.0), axis=-1, keepdims=True))
    probs = jnp.where(live, jnp.exp(scores - lse), 0.0).astype(jnp.bfloat16)
    context = jnp.einsum(
        "ihst,ithd->ishd", probs, value_h, preferred_element_type=jnp.float32
    ).astype(jnp.bfloat16)
    return (context.reshape(query.shape), lse)


def attend_back(query, key, value, lse, context_grad, images):
    query_h = split_heads(query, images)
    key_h = split_heads(key, images)
    value_h = split_heads(value, images)
    grad_h = split_heads(context_grad, images)
    scores = jnp.einsum(
        "ishd,ithd->ihst", query_h, key_h, preferred_element_type=jnp.float32
    ) * HEAD_DIM ** (-0.5)
    live = live_keys(scores.shape[-1])
    probs = jnp.where(live, jnp.exp(scores - lse), 0.0)
    value_grad = jnp.einsum(
        "ihst,ishd->ithd", probs.astype(jnp.bfloat16), grad_h, preferred_element_type=jnp.float32
    ).astype(jnp.bfloat16)
    inner_product = jnp.einsum(
        "ishd,ithd->ihst", grad_h, value_h, preferred_element_type=jnp.float32
    )
    score_grad = (
        probs
        * (inner_product - jnp.sum(probs * inner_product, axis=-1, keepdims=True))
        * HEAD_DIM ** (-0.5)
    ).astype(jnp.bfloat16)
    query_grad = jnp.einsum(
        "ihst,ithd->ishd", score_grad, key_h, preferred_element_type=jnp.float32
    ).astype(jnp.bfloat16)
    key_grad = jnp.einsum(
        "ihst,ishd->ithd", score_grad, query_h, preferred_element_type=jnp.float32
    ).astype(jnp.bfloat16)
    shape = query.shape
    return (query_grad.reshape(shape), key_grad.reshape(shape), value_grad.reshape(shape))


def gather_dense(
    qkv_weight,
    proj_weight,
    router_weight,
    attention_norm_gain,
    attention_norm_shift,
    expert_norm_gain,
    expert_norm_shift,
):
    rows = qkv_weight.shape[1]
    heads_width = qkv_weight.shape[2]
    experts = router_weight.shape[1]
    packed = jnp.concatenate(
        [
            jnp.transpose(qkv_weight, (1, 0, 2)).reshape(rows, -1),
            proj_weight.T,
            router_weight,
            jnp.stack(
                [attention_norm_gain, attention_norm_shift, expert_norm_gain, expert_norm_shift],
                axis=1,
            ),
        ],
        axis=1,
    )
    holders = lax.axis_size("fsdp")
    spread = jnp.broadcast_to(packed[None], (holders,) + packed.shape)
    full = lax.all_to_all(spread, "fsdp", split_axis=0, concat_axis=0, tiled=True)
    full = full.reshape(holders * rows, packed.shape[1])
    width = full.shape[0]
    at = 3 * heads_width
    qkv_full = jnp.transpose(full[:, :at].reshape(width, 3, heads_width), (1, 0, 2))
    proj_full = full[:, at : at + heads_width].T
    at += heads_width
    router_full = full[:, at : at + experts]
    at += experts
    norms = full[:, at : at + 4]
    return (qkv_full, proj_full, router_full, norms[:, 0], norms[:, 1], norms[:, 2], norms[:, 3])


def reduce_dense(qkv_part, proj_part, router_part, norm_parts):
    width = qkv_part.shape[1]
    heads_width = qkv_part.shape[2]
    experts = router_part.shape[1]
    packed = jnp.concatenate(
        [
            jnp.transpose(qkv_part, (1, 0, 2)).reshape(width, -1),
            proj_part.T,
            router_part,
            jnp.stack(norm_parts, axis=1),
        ],
        axis=1,
    )
    holders = lax.axis_size("fsdp")
    rows = width // holders
    moved = lax.all_to_all(
        packed.reshape(holders, rows, packed.shape[1]), "fsdp", split_axis=0, concat_axis=0, tiled=True
    )
    part = jnp.sum(moved, axis=0)
    at = 3 * heads_width
    qkv_grad = jnp.transpose(part[:, :at].reshape(rows, 3, heads_width), (1, 0, 2))
    proj_grad = part[:, at : at + heads_width].T
    at += heads_width
    shared = lax.psum(part[:, at:], "tp")
    router_grad = shared[:, :experts]
    norm_grads = [shared[:, experts + i] for i in range(len(norm_parts))]
    return qkv_grad, proj_grad, router_grad, norm_grads


def group_rows(value, call_id):
    return tp_swap(value, call_id)


def owned_rows(value):
    return lax.psum_scatter(value, "tp", scatter_dimension=0, tiled=True)


def to_owners(slots, holders):
    experts, capacity, width = slots.shape
    spread = jnp.broadcast_to(slots[:, None], (experts, holders, capacity, width)).reshape(
        experts * holders, capacity, width
    )
    moved = lax.all_to_all(spread, "fsdp", split_axis=0, concat_axis=0, tiled=True)
    return moved.reshape(-1, width)


def to_groups(partial_value, experts, holders, capacity):
    width = partial_value.shape[1]
    pieces = partial_value.astype(jnp.bfloat16).reshape(experts * holders, capacity, width)
    moved = lax.all_to_all(pieces, "fsdp", split_axis=0, concat_axis=0, tiled=True)
    return jnp.sum(moved.reshape(experts, holders, capacity, width).astype(jnp.float32), axis=1)


def per_device(
    inputs,
    routes,
    attention_norm_gain,
    attention_norm_shift,
    qkv_weight,
    proj_weight,
    expert_norm_gain,
    expert_norm_shift,
    router_weight,
    expert_in,
    expert_out,
    cotangent,
):
    f32 = jnp.float32
    bf16 = jnp.bfloat16
    dense = gather_dense(
        qkv_weight,
        proj_weight,
        router_weight,
        attention_norm_gain,
        attention_norm_shift,
        expert_norm_gain,
        expert_norm_shift,
    )
    qkv_full, proj_full, router_full, attention_gain, attention_shift, expert_gain, expert_shift = (
        dense
    )
    group = routes.shape[0]
    images = group // SEQ
    experts = router_full.shape[1]
    width = qkv_full.shape[1]
    units = expert_in.shape[2]
    local_rows = expert_in.shape[0]
    holders = lax.axis_size("fsdp") // experts
    block_units = units // holders
    attention_normed, attention_standardized, attention_inverse_deviation = normalize_rows(
        inputs, attention_gain, attention_shift
    )
    tokens_a = group_rows(attention_normed, 0)
    proj = jnp.einsum("td,idh->ith", tokens_a, qkv_full, preferred_element_type=f32).astype(bf16)
    context, lse = attend(proj[0], proj[1], proj[2], images)
    residual_middle = inputs + owned_rows(jnp.dot(context, proj_full, preferred_element_type=f32))
    expert_normed, expert_standardized, expert_inverse_deviation = normalize_rows(
        residual_middle, expert_gain, expert_shift
    )
    tokens_m = group_rows(expert_normed, 1)
    logits = jnp.dot(tokens_m, router_full, preferred_element_type=f32)
    raised = jnp.exp(logits)
    probs = raised / jnp.sum(raised, axis=-1, keepdims=True)
    picked, slot, token_of_slot, filled = slot_table(routes, experts, CAP)
    gates = jnp.sum(picked.astype(f32) * probs[:, None, :], axis=-1)
    slotted = jnp.where(filled[:, None] > 0, tokens_m[token_of_slot], jnp.zeros((), bf16)).reshape(
        experts, CAP, width
    )
    regroup_in = expert_in.reshape(local_rows, experts * holders, block_units)
    regroup_out = expert_out.reshape(local_rows, experts * holders, block_units)
    own_in, own_out = (
        lax.all_to_all(regroup_in, "fsdp", split_axis=1, concat_axis=0, tiled=True),
        lax.all_to_all(regroup_out, "fsdp", split_axis=1, concat_axis=0, tiled=True),
    )
    own_in = own_in.reshape(width, block_units)
    own_out = own_out.reshape(width, block_units)
    owner_x = to_owners(slotted, holders)
    owner_pre = jnp.dot(owner_x, own_in, preferred_element_type=f32)
    owner_hidden = gelu_exact(owner_pre).astype(bf16)
    owner_res = jnp.einsum("cf,df->cd", owner_hidden, own_out, preferred_element_type=f32)
    expert_res = to_groups(owner_res, experts, holders, CAP)
    routed = expert_res.reshape(experts * CAP, width)[slot].reshape(group, 2, width)
    outputs = residual_middle + owned_rows(jnp.sum(gates[:, :, None] * routed, axis=1))
    qkv_back, proj_back, router_back = qkv_full, proj_full, router_full
    attention_gain_gradient, expert_gain_gradient = attention_gain, expert_gain
    dout = group_rows(cotangent.astype(bf16), 2)
    dout_f = dout.astype(f32)
    gate_of_slot = jnp.zeros((experts * CAP,), f32).at[slot].set(gates.reshape(-1))
    slot_grad = (
        jnp.where(filled[:, None] > 0, gate_of_slot[:, None] * dout_f[token_of_slot], 0.0)
        .astype(bf16)
        .reshape(experts, CAP, width)
    )
    gate_grad = jnp.sum(dout_f[:, None, :] * routed, axis=-1)
    owner_g = to_owners(slot_grad, holders)
    owner_hgrad = jnp.dot(owner_g, own_out, preferred_element_type=f32)
    owner_pgrad = jax.vjp(gelu_exact, owner_pre)[1](owner_hgrad)[0].astype(bf16)
    owner_back = jnp.einsum("cf,df->cd", owner_pgrad, own_in, preferred_element_type=f32)
    slot_in_grad = to_groups(owner_back, experts, holders, CAP)
    in_local = jnp.einsum("cd,cf->df", owner_x, owner_pgrad, preferred_element_type=f32)
    out_local = jnp.einsum("cd,cf->df", owner_g, owner_hidden, preferred_element_type=f32)
    in_home, out_home = (
        lax.all_to_all(
            in_local.reshape(width, 1, block_units).astype(jnp.bfloat16),
            "fsdp",
            split_axis=0,
            concat_axis=1,
            tiled=True,
        ).astype(jnp.float32),
        lax.all_to_all(
            out_local.reshape(width, 1, block_units).astype(jnp.bfloat16),
            "fsdp",
            split_axis=0,
            concat_axis=1,
            tiled=True,
        ).astype(jnp.float32),
    )
    in_grad = in_home.reshape(local_rows, experts, units)
    out_grad = out_home.reshape(local_rows, experts, units)
    choice_grad = jnp.sum(picked.astype(f32) * gate_grad[:, :, None], axis=1)
    logit_grad = probs * (choice_grad - jnp.sum(probs * choice_grad, axis=-1, keepdims=True))
    router_part = jnp.einsum("td,te->de", tokens_m.astype(f32), logit_grad, precision=TOP)
    routed_in = slot_in_grad.reshape(experts * CAP, width)[slot].reshape(group, 2, width)
    token_gradient = jnp.sum(routed_in, axis=1) + jnp.einsum(
        "te,de->td", logit_grad, router_back.astype(f32), precision=TOP
    )
    expert_norm_backward, expert_gain_partial, expert_shift_partial = norm_backward(
        owned_rows(token_gradient),
        expert_standardized,
        expert_inverse_deviation,
        expert_gain_gradient,
    )
    middle_grad = cotangent + expert_norm_backward
    mid_rows = group_rows(middle_grad.astype(bf16), 3)
    proj_part = jnp.einsum("th,td->hd", context, mid_rows, preferred_element_type=f32)
    context_grad = jnp.einsum("td,hd->th", mid_rows, proj_back, preferred_element_type=f32).astype(
        bf16
    )
    query_grad, key_grad, value_grad = attend_back(
        proj[0], proj[1], proj[2], lse, context_grad, images
    )
    stacked = jnp.stack([query_grad, key_grad, value_grad])
    qkv_part = jnp.einsum("td,ith->idh", tokens_a, stacked, preferred_element_type=f32)
    attention_input_gradient = owned_rows(
        jnp.einsum("ith,idh->td", stacked, qkv_back, preferred_element_type=f32)
    )
    attention_norm_backward, attention_gain_partial, attention_shift_partial = norm_backward(
        attention_input_gradient,
        attention_standardized,
        attention_inverse_deviation,
        attention_gain_gradient,
    )
    input_grad = middle_grad + attention_norm_backward
    qkv_grad, proj_grad, router_grad, norm_grads = reduce_dense(
        qkv_part,
        proj_part,
        router_part,
        [attention_gain_partial, attention_shift_partial, expert_gain_partial, expert_shift_partial],
    )
    return (
        outputs,
        input_grad,
        norm_grads[0],
        norm_grads[1],
        qkv_grad,
        proj_grad,
        norm_grads[2],
        norm_grads[3],
        router_grad,
        in_grad,
        out_grad,
    )


def solution(mesh):
    return jax.shard_map(
        per_device,
        mesh=mesh,
        in_specs=(
            P(("fsdp", "tp"), None),
            P("fsdp", None),
            P("fsdp"),
            P("fsdp"),
            P(None, "fsdp", "tp"),
            P("tp", "fsdp"),
            P("fsdp"),
            P("fsdp"),
            P("fsdp", None),
            P("fsdp", None, "tp"),
            P("fsdp", None, "tp"),
            P(("fsdp", "tp"), None),
        ),
        out_specs=(
            P(("fsdp", "tp"), None),
            P(("fsdp", "tp"), None),
            P("fsdp"),
            P("fsdp"),
            P(None, "fsdp", "tp"),
            P("tp", "fsdp"),
            P("fsdp"),
            P("fsdp"),
            P("fsdp", None),
            P("fsdp", None, "tp"),
            P("fsdp", None, "tp"),
        ),
        check_vma=False,
    )
```

```python
import jax
import jax.numpy as jnp
from jax import lax
from jax.sharding import Mesh, PartitionSpec as P

HEAD_DIM = 64
SEQ = 200
REAL_TOK = 197
CAP = 63
EXPERTS = 16
FSDP = ("fa", "fb")


EPS = 1e-06
TOP = lax.Precision.HIGHEST


def fsdp_size():
    return lax.axis_size("fa") * lax.axis_size("fb")


def gelu_exact(value):
    return jax.nn.gelu(value, approximate=False)


def normalize_rows(value, norm_gain, norm_shift):
    row_mean = jnp.mean(value, axis=-1, keepdims=True)
    centered_rows = value - row_mean
    inverse_deviation = lax.rsqrt(
        jnp.mean(centered_rows * centered_rows, axis=-1, keepdims=True) + EPS
    )
    standardized_rows = centered_rows * inverse_deviation
    normed_rows = (
        standardized_rows * norm_gain.astype(jnp.float32) + norm_shift.astype(jnp.float32)
    ).astype(jnp.bfloat16)
    return (normed_rows, standardized_rows, inverse_deviation)


def norm_backward(incoming_gradient, standardized_rows, inverse_deviation, norm_gain):
    scaled_gradient = incoming_gradient * norm_gain.astype(jnp.float32)
    inner_product = (
        scaled_gradient
        - jnp.mean(scaled_gradient, axis=-1, keepdims=True)
        - standardized_rows * jnp.mean(scaled_gradient * standardized_rows, axis=-1, keepdims=True)
    )
    return (
        inverse_deviation * inner_product,
        jnp.sum(incoming_gradient * standardized_rows, axis=0),
        jnp.sum(incoming_gradient, axis=0),
    )


def slot_table(routes, experts, capacity):
    picked = (routes[:, :, None] == jnp.arange(experts, dtype=jnp.int32)[None, None, :]).astype(
        jnp.int32
    )
    flat = picked.reshape(-1, experts)
    before = jnp.cumsum(flat, axis=0) - flat
    number = jnp.sum(before * flat, axis=-1)
    slot = routes.reshape(-1) * capacity + number
    owner = jnp.arange(flat.shape[0], dtype=jnp.int32) // 2
    token_of_slot = jnp.zeros((experts * capacity,), jnp.int32).at[slot].set(owner)
    filled = jnp.zeros((experts * capacity,), jnp.int32).at[slot].set(1)
    return (picked, slot, token_of_slot, filled)


def split_heads(value, images):
    input_rows, width = value.shape
    return value.reshape(images, input_rows // images, width // HEAD_DIM, HEAD_DIM)


def live_keys(length):
    return (jnp.arange(length) < REAL_TOK)[None, None, None, :]


def attend(query, key, value, images):
    query_h = split_heads(query, images)
    key_h = split_heads(key, images)
    value_h = split_heads(value, images)
    scores = jnp.einsum(
        "ishd,ithd->ihst", query_h, key_h, preferred_element_type=jnp.float32
    ) * HEAD_DIM ** (-0.5)
    live = live_keys(scores.shape[-1])
    lse = jnp.log(jnp.sum(jnp.where(live, jnp.exp(scores), 0.0), axis=-1, keepdims=True))
    probs = jnp.where(live, jnp.exp(scores - lse), 0.0).astype(jnp.bfloat16)
    context = jnp.einsum(
        "ihst,ithd->ishd", probs, value_h, preferred_element_type=jnp.float32
    ).astype(jnp.bfloat16)
    return (context.reshape(query.shape), lse)


def attend_back(query, key, value, lse, context_grad, images):
    query_h = split_heads(query, images)
    key_h = split_heads(key, images)
    value_h = split_heads(value, images)
    grad_h = split_heads(context_grad, images)
    scores = jnp.einsum(
        "ishd,ithd->ihst", query_h, key_h, preferred_element_type=jnp.float32
    ) * HEAD_DIM ** (-0.5)
    live = live_keys(scores.shape[-1])
    probs = jnp.where(live, jnp.exp(scores - lse), 0.0)
    value_grad = jnp.einsum(
        "ihst,ishd->ithd", probs.astype(jnp.bfloat16), grad_h, preferred_element_type=jnp.float32
    ).astype(jnp.bfloat16)
    inner_product = jnp.einsum(
        "ishd,ithd->ihst", grad_h, value_h, preferred_element_type=jnp.float32
    )
    score_grad = (
        probs
        * (inner_product - jnp.sum(probs * inner_product, axis=-1, keepdims=True))
        * HEAD_DIM ** (-0.5)
    ).astype(jnp.bfloat16)
    query_grad = jnp.einsum(
        "ihst,ithd->ishd", score_grad, key_h, preferred_element_type=jnp.float32
    ).astype(jnp.bfloat16)
    key_grad = jnp.einsum(
        "ihst,ishd->ithd", score_grad, query_h, preferred_element_type=jnp.float32
    ).astype(jnp.bfloat16)
    shape = query.shape
    return (query_grad.reshape(shape), key_grad.reshape(shape), value_grad.reshape(shape))


def gather_dense(
    qkv_weight,
    proj_weight,
    router_weight,
    attention_norm_gain,
    attention_norm_shift,
    expert_norm_gain,
    expert_norm_shift,
):
    rows = qkv_weight.shape[1]
    heads_width = qkv_weight.shape[2]
    experts = router_weight.shape[1]
    packed = jnp.concatenate(
        [
            jnp.transpose(qkv_weight, (1, 0, 2)).reshape(rows, -1),
            proj_weight.T,
            router_weight,
            jnp.stack(
                [attention_norm_gain, attention_norm_shift, expert_norm_gain, expert_norm_shift],
                axis=1,
            ),
        ],
        axis=1,
    )
    holders = fsdp_size()
    spread = jnp.broadcast_to(packed[None], (holders,) + packed.shape)
    full = lax.all_to_all(spread, FSDP, split_axis=0, concat_axis=0, tiled=True)
    full = full.reshape(holders * rows, packed.shape[1])
    width = full.shape[0]
    at = 3 * heads_width
    qkv_full = jnp.transpose(full[:, :at].reshape(width, 3, heads_width), (1, 0, 2))
    proj_full = full[:, at : at + heads_width].T
    at += heads_width
    router_full = full[:, at : at + experts]
    at += experts
    norms = full[:, at : at + 4]
    return (qkv_full, proj_full, router_full, norms[:, 0], norms[:, 1], norms[:, 2], norms[:, 3])


def reduce_dense(qkv_part, proj_part, router_part, norm_parts):
    width = qkv_part.shape[1]
    heads_width = qkv_part.shape[2]
    experts = router_part.shape[1]
    packed = jnp.concatenate(
        [
            jnp.transpose(qkv_part, (1, 0, 2)).reshape(width, -1),
            proj_part.T,
            router_part,
            jnp.stack(norm_parts, axis=1),
        ],
        axis=1,
    )
    holders = fsdp_size()
    rows = width // holders
    moved = lax.all_to_all(
        packed.reshape(holders, rows, packed.shape[1]), FSDP, split_axis=0, concat_axis=0, tiled=True
    )
    part = jnp.sum(moved, axis=0)
    at = 3 * heads_width
    qkv_grad = jnp.transpose(part[:, :at].reshape(rows, 3, heads_width), (1, 0, 2))
    proj_grad = part[:, at : at + heads_width].T
    at += heads_width
    shared = lax.psum(part[:, at:], "tp")
    router_grad = shared[:, :experts]
    norm_grads = [shared[:, experts + i] for i in range(len(norm_parts))]
    return qkv_grad, proj_grad, router_grad, norm_grads


def group_rows(value):
    return lax.all_gather(value, "tp", axis=0, tiled=True)


def owned_rows(value):
    return lax.psum_scatter(value, "tp", scatter_dimension=0, tiled=True)


def to_owners(slots):
    moved = lax.all_to_all(slots, "fa", split_axis=0, concat_axis=0, tiled=True)
    return moved.reshape(-1, slots.shape[2])


def to_groups(result, experts, capacity):
    width = result.shape[1]
    pieces = result.astype(jnp.bfloat16).reshape(experts, capacity, width)
    moved = lax.all_to_all(pieces, "fa", split_axis=0, concat_axis=0, tiled=True)
    return moved.astype(jnp.float32)


def expert_weights(weight, holders):
    rows, experts, units = weight.shape
    spread = jnp.broadcast_to(weight[:, :, None, :], (rows, experts, holders, units))
    moved = lax.all_to_all(
        spread.reshape(rows, experts * holders, units), FSDP, split_axis=1, concat_axis=0, tiled=True
    )
    return moved.reshape(-1, units)


def weight_home(partial, experts, holders):
    width, units = partial.shape
    devices = experts * holders
    rows = width // devices
    moved = lax.all_to_all(
        partial.astype(jnp.bfloat16).reshape(devices, rows, units), FSDP, split_axis=0, concat_axis=0, tiled=True
    )
    summed = jnp.sum(moved.reshape(experts, holders, rows, units).astype(jnp.float32), axis=1)
    return jnp.transpose(summed, (1, 0, 2))


def per_device(
    inputs,
    routes,
    attention_norm_gain,
    attention_norm_shift,
    qkv_weight,
    proj_weight,
    expert_norm_gain,
    expert_norm_shift,
    router_weight,
    expert_in,
    expert_out,
    cotangent,
):
    f32 = jnp.float32
    bf16 = jnp.bfloat16
    dense = gather_dense(
        qkv_weight,
        proj_weight,
        router_weight,
        attention_norm_gain,
        attention_norm_shift,
        expert_norm_gain,
        expert_norm_shift,
    )
    qkv_full, proj_full, router_full, attention_gain, attention_shift, expert_gain, expert_shift = (
        dense
    )
    group = routes.shape[0]
    images = group // SEQ
    experts = router_full.shape[1]
    width = qkv_full.shape[1]
    units = expert_in.shape[2]
    local_rows = expert_in.shape[0]
    holders = fsdp_size() // experts
    block_units = units // holders
    attention_normed, attention_standardized, attention_inverse_deviation = normalize_rows(
        inputs, attention_gain, attention_shift
    )
    tokens_a = group_rows(attention_normed)
    proj = jnp.einsum("td,idh->ith", tokens_a, qkv_full, preferred_element_type=f32).astype(bf16)
    context, lse = attend(proj[0], proj[1], proj[2], images)
    residual_middle = inputs + owned_rows(jnp.dot(context, proj_full, preferred_element_type=f32))
    expert_normed, expert_standardized, expert_inverse_deviation = normalize_rows(
        residual_middle, expert_gain, expert_shift
    )
    tokens_m = group_rows(expert_normed)
    logits = jnp.dot(tokens_m, router_full, preferred_element_type=f32)
    raised = jnp.exp(logits)
    probs = raised / jnp.sum(raised, axis=-1, keepdims=True)
    picked, slot, token_of_slot, filled = slot_table(routes, experts, CAP)
    gates = jnp.sum(picked.astype(f32) * probs[:, None, :], axis=-1)
    slotted = jnp.where(filled[:, None] > 0, tokens_m[token_of_slot], jnp.zeros((), bf16)).reshape(
        experts, CAP, width
    )
    holders = lax.axis_size("fb")
    own_in = expert_weights(expert_in, holders)
    own_out = expert_weights(expert_out, holders)
    owner_x = to_owners(slotted)
    owner_pre = jnp.dot(owner_x, own_in, preferred_element_type=f32)
    owner_hidden = gelu_exact(owner_pre).astype(bf16)
    owner_res = jnp.einsum("cf,df->cd", owner_hidden, own_out, preferred_element_type=f32)
    expert_res = to_groups(owner_res, experts, CAP)
    routed = expert_res.reshape(experts * CAP, width)[slot].reshape(group, 2, width)
    outputs = residual_middle + owned_rows(jnp.sum(gates[:, :, None] * routed, axis=1))
    qkv_back, proj_back, router_back = qkv_full, proj_full, router_full
    attention_gain_gradient, expert_gain_gradient = attention_gain, expert_gain
    dout = group_rows(cotangent.astype(bf16))
    dout_f = dout.astype(f32)
    gate_of_slot = jnp.zeros((experts * CAP,), f32).at[slot].set(gates.reshape(-1))
    slot_grad = (
        jnp.where(filled[:, None] > 0, gate_of_slot[:, None] * dout_f[token_of_slot], 0.0)
        .astype(bf16)
        .reshape(experts, CAP, width)
    )
    gate_grad = jnp.sum(dout_f[:, None, :] * routed, axis=-1)
    owner_g = to_owners(slot_grad)
    owner_hgrad = jnp.dot(owner_g, own_out, preferred_element_type=f32)
    owner_pgrad = jax.vjp(gelu_exact, owner_pre)[1](owner_hgrad)[0].astype(bf16)
    owner_back = jnp.einsum("cf,df->cd", owner_pgrad, own_in, preferred_element_type=f32)
    slot_in_grad = to_groups(owner_back, experts, CAP)
    in_local = jnp.einsum("cd,cf->df", owner_x, owner_pgrad, preferred_element_type=f32)
    out_local = jnp.einsum("cd,cf->df", owner_g, owner_hidden, preferred_element_type=f32)
    in_grad = weight_home(in_local, experts, holders)
    out_grad = weight_home(out_local, experts, holders)
    choice_grad = jnp.sum(picked.astype(f32) * gate_grad[:, :, None], axis=1)
    logit_grad = probs * (choice_grad - jnp.sum(probs * choice_grad, axis=-1, keepdims=True))
    router_part = jnp.einsum("td,te->de", tokens_m.astype(f32), logit_grad, precision=TOP)
    routed_in = slot_in_grad.reshape(experts * CAP, width)[slot].reshape(group, 2, width)
    token_gradient = jnp.sum(routed_in, axis=1) + jnp.einsum(
        "te,de->td", logit_grad, router_back.astype(f32), precision=TOP
    )
    expert_norm_backward, expert_gain_partial, expert_shift_partial = norm_backward(
        owned_rows(token_gradient),
        expert_standardized,
        expert_inverse_deviation,
        expert_gain_gradient,
    )
    middle_grad = cotangent + expert_norm_backward
    mid_rows = group_rows(middle_grad.astype(bf16))
    proj_part = jnp.einsum("th,td->hd", context, mid_rows, preferred_element_type=f32)
    context_grad = jnp.einsum("td,hd->th", mid_rows, proj_back, preferred_element_type=f32).astype(
        bf16
    )
    query_grad, key_grad, value_grad = attend_back(
        proj[0], proj[1], proj[2], lse, context_grad, images
    )
    stacked = jnp.stack([query_grad, key_grad, value_grad])
    qkv_part = jnp.einsum("td,ith->idh", tokens_a, stacked, preferred_element_type=f32)
    attention_input_gradient = owned_rows(
        jnp.einsum("ith,idh->td", stacked, qkv_back, preferred_element_type=f32)
    )
    attention_norm_backward, attention_gain_partial, attention_shift_partial = norm_backward(
        attention_input_gradient,
        attention_standardized,
        attention_inverse_deviation,
        attention_gain_gradient,
    )
    input_grad = middle_grad + attention_norm_backward
    qkv_grad, proj_grad, router_grad, norm_grads = reduce_dense(
        qkv_part,
        proj_part,
        router_part,
        [attention_gain_partial, attention_shift_partial, expert_gain_partial, expert_shift_partial],
    )
    return (
        outputs,
        input_grad,
        norm_grads[0],
        norm_grads[1],
        qkv_grad,
        proj_grad,
        norm_grads[2],
        norm_grads[3],
        router_grad,
        in_grad,
        out_grad,
    )


def solution(mesh):
    fsdp = mesh.shape["fsdp"]
    sub = Mesh(
        mesh.devices.reshape(EXPERTS, fsdp // EXPERTS, mesh.shape["tp"]), ("fa", "fb", "tp")
    )
    return jax.shard_map(
        per_device,
        mesh=sub,
        in_specs=(
            P(("fa", "fb", "tp"), None),
            P(("fa", "fb"), None),
            P(("fa", "fb")),
            P(("fa", "fb")),
            P(None, ("fa", "fb"), "tp"),
            P("tp", ("fa", "fb")),
            P(("fa", "fb")),
            P(("fa", "fb")),
            P(("fa", "fb"), None),
            P(("fa", "fb"), None, "tp"),
            P(("fa", "fb"), None, "tp"),
            P(("fa", "fb", "tp"), None),
        ),
        out_specs=(
            P(("fa", "fb", "tp"), None),
            P(("fa", "fb", "tp"), None),
            P(("fa", "fb")),
            P(("fa", "fb")),
            P(None, ("fa", "fb"), "tp"),
            P("tp", ("fa", "fb")),
            P(("fa", "fb")),
            P(("fa", "fb")),
            P(("fa", "fb"), None),
            P(("fa", "fb"), None, "tp"),
            P(("fa", "fb"), None, "tp"),
        ),
        check_vma=False,
    )
```

```python
import jax
import jax.numpy as jnp
from jax import lax
from jax.sharding import Mesh, PartitionSpec as P

HEAD_DIM = 64
SEQ = 200
REAL_TOK = 197
CAP = 63
EXPERTS = 16
FSDP = ("fa", "fb")


EPS = 1e-06
TOP = lax.Precision.HIGHEST


def fsdp_size():
    return lax.axis_size("fa") * lax.axis_size("fb")


def gelu_exact(value):
    return jax.nn.gelu(value, approximate=False)


def normalize_rows(value, norm_gain, norm_shift):
    row_mean = jnp.mean(value, axis=-1, keepdims=True)
    centered_rows = value - row_mean
    inverse_deviation = lax.rsqrt(
        jnp.mean(centered_rows * centered_rows, axis=-1, keepdims=True) + EPS
    )
    standardized_rows = centered_rows * inverse_deviation
    normed_rows = (
        standardized_rows * norm_gain.astype(jnp.float32) + norm_shift.astype(jnp.float32)
    ).astype(jnp.bfloat16)
    return (normed_rows, standardized_rows, inverse_deviation)


def norm_backward(incoming_gradient, standardized_rows, inverse_deviation, norm_gain):
    scaled_gradient = incoming_gradient * norm_gain.astype(jnp.float32)
    inner_product = (
        scaled_gradient
        - jnp.mean(scaled_gradient, axis=-1, keepdims=True)
        - standardized_rows * jnp.mean(scaled_gradient * standardized_rows, axis=-1, keepdims=True)
    )
    return (
        inverse_deviation * inner_product,
        jnp.sum(incoming_gradient * standardized_rows, axis=0),
        jnp.sum(incoming_gradient, axis=0),
    )


def slot_table(routes, experts, capacity):
    picked = (routes[:, :, None] == jnp.arange(experts, dtype=jnp.int32)[None, None, :]).astype(
        jnp.int32
    )
    flat = picked.reshape(-1, experts)
    before = jnp.cumsum(flat, axis=0) - flat
    number = jnp.sum(before * flat, axis=-1)
    slot = routes.reshape(-1) * capacity + number
    owner = jnp.arange(flat.shape[0], dtype=jnp.int32) // 2
    token_of_slot = jnp.zeros((experts * capacity,), jnp.int32).at[slot].set(owner)
    filled = jnp.zeros((experts * capacity,), jnp.int32).at[slot].set(1)
    return (picked, slot, token_of_slot, filled)


def split_heads(value, images):
    input_rows, width = value.shape
    return value.reshape(images, input_rows // images, width // HEAD_DIM, HEAD_DIM)


def live_keys(length):
    return (jnp.arange(length) < REAL_TOK)[None, None, None, :]


def attend(query, key, value, images):
    query_h = split_heads(query, images)
    key_h = split_heads(key, images)
    value_h = split_heads(value, images)
    scores = jnp.einsum(
        "ishd,ithd->ihst", query_h, key_h, preferred_element_type=jnp.float32
    ) * HEAD_DIM ** (-0.5)
    live = live_keys(scores.shape[-1])
    lse = jnp.log(jnp.sum(jnp.where(live, jnp.exp(scores), 0.0), axis=-1, keepdims=True))
    probs = jnp.where(live, jnp.exp(scores - lse), 0.0).astype(jnp.bfloat16)
    context = jnp.einsum(
        "ihst,ithd->ishd", probs, value_h, preferred_element_type=jnp.float32
    ).astype(jnp.bfloat16)
    return (context.reshape(query.shape), lse)


def attend_back(query, key, value, lse, context_grad, images):
    query_h = split_heads(query, images)
    key_h = split_heads(key, images)
    value_h = split_heads(value, images)
    grad_h = split_heads(context_grad, images)
    scores = jnp.einsum(
        "ishd,ithd->ihst", query_h, key_h, preferred_element_type=jnp.float32
    ) * HEAD_DIM ** (-0.5)
    live = live_keys(scores.shape[-1])
    probs = jnp.where(live, jnp.exp(scores - lse), 0.0)
    value_grad = jnp.einsum(
        "ihst,ishd->ithd", probs.astype(jnp.bfloat16), grad_h, preferred_element_type=jnp.float32
    ).astype(jnp.bfloat16)
    inner_product = jnp.einsum(
        "ishd,ithd->ihst", grad_h, value_h, preferred_element_type=jnp.float32
    )
    score_grad = (
        probs
        * (inner_product - jnp.sum(probs * inner_product, axis=-1, keepdims=True))
        * HEAD_DIM ** (-0.5)
    ).astype(jnp.bfloat16)
    query_grad = jnp.einsum(
        "ihst,ithd->ishd", score_grad, key_h, preferred_element_type=jnp.float32
    ).astype(jnp.bfloat16)
    key_grad = jnp.einsum(
        "ihst,ishd->ithd", score_grad, query_h, preferred_element_type=jnp.float32
    ).astype(jnp.bfloat16)
    shape = query.shape
    return (query_grad.reshape(shape), key_grad.reshape(shape), value_grad.reshape(shape))


def gather_dense(
    qkv_weight,
    proj_weight,
    router_weight,
    attention_norm_gain,
    attention_norm_shift,
    expert_norm_gain,
    expert_norm_shift,
):
    rows = qkv_weight.shape[1]
    heads_width = qkv_weight.shape[2]
    experts = router_weight.shape[1]
    packed = jnp.concatenate(
        [
            jnp.transpose(qkv_weight, (1, 0, 2)).reshape(rows, -1),
            proj_weight.T,
            router_weight,
            jnp.stack(
                [attention_norm_gain, attention_norm_shift, expert_norm_gain, expert_norm_shift],
                axis=1,
            ),
        ],
        axis=1,
    )
    holders = fsdp_size()
    spread = jnp.broadcast_to(packed[None], (holders,) + packed.shape)
    full = lax.all_to_all(spread, FSDP, split_axis=0, concat_axis=0, tiled=True)
    full = full.reshape(holders * rows, packed.shape[1])
    width = full.shape[0]
    at = 3 * heads_width
    qkv_full = jnp.transpose(full[:, :at].reshape(width, 3, heads_width), (1, 0, 2))
    proj_full = full[:, at : at + heads_width].T
    at += heads_width
    router_full = full[:, at : at + experts]
    at += experts
    norms = full[:, at : at + 4]
    return (qkv_full, proj_full, router_full, norms[:, 0], norms[:, 1], norms[:, 2], norms[:, 3])


def reduce_dense(qkv_part, proj_part, router_part, norm_parts):
    width = qkv_part.shape[1]
    heads_width = qkv_part.shape[2]
    experts = router_part.shape[1]
    packed = jnp.concatenate(
        [
            jnp.transpose(qkv_part, (1, 0, 2)).reshape(width, -1),
            proj_part.T,
            router_part,
            jnp.stack(norm_parts, axis=1),
        ],
        axis=1,
    )
    holders = fsdp_size()
    rows = width // holders
    at = 4 * heads_width
    small = packed[:, at:]
    high = lax.reduce_precision(small, exponent_bits=8, mantissa_bits=7)
    wire = jnp.concatenate(
        [
            packed[:, :at].astype(jnp.bfloat16),
            high.astype(jnp.bfloat16),
            (small - high).astype(jnp.bfloat16),
        ],
        axis=1,
    )
    moved = lax.all_to_all(
        wire.reshape(holders, rows, wire.shape[1]), FSDP, split_axis=0, concat_axis=0, tiled=True
    ).astype(jnp.float32)
    count = small.shape[1]
    part = jnp.concatenate(
        [
            jnp.sum(moved[..., :at], axis=0),
            jnp.sum(moved[..., at : at + count] + moved[..., at + count :], axis=0),
        ],
        axis=1,
    )
    at = 3 * heads_width
    qkv_grad = jnp.transpose(part[:, :at].reshape(rows, 3, heads_width), (1, 0, 2))
    proj_grad = part[:, at : at + heads_width].T
    at += heads_width
    shared = lax.psum(part[:, at:], "tp")
    router_grad = shared[:, :experts]
    norm_grads = [shared[:, experts + i] for i in range(len(norm_parts))]
    return qkv_grad, proj_grad, router_grad, norm_grads


def group_rows(value):
    return lax.all_gather(value, "tp", axis=0, tiled=True)


def owned_rows(value):
    return lax.psum_scatter(value, "tp", scatter_dimension=0, tiled=True)


def to_owners(slots):
    moved = lax.all_to_all(slots, "fa", split_axis=0, concat_axis=0, tiled=True)
    return moved.reshape(-1, slots.shape[2])


def to_groups(result, experts, capacity):
    width = result.shape[1]
    pieces = result.astype(jnp.bfloat16).reshape(experts, capacity, width)
    moved = lax.all_to_all(pieces, "fa", split_axis=0, concat_axis=0, tiled=True)
    return moved.astype(jnp.float32)


def expert_weights(weight, holders):
    rows, experts, units = weight.shape
    spread = jnp.broadcast_to(weight[:, :, None, :], (rows, experts, holders, units))
    moved = lax.all_to_all(
        spread.reshape(rows, experts * holders, units), FSDP, split_axis=1, concat_axis=0, tiled=True
    )
    return moved.reshape(-1, units)


def weight_home(partial, experts, holders):
    width, units = partial.shape
    devices = experts * holders
    rows = width // devices
    moved = lax.all_to_all(
        partial.astype(jnp.bfloat16).reshape(devices, rows, units), FSDP, split_axis=0, concat_axis=0, tiled=True
    )
    summed = jnp.sum(moved.reshape(experts, holders, rows, units).astype(jnp.float32), axis=1)
    return jnp.transpose(summed, (1, 0, 2))


def per_device(
    inputs,
    routes,
    attention_norm_gain,
    attention_norm_shift,
    qkv_weight,
    proj_weight,
    expert_norm_gain,
    expert_norm_shift,
    router_weight,
    expert_in,
    expert_out,
    cotangent,
):
    f32 = jnp.float32
    bf16 = jnp.bfloat16
    dense = gather_dense(
        qkv_weight,
        proj_weight,
        router_weight,
        attention_norm_gain,
        attention_norm_shift,
        expert_norm_gain,
        expert_norm_shift,
    )
    qkv_full, proj_full, router_full, attention_gain, attention_shift, expert_gain, expert_shift = (
        dense
    )
    group = routes.shape[0]
    images = group // SEQ
    experts = router_full.shape[1]
    width = qkv_full.shape[1]
    units = expert_in.shape[2]
    local_rows = expert_in.shape[0]
    holders = fsdp_size() // experts
    block_units = units // holders
    attention_normed, attention_standardized, attention_inverse_deviation = normalize_rows(
        inputs, attention_gain, attention_shift
    )
    tokens_a = group_rows(attention_normed)
    proj = jnp.einsum("td,idh->ith", tokens_a, qkv_full, preferred_element_type=f32).astype(bf16)
    context, lse = attend(proj[0], proj[1], proj[2], images)
    residual_middle = inputs + owned_rows(jnp.dot(context, proj_full, preferred_element_type=f32))
    expert_normed, expert_standardized, expert_inverse_deviation = normalize_rows(
        residual_middle, expert_gain, expert_shift
    )
    tokens_m = group_rows(expert_normed)
    logits = jnp.dot(tokens_m, router_full, preferred_element_type=f32)
    raised = jnp.exp(logits)
    probs = raised / jnp.sum(raised, axis=-1, keepdims=True)
    picked, slot, token_of_slot, filled = slot_table(routes, experts, CAP)
    gates = jnp.sum(picked.astype(f32) * probs[:, None, :], axis=-1)
    slotted = jnp.where(filled[:, None] > 0, tokens_m[token_of_slot], jnp.zeros((), bf16)).reshape(
        experts, CAP, width
    )
    holders = lax.axis_size("fb")
    own_in = expert_weights(expert_in, holders)
    own_out = expert_weights(expert_out, holders)
    owner_x = to_owners(slotted)
    owner_pre = jnp.dot(owner_x, own_in, preferred_element_type=f32)
    owner_hidden = gelu_exact(owner_pre).astype(bf16)
    owner_res = jnp.einsum("cf,df->cd", owner_hidden, own_out, preferred_element_type=f32)
    expert_res = to_groups(owner_res, experts, CAP)
    routed = expert_res.reshape(experts * CAP, width)[slot].reshape(group, 2, width)
    outputs = residual_middle + owned_rows(jnp.sum(gates[:, :, None] * routed, axis=1))
    qkv_back, proj_back, router_back = qkv_full, proj_full, router_full
    attention_gain_gradient, expert_gain_gradient = attention_gain, expert_gain
    dout = group_rows(cotangent.astype(bf16))
    dout_f = dout.astype(f32)
    gate_of_slot = jnp.zeros((experts * CAP,), f32).at[slot].set(gates.reshape(-1))
    slot_grad = (
        jnp.where(filled[:, None] > 0, gate_of_slot[:, None] * dout_f[token_of_slot], 0.0)
        .astype(bf16)
        .reshape(experts, CAP, width)
    )
    gate_grad = jnp.sum(dout_f[:, None, :] * routed, axis=-1)
    owner_g = to_owners(slot_grad)
    owner_hgrad = jnp.dot(owner_g, own_out, preferred_element_type=f32)
    owner_pgrad = jax.vjp(gelu_exact, owner_pre)[1](owner_hgrad)[0].astype(bf16)
    owner_back = jnp.einsum("cf,df->cd", owner_pgrad, own_in, preferred_element_type=f32)
    slot_in_grad = to_groups(owner_back, experts, CAP)
    in_local = jnp.einsum("cd,cf->df", owner_x, owner_pgrad, preferred_element_type=f32)
    out_local = jnp.einsum("cd,cf->df", owner_g, owner_hidden, preferred_element_type=f32)
    in_grad = weight_home(in_local, experts, holders)
    out_grad = weight_home(out_local, experts, holders)
    choice_grad = jnp.sum(picked.astype(f32) * gate_grad[:, :, None], axis=1)
    logit_grad = probs * (choice_grad - jnp.sum(probs * choice_grad, axis=-1, keepdims=True))
    router_part = jnp.einsum("td,te->de", tokens_m.astype(f32), logit_grad, precision=TOP)
    routed_in = slot_in_grad.reshape(experts * CAP, width)[slot].reshape(group, 2, width)
    token_gradient = jnp.sum(routed_in, axis=1) + jnp.einsum(
        "te,de->td", logit_grad, router_back.astype(f32), precision=TOP
    )
    expert_norm_backward, expert_gain_partial, expert_shift_partial = norm_backward(
        owned_rows(token_gradient),
        expert_standardized,
        expert_inverse_deviation,
        expert_gain_gradient,
    )
    middle_grad = cotangent + expert_norm_backward
    mid_rows = group_rows(middle_grad.astype(bf16))
    proj_part = jnp.einsum("th,td->hd", context, mid_rows, preferred_element_type=f32)
    context_grad = jnp.einsum("td,hd->th", mid_rows, proj_back, preferred_element_type=f32).astype(
        bf16
    )
    query_grad, key_grad, value_grad = attend_back(
        proj[0], proj[1], proj[2], lse, context_grad, images
    )
    stacked = jnp.stack([query_grad, key_grad, value_grad])
    qkv_part = jnp.einsum("td,ith->idh", tokens_a, stacked, preferred_element_type=f32)
    attention_input_gradient = owned_rows(
        jnp.einsum("ith,idh->td", stacked, qkv_back, preferred_element_type=f32)
    )
    attention_norm_backward, attention_gain_partial, attention_shift_partial = norm_backward(
        attention_input_gradient,
        attention_standardized,
        attention_inverse_deviation,
        attention_gain_gradient,
    )
    input_grad = middle_grad + attention_norm_backward
    qkv_grad, proj_grad, router_grad, norm_grads = reduce_dense(
        qkv_part,
        proj_part,
        router_part,
        [attention_gain_partial, attention_shift_partial, expert_gain_partial, expert_shift_partial],
    )
    return (
        outputs,
        input_grad,
        norm_grads[0],
        norm_grads[1],
        qkv_grad,
        proj_grad,
        norm_grads[2],
        norm_grads[3],
        router_grad,
        in_grad,
        out_grad,
    )


def solution(mesh):
    fsdp = mesh.shape["fsdp"]
    sub = Mesh(
        mesh.devices.reshape(EXPERTS, fsdp // EXPERTS, mesh.shape["tp"]), ("fa", "fb", "tp")
    )
    return jax.shard_map(
        per_device,
        mesh=sub,
        in_specs=(
            P(("fa", "fb", "tp"), None),
            P(("fa", "fb"), None),
            P(("fa", "fb")),
            P(("fa", "fb")),
            P(None, ("fa", "fb"), "tp"),
            P("tp", ("fa", "fb")),
            P(("fa", "fb")),
            P(("fa", "fb")),
            P(("fa", "fb"), None),
            P(("fa", "fb"), None, "tp"),
            P(("fa", "fb"), None, "tp"),
            P(("fa", "fb", "tp"), None),
        ),
        out_specs=(
            P(("fa", "fb", "tp"), None),
            P(("fa", "fb", "tp"), None),
            P(("fa", "fb")),
            P(("fa", "fb")),
            P(None, ("fa", "fb"), "tp"),
            P("tp", ("fa", "fb")),
            P(("fa", "fb")),
            P(("fa", "fb")),
            P(("fa", "fb"), None),
            P(("fa", "fb"), None, "tp"),
            P(("fa", "fb"), None, "tp"),
        ),
        check_vma=False,
    )
```

```python
import jax
import jax.numpy as jnp
from jax import lax
from jax.sharding import Mesh, PartitionSpec as P

HEAD_DIM = 64
SEQ = 200
REAL_TOK = 197
CAP = 63
EXPERTS = 16
FSDP = ("fa", "fb")


EPS = 1e-06
TOP = lax.Precision.HIGHEST


def fsdp_size():
    return lax.axis_size("fa") * lax.axis_size("fb")


def gelu_exact(value):
    return jax.nn.gelu(value, approximate=False)


def normalize_rows(value, norm_gain, norm_shift):
    row_mean = jnp.mean(value, axis=-1, keepdims=True)
    centered_rows = value - row_mean
    inverse_deviation = lax.rsqrt(
        jnp.mean(centered_rows * centered_rows, axis=-1, keepdims=True) + EPS
    )
    standardized_rows = centered_rows * inverse_deviation
    normed_rows = (
        standardized_rows * norm_gain.astype(jnp.float32) + norm_shift.astype(jnp.float32)
    ).astype(jnp.bfloat16)
    return (normed_rows, standardized_rows, inverse_deviation)


def norm_backward(incoming_gradient, standardized_rows, inverse_deviation, norm_gain):
    scaled_gradient = incoming_gradient * norm_gain.astype(jnp.float32)
    inner_product = (
        scaled_gradient
        - jnp.mean(scaled_gradient, axis=-1, keepdims=True)
        - standardized_rows * jnp.mean(scaled_gradient * standardized_rows, axis=-1, keepdims=True)
    )
    return (
        inverse_deviation * inner_product,
        jnp.sum(incoming_gradient * standardized_rows, axis=0),
        jnp.sum(incoming_gradient, axis=0),
    )


def slot_table(routes, experts, capacity):
    picked = (routes[:, :, None] == jnp.arange(experts, dtype=jnp.int32)[None, None, :]).astype(
        jnp.int32
    )
    flat = picked.reshape(-1, experts)
    before = jnp.cumsum(flat, axis=0) - flat
    number = jnp.sum(before * flat, axis=-1)
    slot = routes.reshape(-1) * capacity + number
    owner = jnp.arange(flat.shape[0], dtype=jnp.int32) // 2
    token_of_slot = jnp.zeros((experts * capacity,), jnp.int32).at[slot].set(owner)
    filled = jnp.zeros((experts * capacity,), jnp.int32).at[slot].set(1)
    return (picked, slot, token_of_slot, filled)


def split_heads(value, images):
    input_rows, width = value.shape
    return value.reshape(images, input_rows // images, width // HEAD_DIM, HEAD_DIM)


def live_keys(length):
    return (jnp.arange(length) < REAL_TOK)[None, None, None, :]


def attend(query, key, value, images):
    query_h = split_heads(query, images)
    key_h = split_heads(key, images)
    value_h = split_heads(value, images)
    scores = jnp.einsum(
        "ishd,ithd->ihst", query_h, key_h, preferred_element_type=jnp.float32
    ) * HEAD_DIM ** (-0.5)
    live = live_keys(scores.shape[-1])
    lse = jnp.log(jnp.sum(jnp.where(live, jnp.exp(scores), 0.0), axis=-1, keepdims=True))
    probs = jnp.where(live, jnp.exp(scores - lse), 0.0).astype(jnp.bfloat16)
    context = jnp.einsum(
        "ihst,ithd->ishd", probs, value_h, preferred_element_type=jnp.float32
    ).astype(jnp.bfloat16)
    return (context.reshape(query.shape), lse)


def attend_back(query, key, value, lse, context_grad, images):
    query_h = split_heads(query, images)
    key_h = split_heads(key, images)
    value_h = split_heads(value, images)
    grad_h = split_heads(context_grad, images)
    scores = jnp.einsum(
        "ishd,ithd->ihst", query_h, key_h, preferred_element_type=jnp.float32
    ) * HEAD_DIM ** (-0.5)
    live = live_keys(scores.shape[-1])
    probs = jnp.where(live, jnp.exp(scores - lse), 0.0)
    value_grad = jnp.einsum(
        "ihst,ishd->ithd", probs.astype(jnp.bfloat16), grad_h, preferred_element_type=jnp.float32
    ).astype(jnp.bfloat16)
    inner_product = jnp.einsum(
        "ishd,ithd->ihst", grad_h, value_h, preferred_element_type=jnp.float32
    )
    score_grad = (
        probs
        * (inner_product - jnp.sum(probs * inner_product, axis=-1, keepdims=True))
        * HEAD_DIM ** (-0.5)
    ).astype(jnp.bfloat16)
    query_grad = jnp.einsum(
        "ihst,ithd->ishd", score_grad, key_h, preferred_element_type=jnp.float32
    ).astype(jnp.bfloat16)
    key_grad = jnp.einsum(
        "ihst,ishd->ithd", score_grad, query_h, preferred_element_type=jnp.float32
    ).astype(jnp.bfloat16)
    shape = query.shape
    return (query_grad.reshape(shape), key_grad.reshape(shape), value_grad.reshape(shape))


def gather_dense(
    qkv_weight,
    proj_weight,
    router_weight,
    attention_norm_gain,
    attention_norm_shift,
    expert_norm_gain,
    expert_norm_shift,
):
    rows = qkv_weight.shape[1]
    heads_width = qkv_weight.shape[2]
    experts = router_weight.shape[1]
    packed = jnp.concatenate(
        [
            jnp.transpose(qkv_weight, (1, 0, 2)).reshape(rows, -1),
            proj_weight.T,
            router_weight,
            jnp.stack(
                [attention_norm_gain, attention_norm_shift, expert_norm_gain, expert_norm_shift],
                axis=1,
            ),
        ],
        axis=1,
    )
    holders = fsdp_size()
    spread = jnp.broadcast_to(packed[None], (holders,) + packed.shape)
    full = lax.all_to_all(spread, FSDP, split_axis=0, concat_axis=0, tiled=True)
    full = full.reshape(holders * rows, packed.shape[1])
    width = full.shape[0]
    at = 3 * heads_width
    qkv_full = jnp.transpose(full[:, :at].reshape(width, 3, heads_width), (1, 0, 2))
    proj_full = full[:, at : at + heads_width].T
    at += heads_width
    router_full = full[:, at : at + experts]
    at += experts
    norms = full[:, at : at + 4]
    return (qkv_full, proj_full, router_full, norms[:, 0], norms[:, 1], norms[:, 2], norms[:, 3])


def reduce_dense(qkv_part, proj_part, router_part, norm_parts):
    width = qkv_part.shape[1]
    heads_width = qkv_part.shape[2]
    experts = router_part.shape[1]
    packed = jnp.concatenate(
        [
            jnp.transpose(qkv_part, (1, 0, 2)).reshape(width, -1),
            proj_part.T,
            router_part,
            jnp.stack(norm_parts, axis=1),
        ],
        axis=1,
    )
    holders = fsdp_size()
    rows = width // holders
    at = 4 * heads_width
    small = packed[:, at:]
    high = lax.reduce_precision(small, exponent_bits=8, mantissa_bits=7)
    wire = jnp.concatenate(
        [
            packed[:, :at].astype(jnp.bfloat16),
            high.astype(jnp.bfloat16),
            (small - high).astype(jnp.bfloat16),
        ],
        axis=1,
    )
    moved = lax.all_to_all(
        wire.reshape(holders, rows, wire.shape[1]), FSDP, split_axis=0, concat_axis=0, tiled=True
    ).astype(jnp.float32)
    count = small.shape[1]
    part = jnp.concatenate(
        [
            jnp.sum(moved[..., :at], axis=0),
            jnp.sum(moved[..., at : at + count] + moved[..., at + count :], axis=0),
        ],
        axis=1,
    )
    at = 3 * heads_width
    qkv_grad = jnp.transpose(part[:, :at].reshape(rows, 3, heads_width), (1, 0, 2))
    proj_grad = part[:, at : at + heads_width].T
    at += heads_width
    shared = lax.psum(part[:, at:], "tp")
    router_grad = shared[:, :experts]
    norm_grads = [shared[:, experts + i] for i in range(len(norm_parts))]
    return qkv_grad, proj_grad, router_grad, norm_grads


def group_rows(value):
    halves = lax.axis_size("tp")
    spread = jnp.broadcast_to(value[None], (halves,) + value.shape)
    moved = lax.all_to_all(spread, "tp", split_axis=0, concat_axis=0, tiled=True)
    return moved.reshape(-1, value.shape[1])


def owned_rows(value):
    halves = lax.axis_size("tp")
    moved = lax.all_to_all(
        value.reshape(halves, -1, value.shape[1]), "tp", split_axis=0, concat_axis=0, tiled=True
    )
    return jnp.sum(moved, axis=0)


def to_owners(slots):
    moved = lax.all_to_all(slots, "fa", split_axis=0, concat_axis=0, tiled=True)
    return moved.reshape(-1, slots.shape[2])


def to_groups(result, experts, capacity):
    width = result.shape[1]
    pieces = result.astype(jnp.bfloat16).reshape(experts, capacity, width)
    moved = lax.all_to_all(pieces, "fa", split_axis=0, concat_axis=0, tiled=True)
    return moved.astype(jnp.float32)


def expert_weights(weight, holders):
    rows, experts, units = weight.shape
    spread = jnp.broadcast_to(weight[:, :, None, :], (rows, experts, holders, units))
    moved = lax.all_to_all(
        spread.reshape(rows, experts * holders, units), FSDP, split_axis=1, concat_axis=0, tiled=True
    )
    return moved.reshape(-1, units)


def weight_home(partial, experts, holders):
    width, units = partial.shape
    devices = experts * holders
    rows = width // devices
    moved = lax.all_to_all(
        partial.astype(jnp.bfloat16).reshape(devices, rows, units), FSDP, split_axis=0, concat_axis=0, tiled=True
    )
    summed = jnp.sum(moved.reshape(experts, holders, rows, units).astype(jnp.float32), axis=1)
    return jnp.transpose(summed, (1, 0, 2))


def per_device(
    inputs,
    routes,
    attention_norm_gain,
    attention_norm_shift,
    qkv_weight,
    proj_weight,
    expert_norm_gain,
    expert_norm_shift,
    router_weight,
    expert_in,
    expert_out,
    cotangent,
):
    f32 = jnp.float32
    bf16 = jnp.bfloat16
    dense = gather_dense(
        qkv_weight,
        proj_weight,
        router_weight,
        attention_norm_gain,
        attention_norm_shift,
        expert_norm_gain,
        expert_norm_shift,
    )
    qkv_full, proj_full, router_full, attention_gain, attention_shift, expert_gain, expert_shift = (
        dense
    )
    group = routes.shape[0]
    images = group // SEQ
    experts = router_full.shape[1]
    width = qkv_full.shape[1]
    units = expert_in.shape[2]
    local_rows = expert_in.shape[0]
    holders = fsdp_size() // experts
    block_units = units // holders
    attention_normed, attention_standardized, attention_inverse_deviation = normalize_rows(
        inputs, attention_gain, attention_shift
    )
    tokens_a = group_rows(attention_normed)
    proj = jnp.einsum("td,idh->ith", tokens_a, qkv_full, preferred_element_type=f32).astype(bf16)
    context, lse = attend(proj[0], proj[1], proj[2], images)
    residual_middle = inputs + owned_rows(jnp.dot(context, proj_full, preferred_element_type=f32))
    expert_normed, expert_standardized, expert_inverse_deviation = normalize_rows(
        residual_middle, expert_gain, expert_shift
    )
    tokens_m = group_rows(expert_normed)
    logits = jnp.dot(tokens_m, router_full, preferred_element_type=f32)
    raised = jnp.exp(logits)
    probs = raised / jnp.sum(raised, axis=-1, keepdims=True)
    picked, slot, token_of_slot, filled = slot_table(routes, experts, CAP)
    gates = jnp.sum(picked.astype(f32) * probs[:, None, :], axis=-1)
    slotted = jnp.where(filled[:, None] > 0, tokens_m[token_of_slot], jnp.zeros((), bf16)).reshape(
        experts, CAP, width
    )
    holders = lax.axis_size("fb")
    own_in = expert_weights(expert_in, holders)
    own_out = expert_weights(expert_out, holders)
    owner_x = to_owners(slotted)
    owner_pre = jnp.dot(owner_x, own_in, preferred_element_type=f32)
    owner_hidden = gelu_exact(owner_pre).astype(bf16)
    owner_res = jnp.einsum("cf,df->cd", owner_hidden, own_out, preferred_element_type=f32)
    expert_res = to_groups(owner_res, experts, CAP)
    routed = expert_res.reshape(experts * CAP, width)[slot].reshape(group, 2, width)
    outputs = residual_middle + owned_rows(jnp.sum(gates[:, :, None] * routed, axis=1))
    qkv_back, proj_back, router_back = qkv_full, proj_full, router_full
    attention_gain_gradient, expert_gain_gradient = attention_gain, expert_gain
    dout = group_rows(cotangent.astype(bf16))
    dout_f = dout.astype(f32)
    gate_of_slot = jnp.zeros((experts * CAP,), f32).at[slot].set(gates.reshape(-1))
    slot_grad = (
        jnp.where(filled[:, None] > 0, gate_of_slot[:, None] * dout_f[token_of_slot], 0.0)
        .astype(bf16)
        .reshape(experts, CAP, width)
    )
    gate_grad = jnp.sum(dout_f[:, None, :] * routed, axis=-1)
    owner_g = to_owners(slot_grad)
    owner_hgrad = jnp.dot(owner_g, own_out, preferred_element_type=f32)
    owner_pgrad = jax.vjp(gelu_exact, owner_pre)[1](owner_hgrad)[0].astype(bf16)
    owner_back = jnp.einsum("cf,df->cd", owner_pgrad, own_in, preferred_element_type=f32)
    slot_in_grad = to_groups(owner_back, experts, CAP)
    in_local = jnp.einsum("cd,cf->df", owner_x, owner_pgrad, preferred_element_type=f32)
    out_local = jnp.einsum("cd,cf->df", owner_g, owner_hidden, preferred_element_type=f32)
    in_grad = weight_home(in_local, experts, holders)
    out_grad = weight_home(out_local, experts, holders)
    choice_grad = jnp.sum(picked.astype(f32) * gate_grad[:, :, None], axis=1)
    logit_grad = probs * (choice_grad - jnp.sum(probs * choice_grad, axis=-1, keepdims=True))
    router_part = jnp.einsum("td,te->de", tokens_m.astype(f32), logit_grad, precision=TOP)
    routed_in = slot_in_grad.reshape(experts * CAP, width)[slot].reshape(group, 2, width)
    token_gradient = jnp.sum(routed_in, axis=1) + jnp.einsum(
        "te,de->td", logit_grad, router_back.astype(f32), precision=TOP
    )
    expert_norm_backward, expert_gain_partial, expert_shift_partial = norm_backward(
        owned_rows(token_gradient),
        expert_standardized,
        expert_inverse_deviation,
        expert_gain_gradient,
    )
    middle_grad = cotangent + expert_norm_backward
    mid_rows = group_rows(middle_grad.astype(bf16))
    proj_part = jnp.einsum("th,td->hd", context, mid_rows, preferred_element_type=f32)
    context_grad = jnp.einsum("td,hd->th", mid_rows, proj_back, preferred_element_type=f32).astype(
        bf16
    )
    query_grad, key_grad, value_grad = attend_back(
        proj[0], proj[1], proj[2], lse, context_grad, images
    )
    stacked = jnp.stack([query_grad, key_grad, value_grad])
    qkv_part = jnp.einsum("td,ith->idh", tokens_a, stacked, preferred_element_type=f32)
    attention_input_gradient = owned_rows(
        jnp.einsum("ith,idh->td", stacked, qkv_back, preferred_element_type=f32)
    )
    attention_norm_backward, attention_gain_partial, attention_shift_partial = norm_backward(
        attention_input_gradient,
        attention_standardized,
        attention_inverse_deviation,
        attention_gain_gradient,
    )
    input_grad = middle_grad + attention_norm_backward
    qkv_grad, proj_grad, router_grad, norm_grads = reduce_dense(
        qkv_part,
        proj_part,
        router_part,
        [attention_gain_partial, attention_shift_partial, expert_gain_partial, expert_shift_partial],
    )
    return (
        outputs,
        input_grad,
        norm_grads[0],
        norm_grads[1],
        qkv_grad,
        proj_grad,
        norm_grads[2],
        norm_grads[3],
        router_grad,
        in_grad,
        out_grad,
    )


def solution(mesh):
    fsdp = mesh.shape["fsdp"]
    sub = Mesh(
        mesh.devices.reshape(EXPERTS, fsdp // EXPERTS, mesh.shape["tp"]), ("fa", "fb", "tp")
    )
    return jax.shard_map(
        per_device,
        mesh=sub,
        in_specs=(
            P(("fa", "fb", "tp"), None),
            P(("fa", "fb"), None),
            P(("fa", "fb")),
            P(("fa", "fb")),
            P(None, ("fa", "fb"), "tp"),
            P("tp", ("fa", "fb")),
            P(("fa", "fb")),
            P(("fa", "fb")),
            P(("fa", "fb"), None),
            P(("fa", "fb"), None, "tp"),
            P(("fa", "fb"), None, "tp"),
            P(("fa", "fb", "tp"), None),
        ),
        out_specs=(
            P(("fa", "fb", "tp"), None),
            P(("fa", "fb", "tp"), None),
            P(("fa", "fb")),
            P(("fa", "fb")),
            P(None, ("fa", "fb"), "tp"),
            P("tp", ("fa", "fb")),
            P(("fa", "fb")),
            P(("fa", "fb")),
            P(("fa", "fb"), None),
            P(("fa", "fb"), None, "tp"),
            P(("fa", "fb"), None, "tp"),
        ),
        check_vma=False,
    )
```

```python
import jax
import jax.numpy as jnp
from jax import lax
from jax.sharding import Mesh, PartitionSpec as P

HEAD_DIM = 64
SEQ = 200
REAL_TOK = 197
CAP = 63
EXPERTS = 16
FSDP = ("fa", "fb")


EPS = 1e-06
TOP = lax.Precision.HIGHEST


def fsdp_size():
    return lax.axis_size("fa") * lax.axis_size("fb")


def gelu_exact(value):
    return jax.nn.gelu(value, approximate=False)


def normalize_rows(value, norm_gain, norm_shift):
    row_mean = jnp.mean(value, axis=-1, keepdims=True)
    centered_rows = value - row_mean
    inverse_deviation = lax.rsqrt(
        jnp.mean(centered_rows * centered_rows, axis=-1, keepdims=True) + EPS
    )
    standardized_rows = centered_rows * inverse_deviation
    normed_rows = (
        standardized_rows * norm_gain.astype(jnp.float32) + norm_shift.astype(jnp.float32)
    ).astype(jnp.bfloat16)
    return (normed_rows, standardized_rows, inverse_deviation)


def norm_backward(incoming_gradient, standardized_rows, inverse_deviation, norm_gain):
    scaled_gradient = incoming_gradient * norm_gain.astype(jnp.float32)
    inner_product = (
        scaled_gradient
        - jnp.mean(scaled_gradient, axis=-1, keepdims=True)
        - standardized_rows * jnp.mean(scaled_gradient * standardized_rows, axis=-1, keepdims=True)
    )
    return (
        inverse_deviation * inner_product,
        jnp.sum(incoming_gradient * standardized_rows, axis=0),
        jnp.sum(incoming_gradient, axis=0),
    )


def slot_table(routes, experts, capacity):
    picked = (routes[:, :, None] == jnp.arange(experts, dtype=jnp.int32)[None, None, :]).astype(
        jnp.int32
    )
    flat = picked.reshape(-1, experts)
    before = jnp.cumsum(flat, axis=0) - flat
    number = jnp.sum(before * flat, axis=-1)
    slot = routes.reshape(-1) * capacity + number
    owner = jnp.arange(flat.shape[0], dtype=jnp.int32) // 2
    token_of_slot = jnp.zeros((experts * capacity,), jnp.int32).at[slot].set(owner)
    filled = jnp.zeros((experts * capacity,), jnp.int32).at[slot].set(1)
    return (picked, slot, token_of_slot, filled)


def split_heads(value, images):
    input_rows, width = value.shape
    return value.reshape(images, input_rows // images, width // HEAD_DIM, HEAD_DIM)


def live_keys(length):
    return (jnp.arange(length) < REAL_TOK)[None, None, None, :]


def attend(query, key, value, images):
    query_h = split_heads(query, images)
    key_h = split_heads(key, images)
    value_h = split_heads(value, images)
    scores = jnp.einsum(
        "ishd,ithd->ihst", query_h, key_h, preferred_element_type=jnp.float32
    ) * HEAD_DIM ** (-0.5)
    live = live_keys(scores.shape[-1])
    lse = jnp.log(jnp.sum(jnp.where(live, jnp.exp(scores), 0.0), axis=-1, keepdims=True))
    probs = jnp.where(live, jnp.exp(scores - lse), 0.0).astype(jnp.bfloat16)
    context = jnp.einsum(
        "ihst,ithd->ishd", probs, value_h, preferred_element_type=jnp.float32
    ).astype(jnp.bfloat16)
    return (context.reshape(query.shape), lse)


def attend_back(query, key, value, lse, context_grad, images):
    query_h = split_heads(query, images)
    key_h = split_heads(key, images)
    value_h = split_heads(value, images)
    grad_h = split_heads(context_grad, images)
    scores = jnp.einsum(
        "ishd,ithd->ihst", query_h, key_h, preferred_element_type=jnp.float32
    ) * HEAD_DIM ** (-0.5)
    live = live_keys(scores.shape[-1])
    probs = jnp.where(live, jnp.exp(scores - lse), 0.0)
    value_grad = jnp.einsum(
        "ihst,ishd->ithd", probs.astype(jnp.bfloat16), grad_h, preferred_element_type=jnp.float32
    ).astype(jnp.bfloat16)
    inner_product = jnp.einsum(
        "ishd,ithd->ihst", grad_h, value_h, preferred_element_type=jnp.float32
    )
    score_grad = (
        probs
        * (inner_product - jnp.sum(probs * inner_product, axis=-1, keepdims=True))
        * HEAD_DIM ** (-0.5)
    ).astype(jnp.bfloat16)
    query_grad = jnp.einsum(
        "ihst,ithd->ishd", score_grad, key_h, preferred_element_type=jnp.float32
    ).astype(jnp.bfloat16)
    key_grad = jnp.einsum(
        "ihst,ishd->ithd", score_grad, query_h, preferred_element_type=jnp.float32
    ).astype(jnp.bfloat16)
    shape = query.shape
    return (query_grad.reshape(shape), key_grad.reshape(shape), value_grad.reshape(shape))


def gather_dense(
    qkv_weight,
    proj_weight,
    router_weight,
    attention_norm_gain,
    attention_norm_shift,
    expert_norm_gain,
    expert_norm_shift,
):
    rows = qkv_weight.shape[1]
    heads_width = qkv_weight.shape[2]
    experts = router_weight.shape[1]
    packed = jnp.concatenate(
        [
            jnp.transpose(qkv_weight, (1, 0, 2)).reshape(rows, -1),
            proj_weight.T,
            router_weight,
            jnp.stack(
                [attention_norm_gain, attention_norm_shift, expert_norm_gain, expert_norm_shift],
                axis=1,
            ),
        ],
        axis=1,
    )
    holders = fsdp_size()
    spread = jnp.broadcast_to(packed[None], (holders,) + packed.shape)
    full = lax.all_to_all(spread, FSDP, split_axis=0, concat_axis=0, tiled=True)
    full = full.reshape(holders * rows, packed.shape[1])
    width = full.shape[0]
    at = 3 * heads_width
    qkv_full = jnp.transpose(full[:, :at].reshape(width, 3, heads_width), (1, 0, 2))
    proj_full = full[:, at : at + heads_width].T
    at += heads_width
    router_full = full[:, at : at + experts]
    at += experts
    norms = full[:, at : at + 4]
    return (qkv_full, proj_full, router_full, norms[:, 0], norms[:, 1], norms[:, 2], norms[:, 3])


def reduce_dense(qkv_part, proj_part, router_part, norm_parts):
    width = qkv_part.shape[1]
    heads_width = qkv_part.shape[2]
    experts = router_part.shape[1]
    packed = jnp.concatenate(
        [
            jnp.transpose(qkv_part, (1, 0, 2)).reshape(width, -1),
            proj_part.T,
            router_part,
            jnp.stack(norm_parts, axis=1),
        ],
        axis=1,
    )
    holders = fsdp_size()
    rows = width // holders
    at = 4 * heads_width
    small = packed[:, at:]
    high = lax.reduce_precision(small, exponent_bits=8, mantissa_bits=7)
    wire = jnp.concatenate(
        [
            packed[:, :at].astype(jnp.bfloat16),
            high.astype(jnp.bfloat16),
            (small - high).astype(jnp.bfloat16),
        ],
        axis=1,
    )
    moved = lax.all_to_all(
        wire.reshape(holders, rows, wire.shape[1]), FSDP, split_axis=0, concat_axis=0, tiled=True
    ).astype(jnp.float32)
    count = small.shape[1]
    part = jnp.concatenate(
        [
            jnp.sum(moved[..., :at], axis=0),
            jnp.sum(moved[..., at : at + count] + moved[..., at + count :], axis=0),
        ],
        axis=1,
    )
    at = 3 * heads_width
    qkv_grad = jnp.transpose(part[:, :at].reshape(rows, 3, heads_width), (1, 0, 2))
    proj_grad = part[:, at : at + heads_width].T
    at += heads_width
    shared = lax.psum(part[:, at:], "tp")
    router_grad = shared[:, :experts]
    norm_grads = [shared[:, experts + i] for i in range(len(norm_parts))]
    return qkv_grad, proj_grad, router_grad, norm_grads


def group_rows(value):
    halves = lax.axis_size("tp")
    spread = jnp.broadcast_to(value[None], (halves,) + value.shape)
    moved = lax.all_to_all(spread, "tp", split_axis=0, concat_axis=0, tiled=True)
    return moved.reshape(-1, value.shape[1])


def owned_rows(value):
    halves = lax.axis_size("tp")
    moved = lax.all_to_all(
        value.reshape(halves, -1, value.shape[1]), "tp", split_axis=0, concat_axis=0, tiled=True
    )
    return jnp.sum(moved, axis=0)


def to_owners(slots):
    moved = lax.all_to_all(slots, "fa", split_axis=0, concat_axis=0, tiled=True)
    return moved.reshape(-1, slots.shape[2])


def to_groups(result, experts, capacity):
    width = result.shape[1]
    pieces = result.astype(jnp.bfloat16).reshape(experts, capacity, width)
    moved = lax.all_to_all(pieces, "fa", split_axis=0, concat_axis=0, tiled=True)
    return moved.astype(jnp.float32)


def expert_weights(weight, holders):
    rows, experts, units = weight.shape
    spread = jnp.broadcast_to(weight[:, :, None, :], (rows, experts, holders, units))
    moved = lax.all_to_all(
        spread.reshape(rows, experts * holders, units), FSDP, split_axis=1, concat_axis=0, tiled=True
    )
    return moved.reshape(-1, units)


def weight_home(partial, experts, holders):
    width, units = partial.shape
    devices = experts * holders
    rows = width // devices
    moved = lax.all_to_all(
        partial.astype(jnp.bfloat16).reshape(devices, rows, units), FSDP, split_axis=0, concat_axis=0, tiled=True
    )
    summed = jnp.sum(moved.reshape(experts, holders, rows, units).astype(jnp.float32), axis=1)
    return jnp.transpose(summed, (1, 0, 2))


def per_device(
    inputs,
    routes,
    attention_norm_gain,
    attention_norm_shift,
    qkv_weight,
    proj_weight,
    expert_norm_gain,
    expert_norm_shift,
    router_weight,
    expert_in,
    expert_out,
    cotangent,
):
    f32 = jnp.float32
    bf16 = jnp.bfloat16
    dense = gather_dense(
        qkv_weight,
        proj_weight,
        router_weight,
        attention_norm_gain,
        attention_norm_shift,
        expert_norm_gain,
        expert_norm_shift,
    )
    qkv_full, proj_full, router_full, attention_gain, attention_shift, expert_gain, expert_shift = (
        dense
    )
    group = routes.shape[0]
    images = group // SEQ
    experts = router_full.shape[1]
    width = qkv_full.shape[1]
    units = expert_in.shape[2]
    local_rows = expert_in.shape[0]
    holders = fsdp_size() // experts
    block_units = units // holders
    attention_normed, attention_standardized, attention_inverse_deviation = normalize_rows(
        inputs, attention_gain, attention_shift
    )
    tokens_a = group_rows(attention_normed)
    proj = jnp.einsum("td,idh->ith", tokens_a, qkv_full, preferred_element_type=f32).astype(bf16)
    context, lse = attend(proj[0], proj[1], proj[2], images)
    residual_middle = inputs + owned_rows(jnp.dot(context, proj_full, preferred_element_type=f32))
    expert_normed, expert_standardized, expert_inverse_deviation = normalize_rows(
        residual_middle, expert_gain, expert_shift
    )
    tokens_m = group_rows(expert_normed)
    logits = jnp.dot(tokens_m, router_full, preferred_element_type=f32)
    raised = jnp.exp(logits)
    probs = raised / jnp.sum(raised, axis=-1, keepdims=True)
    picked, slot, token_of_slot, filled = slot_table(routes, experts, CAP)
    gates = jnp.sum(picked.astype(f32) * probs[:, None, :], axis=-1)
    slotted = jnp.where(filled[:, None] > 0, tokens_m[token_of_slot], jnp.zeros((), bf16)).reshape(
        experts, CAP, width
    )
    holders = lax.axis_size("fb")
    units_half = expert_in.shape[2]
    own_both = expert_weights(jnp.concatenate([expert_in, expert_out], axis=2), holders)
    own_in = own_both[:, :units_half]
    own_out = own_both[:, units_half:]
    owner_x = to_owners(slotted)
    owner_pre = jnp.dot(owner_x, own_in, preferred_element_type=f32)
    owner_hidden = gelu_exact(owner_pre).astype(bf16)
    owner_res = jnp.einsum("cf,df->cd", owner_hidden, own_out, preferred_element_type=f32)
    expert_res = to_groups(owner_res, experts, CAP)
    routed = expert_res.reshape(experts * CAP, width)[slot].reshape(group, 2, width)
    outputs = residual_middle + owned_rows(jnp.sum(gates[:, :, None] * routed, axis=1))
    qkv_back, proj_back, router_back = qkv_full, proj_full, router_full
    attention_gain_gradient, expert_gain_gradient = attention_gain, expert_gain
    dout = group_rows(cotangent.astype(bf16))
    dout_f = dout.astype(f32)
    gate_of_slot = jnp.zeros((experts * CAP,), f32).at[slot].set(gates.reshape(-1))
    slot_grad = (
        jnp.where(filled[:, None] > 0, gate_of_slot[:, None] * dout_f[token_of_slot], 0.0)
        .astype(bf16)
        .reshape(experts, CAP, width)
    )
    gate_grad = jnp.sum(dout_f[:, None, :] * routed, axis=-1)
    owner_g = to_owners(slot_grad)
    owner_hgrad = jnp.dot(owner_g, own_out, preferred_element_type=f32)
    owner_pgrad = jax.vjp(gelu_exact, owner_pre)[1](owner_hgrad)[0].astype(bf16)
    owner_back = jnp.einsum("cf,df->cd", owner_pgrad, own_in, preferred_element_type=f32)
    slot_in_grad = to_groups(owner_back, experts, CAP)
    in_local = jnp.einsum("cd,cf->df", owner_x, owner_pgrad, preferred_element_type=f32)
    out_local = jnp.einsum("cd,cf->df", owner_g, owner_hidden, preferred_element_type=f32)
    both_grad = weight_home(jnp.concatenate([in_local, out_local], axis=1), experts, holders)
    in_grad = both_grad[:, :, :units_half]
    out_grad = both_grad[:, :, units_half:]
    choice_grad = jnp.sum(picked.astype(f32) * gate_grad[:, :, None], axis=1)
    logit_grad = probs * (choice_grad - jnp.sum(probs * choice_grad, axis=-1, keepdims=True))
    router_part = jnp.einsum("td,te->de", tokens_m.astype(f32), logit_grad, precision=TOP)
    routed_in = slot_in_grad.reshape(experts * CAP, width)[slot].reshape(group, 2, width)
    token_gradient = jnp.sum(routed_in, axis=1) + jnp.einsum(
        "te,de->td", logit_grad, router_back.astype(f32), precision=TOP
    )
    expert_norm_backward, expert_gain_partial, expert_shift_partial = norm_backward(
        owned_rows(token_gradient),
        expert_standardized,
        expert_inverse_deviation,
        expert_gain_gradient,
    )
    middle_grad = cotangent + expert_norm_backward
    mid_rows = group_rows(middle_grad.astype(bf16))
    proj_part = jnp.einsum("th,td->hd", context, mid_rows, preferred_element_type=f32)
    context_grad = jnp.einsum("td,hd->th", mid_rows, proj_back, preferred_element_type=f32).astype(
        bf16
    )
    query_grad, key_grad, value_grad = attend_back(
        proj[0], proj[1], proj[2], lse, context_grad, images
    )
    stacked = jnp.stack([query_grad, key_grad, value_grad])
    qkv_part = jnp.einsum("td,ith->idh", tokens_a, stacked, preferred_element_type=f32)
    attention_input_gradient = owned_rows(
        jnp.einsum("ith,idh->td", stacked, qkv_back, preferred_element_type=f32)
    )
    attention_norm_backward, attention_gain_partial, attention_shift_partial = norm_backward(
        attention_input_gradient,
        attention_standardized,
        attention_inverse_deviation,
        attention_gain_gradient,
    )
    input_grad = middle_grad + attention_norm_backward
    qkv_grad, proj_grad, router_grad, norm_grads = reduce_dense(
        qkv_part,
        proj_part,
        router_part,
        [attention_gain_partial, attention_shift_partial, expert_gain_partial, expert_shift_partial],
    )
    return (
        outputs,
        input_grad,
        norm_grads[0],
        norm_grads[1],
        qkv_grad,
        proj_grad,
        norm_grads[2],
        norm_grads[3],
        router_grad,
        in_grad,
        out_grad,
    )


def solution(mesh):
    fsdp = mesh.shape["fsdp"]
    sub = Mesh(
        mesh.devices.reshape(EXPERTS, fsdp // EXPERTS, mesh.shape["tp"]), ("fa", "fb", "tp")
    )
    return jax.shard_map(
        per_device,
        mesh=sub,
        in_specs=(
            P(("fa", "fb", "tp"), None),
            P(("fa", "fb"), None),
            P(("fa", "fb")),
            P(("fa", "fb")),
            P(None, ("fa", "fb"), "tp"),
            P("tp", ("fa", "fb")),
            P(("fa", "fb")),
            P(("fa", "fb")),
            P(("fa", "fb"), None),
            P(("fa", "fb"), None, "tp"),
            P(("fa", "fb"), None, "tp"),
            P(("fa", "fb", "tp"), None),
        ),
        out_specs=(
            P(("fa", "fb", "tp"), None),
            P(("fa", "fb", "tp"), None),
            P(("fa", "fb")),
            P(("fa", "fb")),
            P(None, ("fa", "fb"), "tp"),
            P("tp", ("fa", "fb")),
            P(("fa", "fb")),
            P(("fa", "fb")),
            P(("fa", "fb"), None),
            P(("fa", "fb"), None, "tp"),
            P(("fa", "fb"), None, "tp"),
        ),
        check_vma=False,
    )
```

```python
import jax
import jax.numpy as jnp
from jax import lax
from jax.sharding import Mesh, PartitionSpec as P

HEAD_DIM = 64
SEQ = 200
REAL_TOK = 197
CAP = 63
EXPERTS = 16
FSDP = ("fa", "fb")


EPS = 1e-06
TOP = lax.Precision.HIGHEST


def fsdp_size():
    return lax.axis_size("fa") * lax.axis_size("fb")


def gelu_exact(value):
    return jax.nn.gelu(value, approximate=False)


def normalize_rows(value, norm_gain, norm_shift):
    row_mean = jnp.mean(value, axis=-1, keepdims=True)
    centered_rows = value - row_mean
    inverse_deviation = lax.rsqrt(
        jnp.mean(centered_rows * centered_rows, axis=-1, keepdims=True) + EPS
    )
    standardized_rows = centered_rows * inverse_deviation
    normed_rows = (
        standardized_rows * norm_gain.astype(jnp.float32) + norm_shift.astype(jnp.float32)
    ).astype(jnp.bfloat16)
    return (normed_rows, standardized_rows, inverse_deviation)


def norm_backward(incoming_gradient, standardized_rows, inverse_deviation, norm_gain):
    scaled_gradient = incoming_gradient * norm_gain.astype(jnp.float32)
    inner_product = (
        scaled_gradient
        - jnp.mean(scaled_gradient, axis=-1, keepdims=True)
        - standardized_rows * jnp.mean(scaled_gradient * standardized_rows, axis=-1, keepdims=True)
    )
    return (
        inverse_deviation * inner_product,
        jnp.sum(incoming_gradient * standardized_rows, axis=0),
        jnp.sum(incoming_gradient, axis=0),
    )


def slot_table(routes, experts, capacity):
    picked = (routes[:, :, None] == jnp.arange(experts, dtype=jnp.int32)[None, None, :]).astype(
        jnp.int32
    )
    flat = picked.reshape(-1, experts)
    before = jnp.cumsum(flat, axis=0) - flat
    number = jnp.sum(before * flat, axis=-1)
    slot = routes.reshape(-1) * capacity + number
    owner = jnp.arange(flat.shape[0], dtype=jnp.int32) // 2
    token_of_slot = jnp.zeros((experts * capacity,), jnp.int32).at[slot].set(owner)
    filled = jnp.zeros((experts * capacity,), jnp.int32).at[slot].set(1)
    return (picked, slot, token_of_slot, filled)


def split_heads(value, images):
    input_rows, width = value.shape
    return value.reshape(images, input_rows // images, width // HEAD_DIM, HEAD_DIM)


def live_keys(length):
    return (jnp.arange(length) < REAL_TOK)[None, None, None, :]


def attend(query, key, value, images):
    query_h = split_heads(query, images)
    key_h = split_heads(key, images)
    value_h = split_heads(value, images)
    scores = jnp.einsum(
        "ishd,ithd->ihst", query_h, key_h, preferred_element_type=jnp.float32
    ) * HEAD_DIM ** (-0.5)
    live = live_keys(scores.shape[-1])
    lse = jnp.log(jnp.sum(jnp.where(live, jnp.exp(scores), 0.0), axis=-1, keepdims=True))
    probs = jnp.where(live, jnp.exp(scores - lse), 0.0).astype(jnp.bfloat16)
    context = jnp.einsum(
        "ihst,ithd->ishd", probs, value_h, preferred_element_type=jnp.float32
    ).astype(jnp.bfloat16)
    return (context.reshape(query.shape), lse)


def attend_back(query, key, value, lse, context_grad, images):
    query_h = split_heads(query, images)
    key_h = split_heads(key, images)
    value_h = split_heads(value, images)
    grad_h = split_heads(context_grad, images)
    scores = jnp.einsum(
        "ishd,ithd->ihst", query_h, key_h, preferred_element_type=jnp.float32
    ) * HEAD_DIM ** (-0.5)
    live = live_keys(scores.shape[-1])
    probs = jnp.where(live, jnp.exp(scores - lse), 0.0)
    value_grad = jnp.einsum(
        "ihst,ishd->ithd", probs.astype(jnp.bfloat16), grad_h, preferred_element_type=jnp.float32
    ).astype(jnp.bfloat16)
    inner_product = jnp.einsum(
        "ishd,ithd->ihst", grad_h, value_h, preferred_element_type=jnp.float32
    )
    score_grad = (
        probs
        * (inner_product - jnp.sum(probs * inner_product, axis=-1, keepdims=True))
        * HEAD_DIM ** (-0.5)
    ).astype(jnp.bfloat16)
    query_grad = jnp.einsum(
        "ihst,ithd->ishd", score_grad, key_h, preferred_element_type=jnp.float32
    ).astype(jnp.bfloat16)
    key_grad = jnp.einsum(
        "ihst,ishd->ithd", score_grad, query_h, preferred_element_type=jnp.float32
    ).astype(jnp.bfloat16)
    shape = query.shape
    return (query_grad.reshape(shape), key_grad.reshape(shape), value_grad.reshape(shape))


def gather_dense(
    qkv_weight,
    proj_weight,
    router_weight,
    attention_norm_gain,
    attention_norm_shift,
    expert_norm_gain,
    expert_norm_shift,
):
    rows = qkv_weight.shape[1]
    heads_width = qkv_weight.shape[2]
    experts = router_weight.shape[1]
    packed = jnp.concatenate(
        [
            jnp.transpose(qkv_weight, (1, 0, 2)).reshape(rows, -1),
            proj_weight.T,
            router_weight,
            jnp.stack(
                [attention_norm_gain, attention_norm_shift, expert_norm_gain, expert_norm_shift],
                axis=1,
            ),
        ],
        axis=1,
    )
    holders = fsdp_size()
    spread = jnp.broadcast_to(packed[None], (holders,) + packed.shape)
    full = lax.all_to_all(spread, FSDP, split_axis=0, concat_axis=0, tiled=True)
    full = full.reshape(holders * rows, packed.shape[1])
    width = full.shape[0]
    at = 3 * heads_width
    qkv_full = jnp.transpose(full[:, :at].reshape(width, 3, heads_width), (1, 0, 2))
    proj_full = full[:, at : at + heads_width].T
    at += heads_width
    router_full = full[:, at : at + experts]
    at += experts
    norms = full[:, at : at + 4]
    return (qkv_full, proj_full, router_full, norms[:, 0], norms[:, 1], norms[:, 2], norms[:, 3])


def reduce_pack(big, small):
    width = big.shape[0]
    holders = fsdp_size()
    rows = width // holders
    high = lax.reduce_precision(small, exponent_bits=8, mantissa_bits=7)
    wire = jnp.concatenate(
        [big.astype(jnp.bfloat16), high.astype(jnp.bfloat16), (small - high).astype(jnp.bfloat16)],
        axis=1,
    )
    moved = lax.all_to_all(
        wire.reshape(holders, rows, wire.shape[1]), FSDP, split_axis=0, concat_axis=0, tiled=True
    ).astype(jnp.float32)
    at = big.shape[1]
    count = small.shape[1]
    big_sum = jnp.sum(moved[..., :at], axis=0)
    small_sum = jnp.sum(moved[..., at : at + count] + moved[..., at + count :], axis=0)
    return big_sum, small_sum


def group_rows(value):
    halves = lax.axis_size("tp")
    spread = jnp.broadcast_to(value[None], (halves,) + value.shape)
    moved = lax.all_to_all(spread, "tp", split_axis=0, concat_axis=0, tiled=True)
    return moved.reshape(-1, value.shape[1])


def owned_rows(value):
    halves = lax.axis_size("tp")
    moved = lax.all_to_all(
        value.reshape(halves, -1, value.shape[1]), "tp", split_axis=0, concat_axis=0, tiled=True
    )
    return jnp.sum(moved, axis=0)


def to_owners(slots):
    moved = lax.all_to_all(slots, "fa", split_axis=0, concat_axis=0, tiled=True)
    return moved.reshape(-1, slots.shape[2])


def to_groups(result, experts, capacity):
    width = result.shape[1]
    pieces = result.astype(jnp.bfloat16).reshape(experts, capacity, width)
    moved = lax.all_to_all(pieces, "fa", split_axis=0, concat_axis=0, tiled=True)
    return moved.astype(jnp.float32)


def expert_weights(weight, holders):
    rows, experts, units = weight.shape
    spread = jnp.broadcast_to(weight[:, :, None, :], (rows, experts, holders, units))
    moved = lax.all_to_all(
        spread.reshape(rows, experts * holders, units), FSDP, split_axis=1, concat_axis=0, tiled=True
    )
    return moved.reshape(-1, units)


def weight_home(partial, experts, holders):
    width, units = partial.shape
    devices = experts * holders
    rows = width // devices
    moved = lax.all_to_all(
        partial.astype(jnp.bfloat16).reshape(devices, rows, units), FSDP, split_axis=0, concat_axis=0, tiled=True
    )
    summed = jnp.sum(moved.reshape(experts, holders, rows, units).astype(jnp.float32), axis=1)
    return jnp.transpose(summed, (1, 0, 2))


def per_device(
    inputs,
    routes,
    attention_norm_gain,
    attention_norm_shift,
    qkv_weight,
    proj_weight,
    expert_norm_gain,
    expert_norm_shift,
    router_weight,
    expert_in,
    expert_out,
    cotangent,
):
    f32 = jnp.float32
    bf16 = jnp.bfloat16
    dense = gather_dense(
        qkv_weight,
        proj_weight,
        router_weight,
        attention_norm_gain,
        attention_norm_shift,
        expert_norm_gain,
        expert_norm_shift,
    )
    qkv_full, proj_full, router_full, attention_gain, attention_shift, expert_gain, expert_shift = (
        dense
    )
    group = routes.shape[0]
    images = group // SEQ
    experts = router_full.shape[1]
    width = qkv_full.shape[1]
    units = expert_in.shape[2]
    local_rows = expert_in.shape[0]
    holders = fsdp_size() // experts
    block_units = units // holders
    attention_normed, attention_standardized, attention_inverse_deviation = normalize_rows(
        inputs, attention_gain, attention_shift
    )
    tokens_a = group_rows(attention_normed)
    proj = jnp.einsum("td,idh->ith", tokens_a, qkv_full, preferred_element_type=f32).astype(bf16)
    context, lse = attend(proj[0], proj[1], proj[2], images)
    residual_middle = inputs + owned_rows(jnp.dot(context, proj_full, preferred_element_type=f32))
    expert_normed, expert_standardized, expert_inverse_deviation = normalize_rows(
        residual_middle, expert_gain, expert_shift
    )
    tokens_m = group_rows(expert_normed)
    logits = jnp.dot(tokens_m, router_full, preferred_element_type=f32)
    raised = jnp.exp(logits)
    probs = raised / jnp.sum(raised, axis=-1, keepdims=True)
    picked, slot, token_of_slot, filled = slot_table(routes, experts, CAP)
    gates = jnp.sum(picked.astype(f32) * probs[:, None, :], axis=-1)
    slotted = jnp.where(filled[:, None] > 0, tokens_m[token_of_slot], jnp.zeros((), bf16)).reshape(
        experts, CAP, width
    )
    holders = lax.axis_size("fb")
    own_in = expert_weights(expert_in, holders)
    own_out = expert_weights(expert_out, holders)
    owner_x = to_owners(slotted)
    owner_pre = jnp.dot(owner_x, own_in, preferred_element_type=f32)
    owner_hidden = gelu_exact(owner_pre).astype(bf16)
    owner_res = jnp.einsum("cf,df->cd", owner_hidden, own_out, preferred_element_type=f32)
    expert_res = to_groups(owner_res, experts, CAP)
    routed = expert_res.reshape(experts * CAP, width)[slot].reshape(group, 2, width)
    outputs = residual_middle + owned_rows(jnp.sum(gates[:, :, None] * routed, axis=1))
    qkv_back, proj_back, router_back = qkv_full, proj_full, router_full
    attention_gain_gradient, expert_gain_gradient = attention_gain, expert_gain
    dout = group_rows(cotangent.astype(bf16))
    dout_f = dout.astype(f32)
    gate_of_slot = jnp.zeros((experts * CAP,), f32).at[slot].set(gates.reshape(-1))
    slot_grad = (
        jnp.where(filled[:, None] > 0, gate_of_slot[:, None] * dout_f[token_of_slot], 0.0)
        .astype(bf16)
        .reshape(experts, CAP, width)
    )
    gate_grad = jnp.sum(dout_f[:, None, :] * routed, axis=-1)
    owner_g = to_owners(slot_grad)
    owner_hgrad = jnp.dot(owner_g, own_out, preferred_element_type=f32)
    owner_pgrad = jax.vjp(gelu_exact, owner_pre)[1](owner_hgrad)[0].astype(bf16)
    owner_back = jnp.einsum("cf,df->cd", owner_pgrad, own_in, preferred_element_type=f32)
    slot_in_grad = to_groups(owner_back, experts, CAP)
    in_local = jnp.einsum("cd,cf->df", owner_x, owner_pgrad, preferred_element_type=f32)
    out_local = jnp.einsum("cd,cf->df", owner_g, owner_hidden, preferred_element_type=f32)
    in_grad = weight_home(in_local, experts, holders)
    out_grad = weight_home(out_local, experts, holders)
    choice_grad = jnp.sum(picked.astype(f32) * gate_grad[:, :, None], axis=1)
    logit_grad = probs * (choice_grad - jnp.sum(probs * choice_grad, axis=-1, keepdims=True))
    router_part = jnp.einsum("td,te->de", tokens_m.astype(f32), logit_grad, precision=TOP)
    routed_in = slot_in_grad.reshape(experts * CAP, width)[slot].reshape(group, 2, width)
    token_gradient = jnp.sum(routed_in, axis=1) + jnp.einsum(
        "te,de->td", logit_grad, router_back.astype(f32), precision=TOP
    )
    expert_norm_backward, expert_gain_partial, expert_shift_partial = norm_backward(
        owned_rows(token_gradient),
        expert_standardized,
        expert_inverse_deviation,
        expert_gain_gradient,
    )
    middle_grad = cotangent + expert_norm_backward
    mid_rows = group_rows(middle_grad.astype(bf16))
    proj_part = jnp.einsum("th,td->hd", context, mid_rows, preferred_element_type=f32)
    early = reduce_pack(
        proj_part.T,
        jnp.concatenate(
            [router_part, jnp.stack([expert_gain_partial, expert_shift_partial], axis=1)], axis=1
        ),
    )
    context_grad = jnp.einsum("td,hd->th", mid_rows, proj_back, preferred_element_type=f32).astype(
        bf16
    )
    query_grad, key_grad, value_grad = attend_back(
        proj[0], proj[1], proj[2], lse, context_grad, images
    )
    stacked = jnp.stack([query_grad, key_grad, value_grad])
    qkv_part = jnp.einsum("td,ith->idh", tokens_a, stacked, preferred_element_type=f32)
    attention_input_gradient = owned_rows(
        jnp.einsum("ith,idh->td", stacked, qkv_back, preferred_element_type=f32)
    )
    attention_norm_backward, attention_gain_partial, attention_shift_partial = norm_backward(
        attention_input_gradient,
        attention_standardized,
        attention_inverse_deviation,
        attention_gain_gradient,
    )
    input_grad = middle_grad + attention_norm_backward
    late = reduce_pack(
        jnp.transpose(qkv_part, (1, 0, 2)).reshape(qkv_part.shape[1], -1),
        jnp.stack([attention_gain_partial, attention_shift_partial], axis=1),
    )
    rows = late[0].shape[0]
    heads_w = qkv_part.shape[2]
    experts_w = router_part.shape[1]
    qkv_grad = jnp.transpose(late[0].reshape(rows, 3, heads_w), (1, 0, 2))
    proj_grad = early[0].T
    shared = lax.psum(jnp.concatenate([early[1], late[1]], axis=1), "tp")
    return (
        outputs,
        input_grad,
        shared[:, experts_w + 2],
        shared[:, experts_w + 3],
        qkv_grad,
        proj_grad,
        shared[:, experts_w],
        shared[:, experts_w + 1],
        shared[:, :experts_w],
        in_grad,
        out_grad,
    )


def solution(mesh):
    fsdp = mesh.shape["fsdp"]
    sub = Mesh(
        mesh.devices.reshape(EXPERTS, fsdp // EXPERTS, mesh.shape["tp"]), ("fa", "fb", "tp")
    )
    return jax.shard_map(
        per_device,
        mesh=sub,
        in_specs=(
            P(("fa", "fb", "tp"), None),
            P(("fa", "fb"), None),
            P(("fa", "fb")),
            P(("fa", "fb")),
            P(None, ("fa", "fb"), "tp"),
            P("tp", ("fa", "fb")),
            P(("fa", "fb")),
            P(("fa", "fb")),
            P(("fa", "fb"), None),
            P(("fa", "fb"), None, "tp"),
            P(("fa", "fb"), None, "tp"),
            P(("fa", "fb", "tp"), None),
        ),
        out_specs=(
            P(("fa", "fb", "tp"), None),
            P(("fa", "fb", "tp"), None),
            P(("fa", "fb")),
            P(("fa", "fb")),
            P(None, ("fa", "fb"), "tp"),
            P("tp", ("fa", "fb")),
            P(("fa", "fb")),
            P(("fa", "fb")),
            P(("fa", "fb"), None),
            P(("fa", "fb"), None, "tp"),
            P(("fa", "fb"), None, "tp"),
        ),
        check_vma=False,
    )
```

```python
import jax
import jax.numpy as jnp
from jax import lax
from jax.sharding import Mesh, PartitionSpec as P

HEAD_DIM = 64
SEQ = 200
REAL_TOK = 197
CAP = 63
EXPERTS = 16
FSDP = ("fa", "fb")


EPS = 1e-06
TOP = lax.Precision.HIGHEST


def fsdp_size():
    return lax.axis_size("fa") * lax.axis_size("fb")


def gelu_exact(value):
    return jax.nn.gelu(value, approximate=False)


def normalize_rows(value, norm_gain, norm_shift):
    row_mean = jnp.mean(value, axis=-1, keepdims=True)
    centered_rows = value - row_mean
    inverse_deviation = lax.rsqrt(
        jnp.mean(centered_rows * centered_rows, axis=-1, keepdims=True) + EPS
    )
    standardized_rows = centered_rows * inverse_deviation
    normed_rows = (
        standardized_rows * norm_gain.astype(jnp.float32) + norm_shift.astype(jnp.float32)
    ).astype(jnp.bfloat16)
    return (normed_rows, standardized_rows, inverse_deviation)


def norm_backward(incoming_gradient, standardized_rows, inverse_deviation, norm_gain):
    scaled_gradient = incoming_gradient * norm_gain.astype(jnp.float32)
    inner_product = (
        scaled_gradient
        - jnp.mean(scaled_gradient, axis=-1, keepdims=True)
        - standardized_rows * jnp.mean(scaled_gradient * standardized_rows, axis=-1, keepdims=True)
    )
    return (
        inverse_deviation * inner_product,
        jnp.sum(incoming_gradient * standardized_rows, axis=0),
        jnp.sum(incoming_gradient, axis=0),
    )


def slot_table(routes, experts, capacity):
    picked = (routes[:, :, None] == jnp.arange(experts, dtype=jnp.int32)[None, None, :]).astype(
        jnp.int32
    )
    flat = picked.reshape(-1, experts)
    before = jnp.cumsum(flat, axis=0) - flat
    number = jnp.sum(before * flat, axis=-1)
    slot = routes.reshape(-1) * capacity + number
    owner = jnp.arange(flat.shape[0], dtype=jnp.int32) // 2
    token_of_slot = jnp.zeros((experts * capacity,), jnp.int32).at[slot].set(owner)
    filled = jnp.zeros((experts * capacity,), jnp.int32).at[slot].set(1)
    return (picked, slot, token_of_slot, filled)


def split_heads(value, images):
    input_rows, width = value.shape
    return value.reshape(images, input_rows // images, width // HEAD_DIM, HEAD_DIM)


def live_keys(length):
    return (jnp.arange(length) < REAL_TOK)[None, None, None, :]


def attend(query, key, value, images):
    query_h = split_heads(query, images)
    key_h = split_heads(key, images)
    value_h = split_heads(value, images)
    scores = jnp.einsum(
        "ishd,ithd->ihst", query_h, key_h, preferred_element_type=jnp.float32
    ) * HEAD_DIM ** (-0.5)
    live = live_keys(scores.shape[-1])
    lse = jnp.log(jnp.sum(jnp.where(live, jnp.exp(scores), 0.0), axis=-1, keepdims=True))
    probs = jnp.where(live, jnp.exp(scores - lse), 0.0).astype(jnp.bfloat16)
    context = jnp.einsum(
        "ihst,ithd->ishd", probs, value_h, preferred_element_type=jnp.float32
    ).astype(jnp.bfloat16)
    return (context.reshape(query.shape), lse)


def attend_back(query, key, value, lse, context_grad, images):
    query_h = split_heads(query, images)
    key_h = split_heads(key, images)
    value_h = split_heads(value, images)
    grad_h = split_heads(context_grad, images)
    scores = jnp.einsum(
        "ishd,ithd->ihst", query_h, key_h, preferred_element_type=jnp.float32
    ) * HEAD_DIM ** (-0.5)
    live = live_keys(scores.shape[-1])
    probs = jnp.where(live, jnp.exp(scores - lse), 0.0)
    value_grad = jnp.einsum(
        "ihst,ishd->ithd", probs.astype(jnp.bfloat16), grad_h, preferred_element_type=jnp.float32
    ).astype(jnp.bfloat16)
    inner_product = jnp.einsum(
        "ishd,ithd->ihst", grad_h, value_h, preferred_element_type=jnp.float32
    )
    score_grad = (
        probs
        * (inner_product - jnp.sum(probs * inner_product, axis=-1, keepdims=True))
        * HEAD_DIM ** (-0.5)
    ).astype(jnp.bfloat16)
    query_grad = jnp.einsum(
        "ihst,ithd->ishd", score_grad, key_h, preferred_element_type=jnp.float32
    ).astype(jnp.bfloat16)
    key_grad = jnp.einsum(
        "ihst,ishd->ithd", score_grad, query_h, preferred_element_type=jnp.float32
    ).astype(jnp.bfloat16)
    shape = query.shape
    return (query_grad.reshape(shape), key_grad.reshape(shape), value_grad.reshape(shape))


def gather_dense(
    qkv_weight,
    proj_weight,
    router_weight,
    attention_norm_gain,
    attention_norm_shift,
    expert_norm_gain,
    expert_norm_shift,
):
    rows = qkv_weight.shape[1]
    heads_width = qkv_weight.shape[2]
    experts = router_weight.shape[1]
    packed = jnp.concatenate(
        [
            jnp.transpose(qkv_weight, (1, 0, 2)).reshape(rows, -1),
            proj_weight.T,
            router_weight,
            jnp.stack(
                [attention_norm_gain, attention_norm_shift, expert_norm_gain, expert_norm_shift],
                axis=1,
            ),
        ],
        axis=1,
    )
    holders = fsdp_size()
    spread = jnp.broadcast_to(packed[None], (holders,) + packed.shape)
    full = lax.all_to_all(spread, FSDP, split_axis=0, concat_axis=0, tiled=True)
    full = full.reshape(holders * rows, packed.shape[1])
    width = full.shape[0]
    at = 3 * heads_width
    qkv_full = jnp.transpose(full[:, :at].reshape(width, 3, heads_width), (1, 0, 2))
    proj_full = full[:, at : at + heads_width].T
    at += heads_width
    router_full = full[:, at : at + experts]
    at += experts
    norms = full[:, at : at + 4]
    return (qkv_full, proj_full, router_full, norms[:, 0], norms[:, 1], norms[:, 2], norms[:, 3])


def reduce_dense(qkv_part, proj_part, router_part, norm_parts):
    width = qkv_part.shape[1]
    heads_width = qkv_part.shape[2]
    experts = router_part.shape[1]
    packed = jnp.concatenate(
        [
            jnp.transpose(qkv_part, (1, 0, 2)).reshape(width, -1),
            proj_part.T,
            router_part,
            jnp.stack(norm_parts, axis=1),
        ],
        axis=1,
    )
    holders = fsdp_size()
    rows = width // holders
    at = 4 * heads_width
    small = packed[:, at:]
    high = lax.reduce_precision(small, exponent_bits=8, mantissa_bits=7)
    wire = jnp.concatenate(
        [
            packed[:, :at].astype(jnp.bfloat16),
            high.astype(jnp.bfloat16),
            (small - high).astype(jnp.bfloat16),
        ],
        axis=1,
    )
    moved = lax.all_to_all(
        wire.reshape(holders, rows, wire.shape[1]), FSDP, split_axis=0, concat_axis=0, tiled=True
    ).astype(jnp.float32)
    count = small.shape[1]
    part = jnp.concatenate(
        [
            jnp.sum(moved[..., :at], axis=0),
            jnp.sum(moved[..., at : at + count] + moved[..., at + count :], axis=0),
        ],
        axis=1,
    )
    at = 3 * heads_width
    qkv_grad = jnp.transpose(part[:, :at].reshape(rows, 3, heads_width), (1, 0, 2))
    proj_grad = part[:, at : at + heads_width].T
    at += heads_width
    shared = lax.psum(part[:, at:], "tp")
    router_grad = shared[:, :experts]
    norm_grads = [shared[:, experts + i] for i in range(len(norm_parts))]
    return qkv_grad, proj_grad, router_grad, norm_grads


def group_rows(value):
    halves = lax.axis_size("tp")
    spread = jnp.broadcast_to(value[None], (halves,) + value.shape)
    moved = lax.all_to_all(spread, "tp", split_axis=0, concat_axis=0, tiled=True)
    return moved.reshape(-1, value.shape[1])


def owned_rows(value):
    halves = lax.axis_size("tp")
    moved = lax.all_to_all(
        value.reshape(halves, -1, value.shape[1]), "tp", split_axis=0, concat_axis=0, tiled=True
    )
    return jnp.sum(moved, axis=0)


def to_owners(slots):
    moved = lax.all_to_all(slots, "fa", split_axis=0, concat_axis=0, tiled=True)
    return moved.reshape(-1, slots.shape[2])


def to_groups(result, experts, capacity):
    width = result.shape[1]
    pieces = result.astype(jnp.bfloat16).reshape(experts, capacity, width)
    moved = lax.all_to_all(pieces, "fa", split_axis=0, concat_axis=0, tiled=True)
    return moved.astype(jnp.float32)


def expert_weights(weight, holders):
    rows, experts, units = weight.shape
    spread = jnp.broadcast_to(weight[:, :, None, :], (rows, experts, holders, units))
    moved = lax.all_to_all(
        spread.reshape(rows, experts * holders, units), FSDP, split_axis=1, concat_axis=0, tiled=True
    )
    return moved.reshape(-1, units)


def weight_home(partial, experts, holders):
    width, units = partial.shape
    devices = experts * holders
    rows = width // devices
    moved = lax.all_to_all(
        partial.astype(jnp.bfloat16).reshape(devices, rows, units), FSDP, split_axis=0, concat_axis=0, tiled=True
    )
    summed = jnp.sum(moved.reshape(experts, holders, rows, units).astype(jnp.float32), axis=1)
    return jnp.transpose(summed, (1, 0, 2))


def per_device(
    inputs,
    routes,
    attention_norm_gain,
    attention_norm_shift,
    qkv_weight,
    proj_weight,
    expert_norm_gain,
    expert_norm_shift,
    router_weight,
    expert_in,
    expert_out,
    cotangent,
):
    f32 = jnp.float32
    bf16 = jnp.bfloat16
    dense = gather_dense(
        qkv_weight,
        proj_weight,
        router_weight,
        attention_norm_gain,
        attention_norm_shift,
        expert_norm_gain,
        expert_norm_shift,
    )
    qkv_full, proj_full, router_full, attention_gain, attention_shift, expert_gain, expert_shift = (
        dense
    )
    group = routes.shape[0]
    images = group // SEQ
    experts = router_full.shape[1]
    width = qkv_full.shape[1]
    units = expert_in.shape[2]
    local_rows = expert_in.shape[0]
    holders = fsdp_size() // experts
    block_units = units // holders
    attention_normed, attention_standardized, attention_inverse_deviation = normalize_rows(
        inputs, attention_gain, attention_shift
    )
    tokens_a = group_rows(attention_normed)
    proj = jnp.einsum("td,idh->ith", tokens_a, qkv_full, preferred_element_type=f32).astype(bf16)
    context, lse = attend(proj[0], proj[1], proj[2], images)
    residual_middle = inputs + owned_rows(jnp.dot(context, proj_full, preferred_element_type=f32))
    expert_normed, expert_standardized, expert_inverse_deviation = normalize_rows(
        residual_middle, expert_gain, expert_shift
    )
    tokens_m = group_rows(expert_normed)
    logits = jnp.dot(tokens_m, router_full, preferred_element_type=f32)
    raised = jnp.exp(logits)
    probs = raised / jnp.sum(raised, axis=-1, keepdims=True)
    picked, slot, token_of_slot, filled = slot_table(routes, experts, CAP)
    gates = jnp.sum(picked.astype(f32) * probs[:, None, :], axis=-1)
    slotted = jnp.where(filled[:, None] > 0, tokens_m[token_of_slot], jnp.zeros((), bf16)).reshape(
        experts, CAP, width
    )
    holders = lax.axis_size("fb")
    units_half = expert_in.shape[2]
    own_both = expert_weights(jnp.concatenate([expert_in, expert_out], axis=2), holders)
    own_in = own_both[:, :units_half]
    own_out = own_both[:, units_half:]
    owner_x = to_owners(slotted)
    owner_pre = jnp.dot(owner_x, own_in, preferred_element_type=f32)
    owner_hidden = gelu_exact(owner_pre).astype(bf16)
    owner_res = jnp.einsum("cf,df->cd", owner_hidden, own_out, preferred_element_type=f32)
    expert_res = to_groups(owner_res, experts, CAP)
    routed = expert_res.reshape(experts * CAP, width)[slot].reshape(group, 2, width)
    outputs = residual_middle + owned_rows(jnp.sum(gates[:, :, None] * routed, axis=1))
    qkv_back, proj_back, router_back = qkv_full, proj_full, router_full
    attention_gain_gradient, expert_gain_gradient = attention_gain, expert_gain
    dout = group_rows(cotangent.astype(bf16))
    dout_f = dout.astype(f32)
    gate_of_slot = jnp.zeros((experts * CAP,), f32).at[slot].set(gates.reshape(-1))
    slot_grad = (
        jnp.where(filled[:, None] > 0, gate_of_slot[:, None] * dout_f[token_of_slot], 0.0)
        .astype(bf16)
        .reshape(experts, CAP, width)
    )
    gate_grad = jnp.sum(dout_f[:, None, :] * routed, axis=-1)
    owner_g = to_owners(slot_grad)
    owner_hgrad = jnp.dot(owner_g, own_out, preferred_element_type=f32)
    owner_pgrad = jax.vjp(gelu_exact, owner_pre)[1](owner_hgrad)[0].astype(bf16)
    owner_back = jnp.einsum("cf,df->cd", owner_pgrad, own_in, preferred_element_type=f32)
    slot_in_grad = to_groups(owner_back, experts, CAP)
    in_local = jnp.einsum("cd,cf->df", owner_x, owner_pgrad, preferred_element_type=f32)
    out_local = jnp.einsum("cd,cf->df", owner_g, owner_hidden, preferred_element_type=f32)
    in_grad = weight_home(in_local, experts, holders)
    out_grad = weight_home(out_local, experts, holders)
    choice_grad = jnp.sum(picked.astype(f32) * gate_grad[:, :, None], axis=1)
    logit_grad = probs * (choice_grad - jnp.sum(probs * choice_grad, axis=-1, keepdims=True))
    router_part = jnp.einsum("td,te->de", tokens_m.astype(f32), logit_grad, precision=TOP)
    routed_in = slot_in_grad.reshape(experts * CAP, width)[slot].reshape(group, 2, width)
    token_gradient = jnp.sum(routed_in, axis=1) + jnp.einsum(
        "te,de->td", logit_grad, router_back.astype(f32), precision=TOP
    )
    expert_norm_backward, expert_gain_partial, expert_shift_partial = norm_backward(
        owned_rows(token_gradient),
        expert_standardized,
        expert_inverse_deviation,
        expert_gain_gradient,
    )
    middle_grad = cotangent + expert_norm_backward
    mid_rows = group_rows(middle_grad.astype(bf16))
    proj_part = jnp.einsum("th,td->hd", context, mid_rows, preferred_element_type=f32)
    context_grad = jnp.einsum("td,hd->th", mid_rows, proj_back, preferred_element_type=f32).astype(
        bf16
    )
    query_grad, key_grad, value_grad = attend_back(
        proj[0], proj[1], proj[2], lse, context_grad, images
    )
    stacked = jnp.stack([query_grad, key_grad, value_grad])
    qkv_part = jnp.einsum("td,ith->idh", tokens_a, stacked, preferred_element_type=f32)
    attention_input_gradient = owned_rows(
        jnp.einsum("ith,idh->td", stacked, qkv_back, preferred_element_type=f32)
    )
    attention_norm_backward, attention_gain_partial, attention_shift_partial = norm_backward(
        attention_input_gradient,
        attention_standardized,
        attention_inverse_deviation,
        attention_gain_gradient,
    )
    input_grad = middle_grad + attention_norm_backward
    qkv_grad, proj_grad, router_grad, norm_grads = reduce_dense(
        qkv_part,
        proj_part,
        router_part,
        [attention_gain_partial, attention_shift_partial, expert_gain_partial, expert_shift_partial],
    )
    return (
        outputs,
        input_grad,
        norm_grads[0],
        norm_grads[1],
        qkv_grad,
        proj_grad,
        norm_grads[2],
        norm_grads[3],
        router_grad,
        in_grad,
        out_grad,
    )


def solution(mesh):
    fsdp = mesh.shape["fsdp"]
    sub = Mesh(
        mesh.devices.reshape(EXPERTS, fsdp // EXPERTS, mesh.shape["tp"]), ("fa", "fb", "tp")
    )
    return jax.shard_map(
        per_device,
        mesh=sub,
        in_specs=(
            P(("fa", "fb", "tp"), None),
            P(("fa", "fb"), None),
            P(("fa", "fb")),
            P(("fa", "fb")),
            P(None, ("fa", "fb"), "tp"),
            P("tp", ("fa", "fb")),
            P(("fa", "fb")),
            P(("fa", "fb")),
            P(("fa", "fb"), None),
            P(("fa", "fb"), None, "tp"),
            P(("fa", "fb"), None, "tp"),
            P(("fa", "fb", "tp"), None),
        ),
        out_specs=(
            P(("fa", "fb", "tp"), None),
            P(("fa", "fb", "tp"), None),
            P(("fa", "fb")),
            P(("fa", "fb")),
            P(None, ("fa", "fb"), "tp"),
            P("tp", ("fa", "fb")),
            P(("fa", "fb")),
            P(("fa", "fb")),
            P(("fa", "fb"), None),
            P(("fa", "fb"), None, "tp"),
            P(("fa", "fb"), None, "tp"),
        ),
        check_vma=False,
    )
```

```python
import jax
import jax.numpy as jnp
from jax import lax
from jax.sharding import Mesh, PartitionSpec as P

HEAD_DIM = 64
SEQ = 200
REAL_TOK = 197
CAP = 63
EXPERTS = 16
FSDP = ("fa", "fb")


EPS = 1e-06
TOP = lax.Precision.HIGHEST


def fsdp_size():
    return lax.axis_size("fa") * lax.axis_size("fb")


def gelu_exact(value):
    return jax.nn.gelu(value, approximate=False)


def normalize_rows(value, norm_gain, norm_shift):
    row_mean = jnp.mean(value, axis=-1, keepdims=True)
    centered_rows = value - row_mean
    inverse_deviation = lax.rsqrt(
        jnp.mean(centered_rows * centered_rows, axis=-1, keepdims=True) + EPS
    )
    standardized_rows = centered_rows * inverse_deviation
    normed_rows = (
        standardized_rows * norm_gain.astype(jnp.float32) + norm_shift.astype(jnp.float32)
    ).astype(jnp.bfloat16)
    return (normed_rows, standardized_rows, inverse_deviation)


def norm_backward(incoming_gradient, standardized_rows, inverse_deviation, norm_gain):
    scaled_gradient = incoming_gradient * norm_gain.astype(jnp.float32)
    inner_product = (
        scaled_gradient
        - jnp.mean(scaled_gradient, axis=-1, keepdims=True)
        - standardized_rows * jnp.mean(scaled_gradient * standardized_rows, axis=-1, keepdims=True)
    )
    return (
        inverse_deviation * inner_product,
        jnp.sum(incoming_gradient * standardized_rows, axis=0),
        jnp.sum(incoming_gradient, axis=0),
    )


def slot_table(routes, experts, capacity):
    picked = (routes[:, :, None] == jnp.arange(experts, dtype=jnp.int32)[None, None, :]).astype(
        jnp.int32
    )
    flat = picked.reshape(-1, experts)
    before = jnp.cumsum(flat, axis=0) - flat
    number = jnp.sum(before * flat, axis=-1)
    slot = routes.reshape(-1) * capacity + number
    owner = jnp.arange(flat.shape[0], dtype=jnp.int32) // 2
    token_of_slot = jnp.zeros((experts * capacity,), jnp.int32).at[slot].set(owner)
    filled = jnp.zeros((experts * capacity,), jnp.int32).at[slot].set(1)
    return (picked, slot, token_of_slot, filled)


def split_heads(value, images):
    input_rows, width = value.shape
    return value.reshape(images, input_rows // images, width // HEAD_DIM, HEAD_DIM)


def live_keys(length):
    return (jnp.arange(length) < REAL_TOK)[None, None, None, :]


def attend(query, key, value, images):
    query_h = split_heads(query, images)
    key_h = split_heads(key, images)
    value_h = split_heads(value, images)
    scores = jnp.einsum(
        "ishd,ithd->ihst", query_h, key_h, preferred_element_type=jnp.float32
    ) * HEAD_DIM ** (-0.5)
    live = live_keys(scores.shape[-1])
    lse = jnp.log(jnp.sum(jnp.where(live, jnp.exp(scores), 0.0), axis=-1, keepdims=True))
    probs = jnp.where(live, jnp.exp(scores - lse), 0.0).astype(jnp.bfloat16)
    context = jnp.einsum(
        "ihst,ithd->ishd", probs, value_h, preferred_element_type=jnp.float32
    ).astype(jnp.bfloat16)
    return (context.reshape(query.shape), lse)


def attend_back(query, key, value, lse, context_grad, images):
    query_h = split_heads(query, images)
    key_h = split_heads(key, images)
    value_h = split_heads(value, images)
    grad_h = split_heads(context_grad, images)
    scores = jnp.einsum(
        "ishd,ithd->ihst", query_h, key_h, preferred_element_type=jnp.float32
    ) * HEAD_DIM ** (-0.5)
    live = live_keys(scores.shape[-1])
    probs = jnp.where(live, jnp.exp(scores - lse), 0.0)
    value_grad = jnp.einsum(
        "ihst,ishd->ithd", probs.astype(jnp.bfloat16), grad_h, preferred_element_type=jnp.float32
    ).astype(jnp.bfloat16)
    inner_product = jnp.einsum(
        "ishd,ithd->ihst", grad_h, value_h, preferred_element_type=jnp.float32
    )
    score_grad = (
        probs
        * (inner_product - jnp.sum(probs * inner_product, axis=-1, keepdims=True))
        * HEAD_DIM ** (-0.5)
    ).astype(jnp.bfloat16)
    query_grad = jnp.einsum(
        "ihst,ithd->ishd", score_grad, key_h, preferred_element_type=jnp.float32
    ).astype(jnp.bfloat16)
    key_grad = jnp.einsum(
        "ihst,ishd->ithd", score_grad, query_h, preferred_element_type=jnp.float32
    ).astype(jnp.bfloat16)
    shape = query.shape
    return (query_grad.reshape(shape), key_grad.reshape(shape), value_grad.reshape(shape))


def gather_dense(
    qkv_weight,
    proj_weight,
    router_weight,
    attention_norm_gain,
    attention_norm_shift,
    expert_norm_gain,
    expert_norm_shift,
):
    rows = qkv_weight.shape[1]
    heads_width = qkv_weight.shape[2]
    experts = router_weight.shape[1]
    packed = jnp.concatenate(
        [
            jnp.transpose(qkv_weight, (1, 0, 2)).reshape(rows, -1),
            proj_weight.T,
            router_weight,
            jnp.stack(
                [attention_norm_gain, attention_norm_shift, expert_norm_gain, expert_norm_shift],
                axis=1,
            ),
        ],
        axis=1,
    )
    holders = fsdp_size()
    spread = jnp.broadcast_to(packed[None], (holders,) + packed.shape)
    full = lax.all_to_all(spread, FSDP, split_axis=0, concat_axis=0, tiled=True)
    full = full.reshape(holders * rows, packed.shape[1])
    width = full.shape[0]
    at = 3 * heads_width
    qkv_full = jnp.transpose(full[:, :at].reshape(width, 3, heads_width), (1, 0, 2))
    proj_full = full[:, at : at + heads_width].T
    at += heads_width
    router_full = full[:, at : at + experts]
    at += experts
    norms = full[:, at : at + 4]
    return (qkv_full, proj_full, router_full, norms[:, 0], norms[:, 1], norms[:, 2], norms[:, 3])


def reduce_dense(qkv_part, proj_part, router_part, norm_parts):
    width = qkv_part.shape[1]
    heads_width = qkv_part.shape[2]
    experts = router_part.shape[1]
    packed = jnp.concatenate(
        [
            jnp.transpose(qkv_part, (1, 0, 2)).reshape(width, -1),
            proj_part.T,
            router_part,
            jnp.stack(norm_parts, axis=1),
        ],
        axis=1,
    )
    holders = fsdp_size()
    rows = width // holders
    at = 4 * heads_width
    small = packed[:, at:]
    high = lax.reduce_precision(small, exponent_bits=8, mantissa_bits=7)
    wire = jnp.concatenate(
        [
            packed[:, :at].astype(jnp.bfloat16),
            high.astype(jnp.bfloat16),
            (small - high).astype(jnp.bfloat16),
        ],
        axis=1,
    )
    moved = lax.all_to_all(
        wire.reshape(holders, rows, wire.shape[1]), FSDP, split_axis=0, concat_axis=0, tiled=True
    ).astype(jnp.float32)
    count = small.shape[1]
    part = jnp.concatenate(
        [
            jnp.sum(moved[..., :at], axis=0),
            jnp.sum(moved[..., at : at + count] + moved[..., at + count :], axis=0),
        ],
        axis=1,
    )
    at = 3 * heads_width
    qkv_grad = jnp.transpose(part[:, :at].reshape(rows, 3, heads_width), (1, 0, 2))
    proj_grad = part[:, at : at + heads_width].T
    at += heads_width
    shared = lax.psum(part[:, at:], "tp")
    router_grad = shared[:, :experts]
    norm_grads = [shared[:, experts + i] for i in range(len(norm_parts))]
    return qkv_grad, proj_grad, router_grad, norm_grads


def group_rows(value):
    halves = lax.axis_size("tp")
    spread = jnp.broadcast_to(value[None], (halves,) + value.shape)
    moved = lax.all_to_all(spread, "tp", split_axis=0, concat_axis=0, tiled=True)
    return moved.reshape(-1, value.shape[1])


def owned_rows(value):
    halves = lax.axis_size("tp")
    moved = lax.all_to_all(
        value.astype(jnp.bfloat16).reshape(halves, -1, value.shape[1]),
        "tp",
        split_axis=0,
        concat_axis=0,
        tiled=True,
    )
    return jnp.sum(moved.astype(jnp.float32), axis=0)


def to_owners(slots):
    moved = lax.all_to_all(slots, "fa", split_axis=0, concat_axis=0, tiled=True)
    return moved.reshape(-1, slots.shape[2])


def to_groups(result, experts, capacity):
    width = result.shape[1]
    pieces = result.astype(jnp.bfloat16).reshape(experts, capacity, width)
    moved = lax.all_to_all(pieces, "fa", split_axis=0, concat_axis=0, tiled=True)
    return moved.astype(jnp.float32)


def expert_weights(weight, holders):
    rows, experts, units = weight.shape
    spread = jnp.broadcast_to(weight[:, :, None, :], (rows, experts, holders, units))
    moved = lax.all_to_all(
        spread.reshape(rows, experts * holders, units), FSDP, split_axis=1, concat_axis=0, tiled=True
    )
    return moved.reshape(-1, units)


def weight_home(partial, experts, holders):
    width, units = partial.shape
    devices = experts * holders
    rows = width // devices
    moved = lax.all_to_all(
        partial.astype(jnp.bfloat16).reshape(devices, rows, units), FSDP, split_axis=0, concat_axis=0, tiled=True
    )
    summed = jnp.sum(moved.reshape(experts, holders, rows, units).astype(jnp.float32), axis=1)
    return jnp.transpose(summed, (1, 0, 2))


def per_device(
    inputs,
    routes,
    attention_norm_gain,
    attention_norm_shift,
    qkv_weight,
    proj_weight,
    expert_norm_gain,
    expert_norm_shift,
    router_weight,
    expert_in,
    expert_out,
    cotangent,
):
    f32 = jnp.float32
    bf16 = jnp.bfloat16
    dense = gather_dense(
        qkv_weight,
        proj_weight,
        router_weight,
        attention_norm_gain,
        attention_norm_shift,
        expert_norm_gain,
        expert_norm_shift,
    )
    qkv_full, proj_full, router_full, attention_gain, attention_shift, expert_gain, expert_shift = (
        dense
    )
    group = routes.shape[0]
    images = group // SEQ
    experts = router_full.shape[1]
    width = qkv_full.shape[1]
    units = expert_in.shape[2]
    local_rows = expert_in.shape[0]
    holders = fsdp_size() // experts
    block_units = units // holders
    attention_normed, attention_standardized, attention_inverse_deviation = normalize_rows(
        inputs, attention_gain, attention_shift
    )
    tokens_a = group_rows(attention_normed)
    proj = jnp.einsum("td,idh->ith", tokens_a, qkv_full, preferred_element_type=f32).astype(bf16)
    context, lse = attend(proj[0], proj[1], proj[2], images)
    residual_middle = inputs + owned_rows(jnp.dot(context, proj_full, preferred_element_type=f32))
    expert_normed, expert_standardized, expert_inverse_deviation = normalize_rows(
        residual_middle, expert_gain, expert_shift
    )
    tokens_m = group_rows(expert_normed)
    logits = jnp.dot(tokens_m, router_full, preferred_element_type=f32)
    raised = jnp.exp(logits)
    probs = raised / jnp.sum(raised, axis=-1, keepdims=True)
    picked, slot, token_of_slot, filled = slot_table(routes, experts, CAP)
    gates = jnp.sum(picked.astype(f32) * probs[:, None, :], axis=-1)
    slotted = jnp.where(filled[:, None] > 0, tokens_m[token_of_slot], jnp.zeros((), bf16)).reshape(
        experts, CAP, width
    )
    holders = lax.axis_size("fb")
    units_half = expert_in.shape[2]
    own_both = expert_weights(jnp.concatenate([expert_in, expert_out], axis=2), holders)
    own_in = own_both[:, :units_half]
    own_out = own_both[:, units_half:]
    owner_x = to_owners(slotted)
    owner_pre = jnp.dot(owner_x, own_in, preferred_element_type=f32)
    owner_hidden = gelu_exact(owner_pre).astype(bf16)
    owner_res = jnp.einsum("cf,df->cd", owner_hidden, own_out, preferred_element_type=f32)
    expert_res = to_groups(owner_res, experts, CAP)
    routed = expert_res.reshape(experts * CAP, width)[slot].reshape(group, 2, width)
    outputs = residual_middle + owned_rows(jnp.sum(gates[:, :, None] * routed, axis=1))
    qkv_back, proj_back, router_back = qkv_full, proj_full, router_full
    attention_gain_gradient, expert_gain_gradient = attention_gain, expert_gain
    dout = group_rows(cotangent.astype(bf16))
    dout_f = dout.astype(f32)
    gate_of_slot = jnp.zeros((experts * CAP,), f32).at[slot].set(gates.reshape(-1))
    slot_grad = (
        jnp.where(filled[:, None] > 0, gate_of_slot[:, None] * dout_f[token_of_slot], 0.0)
        .astype(bf16)
        .reshape(experts, CAP, width)
    )
    gate_grad = jnp.sum(dout_f[:, None, :] * routed, axis=-1)
    owner_g = to_owners(slot_grad)
    owner_hgrad = jnp.dot(owner_g, own_out, preferred_element_type=f32)
    owner_pgrad = jax.vjp(gelu_exact, owner_pre)[1](owner_hgrad)[0].astype(bf16)
    owner_back = jnp.einsum("cf,df->cd", owner_pgrad, own_in, preferred_element_type=f32)
    slot_in_grad = to_groups(owner_back, experts, CAP)
    in_local = jnp.einsum("cd,cf->df", owner_x, owner_pgrad, preferred_element_type=f32)
    out_local = jnp.einsum("cd,cf->df", owner_g, owner_hidden, preferred_element_type=f32)
    in_grad = weight_home(in_local, experts, holders)
    out_grad = weight_home(out_local, experts, holders)
    choice_grad = jnp.sum(picked.astype(f32) * gate_grad[:, :, None], axis=1)
    logit_grad = probs * (choice_grad - jnp.sum(probs * choice_grad, axis=-1, keepdims=True))
    router_part = jnp.einsum("td,te->de", tokens_m.astype(f32), logit_grad, precision=TOP)
    routed_in = slot_in_grad.reshape(experts * CAP, width)[slot].reshape(group, 2, width)
    token_gradient = jnp.sum(routed_in, axis=1) + jnp.einsum(
        "te,de->td", logit_grad, router_back.astype(f32), precision=TOP
    )
    expert_norm_backward, expert_gain_partial, expert_shift_partial = norm_backward(
        owned_rows(token_gradient),
        expert_standardized,
        expert_inverse_deviation,
        expert_gain_gradient,
    )
    middle_grad = cotangent + expert_norm_backward
    mid_rows = group_rows(middle_grad.astype(bf16))
    proj_part = jnp.einsum("th,td->hd", context, mid_rows, preferred_element_type=f32)
    context_grad = jnp.einsum("td,hd->th", mid_rows, proj_back, preferred_element_type=f32).astype(
        bf16
    )
    query_grad, key_grad, value_grad = attend_back(
        proj[0], proj[1], proj[2], lse, context_grad, images
    )
    stacked = jnp.stack([query_grad, key_grad, value_grad])
    qkv_part = jnp.einsum("td,ith->idh", tokens_a, stacked, preferred_element_type=f32)
    attention_input_gradient = owned_rows(
        jnp.einsum("ith,idh->td", stacked, qkv_back, preferred_element_type=f32)
    )
    attention_norm_backward, attention_gain_partial, attention_shift_partial = norm_backward(
        attention_input_gradient,
        attention_standardized,
        attention_inverse_deviation,
        attention_gain_gradient,
    )
    input_grad = middle_grad + attention_norm_backward
    qkv_grad, proj_grad, router_grad, norm_grads = reduce_dense(
        qkv_part,
        proj_part,
        router_part,
        [attention_gain_partial, attention_shift_partial, expert_gain_partial, expert_shift_partial],
    )
    return (
        outputs,
        input_grad,
        norm_grads[0],
        norm_grads[1],
        qkv_grad,
        proj_grad,
        norm_grads[2],
        norm_grads[3],
        router_grad,
        in_grad,
        out_grad,
    )


def solution(mesh):
    fsdp = mesh.shape["fsdp"]
    sub = Mesh(
        mesh.devices.reshape(EXPERTS, fsdp // EXPERTS, mesh.shape["tp"]), ("fa", "fb", "tp")
    )
    return jax.shard_map(
        per_device,
        mesh=sub,
        in_specs=(
            P(("fa", "fb", "tp"), None),
            P(("fa", "fb"), None),
            P(("fa", "fb")),
            P(("fa", "fb")),
            P(None, ("fa", "fb"), "tp"),
            P("tp", ("fa", "fb")),
            P(("fa", "fb")),
            P(("fa", "fb")),
            P(("fa", "fb"), None),
            P(("fa", "fb"), None, "tp"),
            P(("fa", "fb"), None, "tp"),
            P(("fa", "fb", "tp"), None),
        ),
        out_specs=(
            P(("fa", "fb", "tp"), None),
            P(("fa", "fb", "tp"), None),
            P(("fa", "fb")),
            P(("fa", "fb")),
            P(None, ("fa", "fb"), "tp"),
            P("tp", ("fa", "fb")),
            P(("fa", "fb")),
            P(("fa", "fb")),
            P(("fa", "fb"), None),
            P(("fa", "fb"), None, "tp"),
            P(("fa", "fb"), None, "tp"),
        ),
        check_vma=False,
    )
```

```python
import jax
import jax.numpy as jnp
from jax import lax
from jax.sharding import Mesh, PartitionSpec as P

HEAD_DIM = 64
SEQ = 200
REAL_TOK = 197
CAP = 63
EXPERTS = 16
FSDP = ("fa", "fb")


EPS = 1e-06
TOP = lax.Precision.HIGHEST


def fsdp_size():
    return lax.axis_size("fa") * lax.axis_size("fb")


def gelu_exact(value):
    return jax.nn.gelu(value, approximate=False)


def normalize_rows(value, norm_gain, norm_shift):
    row_mean = jnp.mean(value, axis=-1, keepdims=True)
    centered_rows = value - row_mean
    inverse_deviation = lax.rsqrt(
        jnp.mean(centered_rows * centered_rows, axis=-1, keepdims=True) + EPS
    )
    standardized_rows = centered_rows * inverse_deviation
    normed_rows = (
        standardized_rows * norm_gain.astype(jnp.float32) + norm_shift.astype(jnp.float32)
    ).astype(jnp.bfloat16)
    return (normed_rows, standardized_rows, inverse_deviation)


def norm_backward(incoming_gradient, standardized_rows, inverse_deviation, norm_gain):
    scaled_gradient = incoming_gradient * norm_gain.astype(jnp.float32)
    inner_product = (
        scaled_gradient
        - jnp.mean(scaled_gradient, axis=-1, keepdims=True)
        - standardized_rows * jnp.mean(scaled_gradient * standardized_rows, axis=-1, keepdims=True)
    )
    return (
        inverse_deviation * inner_product,
        jnp.sum(incoming_gradient * standardized_rows, axis=0),
        jnp.sum(incoming_gradient, axis=0),
    )


def slot_table(routes, experts, capacity):
    picked = (routes[:, :, None] == jnp.arange(experts, dtype=jnp.int32)[None, None, :]).astype(
        jnp.int32
    )
    flat = picked.reshape(-1, experts)
    before = jnp.cumsum(flat, axis=0) - flat
    number = jnp.sum(before * flat, axis=-1)
    slot = routes.reshape(-1) * capacity + number
    owner = jnp.arange(flat.shape[0], dtype=jnp.int32) // 2
    token_of_slot = jnp.zeros((experts * capacity,), jnp.int32).at[slot].set(owner)
    filled = jnp.zeros((experts * capacity,), jnp.int32).at[slot].set(1)
    return (picked, slot, token_of_slot, filled)


def split_heads(value, images):
    input_rows, width = value.shape
    return value.reshape(images, input_rows // images, width // HEAD_DIM, HEAD_DIM)


def live_keys(length):
    return (jnp.arange(length) < REAL_TOK)[None, None, None, :]


def attend(query, key, value, images):
    query_h = split_heads(query, images)
    key_h = split_heads(key, images)
    value_h = split_heads(value, images)
    scores = jnp.einsum(
        "ishd,ithd->ihst", query_h, key_h, preferred_element_type=jnp.float32
    ) * HEAD_DIM ** (-0.5)
    live = live_keys(scores.shape[-1])
    lse = jnp.log(jnp.sum(jnp.where(live, jnp.exp(scores), 0.0), axis=-1, keepdims=True))
    probs = jnp.where(live, jnp.exp(scores - lse), 0.0).astype(jnp.bfloat16)
    context = jnp.einsum(
        "ihst,ithd->ishd", probs, value_h, preferred_element_type=jnp.float32
    ).astype(jnp.bfloat16)
    return (context.reshape(query.shape), lse)


def attend_back(query, key, value, lse, context_grad, images):
    query_h = split_heads(query, images)
    key_h = split_heads(key, images)
    value_h = split_heads(value, images)
    grad_h = split_heads(context_grad, images)
    scores = jnp.einsum(
        "ishd,ithd->ihst", query_h, key_h, preferred_element_type=jnp.float32
    ) * HEAD_DIM ** (-0.5)
    live = live_keys(scores.shape[-1])
    probs = jnp.where(live, jnp.exp(scores - lse), 0.0)
    value_grad = jnp.einsum(
        "ihst,ishd->ithd", probs.astype(jnp.bfloat16), grad_h, preferred_element_type=jnp.float32
    ).astype(jnp.bfloat16)
    inner_product = jnp.einsum(
        "ishd,ithd->ihst", grad_h, value_h, preferred_element_type=jnp.float32
    )
    score_grad = (
        probs
        * (inner_product - jnp.sum(probs * inner_product, axis=-1, keepdims=True))
        * HEAD_DIM ** (-0.5)
    ).astype(jnp.bfloat16)
    query_grad = jnp.einsum(
        "ihst,ithd->ishd", score_grad, key_h, preferred_element_type=jnp.float32
    ).astype(jnp.bfloat16)
    key_grad = jnp.einsum(
        "ihst,ishd->ithd", score_grad, query_h, preferred_element_type=jnp.float32
    ).astype(jnp.bfloat16)
    shape = query.shape
    return (query_grad.reshape(shape), key_grad.reshape(shape), value_grad.reshape(shape))


def gather_dense(
    qkv_weight,
    proj_weight,
    router_weight,
    attention_norm_gain,
    attention_norm_shift,
    expert_norm_gain,
    expert_norm_shift,
):
    rows = qkv_weight.shape[1]
    heads_width = qkv_weight.shape[2]
    experts = router_weight.shape[1]
    packed = jnp.concatenate(
        [
            jnp.transpose(qkv_weight, (1, 0, 2)).reshape(rows, -1),
            proj_weight.T,
            router_weight,
            jnp.stack(
                [attention_norm_gain, attention_norm_shift, expert_norm_gain, expert_norm_shift],
                axis=1,
            ),
        ],
        axis=1,
    )
    holders = fsdp_size()
    spread = jnp.broadcast_to(packed[None], (holders,) + packed.shape)
    full = lax.all_to_all(spread, FSDP, split_axis=0, concat_axis=0, tiled=True)
    full = full.reshape(holders * rows, packed.shape[1])
    width = full.shape[0]
    at = 3 * heads_width
    qkv_full = jnp.transpose(full[:, :at].reshape(width, 3, heads_width), (1, 0, 2))
    proj_full = full[:, at : at + heads_width].T
    at += heads_width
    router_full = full[:, at : at + experts]
    at += experts
    norms = full[:, at : at + 4]
    return (qkv_full, proj_full, router_full, norms[:, 0], norms[:, 1], norms[:, 2], norms[:, 3])


def reduce_dense(qkv_part, proj_part, router_part, norm_parts):
    width = qkv_part.shape[1]
    heads_width = qkv_part.shape[2]
    experts = router_part.shape[1]
    packed = jnp.concatenate(
        [
            jnp.transpose(qkv_part, (1, 0, 2)).reshape(width, -1),
            proj_part.T,
            router_part,
            jnp.stack(norm_parts, axis=1),
        ],
        axis=1,
    )
    holders = fsdp_size()
    rows = width // holders
    at = 4 * heads_width
    small = packed[:, at:]
    high = lax.reduce_precision(small, exponent_bits=8, mantissa_bits=7)
    wire = jnp.concatenate(
        [
            packed[:, :at].astype(jnp.bfloat16),
            high.astype(jnp.bfloat16),
            (small - high).astype(jnp.bfloat16),
        ],
        axis=1,
    )
    moved = lax.all_to_all(
        wire.reshape(holders, rows, wire.shape[1]), FSDP, split_axis=0, concat_axis=0, tiled=True
    ).astype(jnp.float32)
    count = small.shape[1]
    part = jnp.concatenate(
        [
            jnp.sum(moved[..., :at], axis=0),
            jnp.sum(moved[..., at : at + count] + moved[..., at + count :], axis=0),
        ],
        axis=1,
    )
    at = 3 * heads_width
    qkv_grad = jnp.transpose(part[:, :at].reshape(rows, 3, heads_width), (1, 0, 2))
    proj_grad = part[:, at : at + heads_width].T
    at += heads_width
    small = part[:, at:]
    halves = lax.axis_size("tp")
    shared = jnp.sum(
        lax.all_to_all(
            jnp.broadcast_to(small[None], (halves,) + small.shape), "tp", 0, 0, tiled=True
        ),
        axis=0,
    )
    router_grad = shared[:, :experts]
    norm_grads = [shared[:, experts + i] for i in range(len(norm_parts))]
    return qkv_grad, proj_grad, router_grad, norm_grads


def group_rows(value):
    halves = lax.axis_size("tp")
    spread = jnp.broadcast_to(value[None], (halves,) + value.shape)
    moved = lax.all_to_all(spread, "tp", split_axis=0, concat_axis=0, tiled=True)
    return moved.reshape(-1, value.shape[1])


def owned_rows(value):
    halves = lax.axis_size("tp")
    moved = lax.all_to_all(
        value.astype(jnp.bfloat16).reshape(halves, -1, value.shape[1]),
        "tp",
        split_axis=0,
        concat_axis=0,
        tiled=True,
    )
    return jnp.sum(moved.astype(jnp.float32), axis=0)


def to_owners(slots):
    moved = lax.all_to_all(slots, "fa", split_axis=0, concat_axis=0, tiled=True)
    return moved.reshape(-1, slots.shape[2])


def to_groups(result, experts, capacity):
    width = result.shape[1]
    pieces = result.astype(jnp.bfloat16).reshape(experts, capacity, width)
    moved = lax.all_to_all(pieces, "fa", split_axis=0, concat_axis=0, tiled=True)
    return moved.astype(jnp.float32)


def expert_weights(weight, holders):
    rows, experts, units = weight.shape
    spread = jnp.broadcast_to(weight[:, :, None, :], (rows, experts, holders, units))
    moved = lax.all_to_all(
        spread.reshape(rows, experts * holders, units), FSDP, split_axis=1, concat_axis=0, tiled=True
    )
    return moved.reshape(-1, units)


def weight_home(partial, experts, holders):
    width, units = partial.shape
    devices = experts * holders
    rows = width // devices
    moved = lax.all_to_all(
        partial.astype(jnp.bfloat16).reshape(devices, rows, units), FSDP, split_axis=0, concat_axis=0, tiled=True
    )
    summed = jnp.sum(moved.reshape(experts, holders, rows, units).astype(jnp.float32), axis=1)
    return jnp.transpose(summed, (1, 0, 2))


def per_device(
    inputs,
    routes,
    attention_norm_gain,
    attention_norm_shift,
    qkv_weight,
    proj_weight,
    expert_norm_gain,
    expert_norm_shift,
    router_weight,
    expert_in,
    expert_out,
    cotangent,
):
    f32 = jnp.float32
    bf16 = jnp.bfloat16
    dense = gather_dense(
        qkv_weight,
        proj_weight,
        router_weight,
        attention_norm_gain,
        attention_norm_shift,
        expert_norm_gain,
        expert_norm_shift,
    )
    qkv_full, proj_full, router_full, attention_gain, attention_shift, expert_gain, expert_shift = (
        dense
    )
    group = routes.shape[0]
    images = group // SEQ
    experts = router_full.shape[1]
    width = qkv_full.shape[1]
    units = expert_in.shape[2]
    local_rows = expert_in.shape[0]
    holders = fsdp_size() // experts
    block_units = units // holders
    attention_normed, attention_standardized, attention_inverse_deviation = normalize_rows(
        inputs, attention_gain, attention_shift
    )
    tokens_a = group_rows(attention_normed)
    proj = jnp.einsum("td,idh->ith", tokens_a, qkv_full, preferred_element_type=f32).astype(bf16)
    context, lse = attend(proj[0], proj[1], proj[2], images)
    residual_middle = inputs + owned_rows(jnp.dot(context, proj_full, preferred_element_type=f32))
    expert_normed, expert_standardized, expert_inverse_deviation = normalize_rows(
        residual_middle, expert_gain, expert_shift
    )
    tokens_m = group_rows(expert_normed)
    logits = jnp.dot(tokens_m, router_full, preferred_element_type=f32)
    raised = jnp.exp(logits)
    probs = raised / jnp.sum(raised, axis=-1, keepdims=True)
    picked, slot, token_of_slot, filled = slot_table(routes, experts, CAP)
    gates = jnp.sum(picked.astype(f32) * probs[:, None, :], axis=-1)
    slotted = jnp.where(filled[:, None] > 0, tokens_m[token_of_slot], jnp.zeros((), bf16)).reshape(
        experts, CAP, width
    )
    holders = lax.axis_size("fb")
    units_half = expert_in.shape[2]
    own_both = expert_weights(jnp.concatenate([expert_in, expert_out], axis=2), holders)
    own_in = own_both[:, :units_half]
    own_out = own_both[:, units_half:]
    owner_x = to_owners(slotted)
    owner_pre = jnp.dot(owner_x, own_in, preferred_element_type=f32)
    owner_hidden = gelu_exact(owner_pre).astype(bf16)
    owner_res = jnp.einsum("cf,df->cd", owner_hidden, own_out, preferred_element_type=f32)
    expert_res = to_groups(owner_res, experts, CAP)
    routed = expert_res.reshape(experts * CAP, width)[slot].reshape(group, 2, width)
    outputs = residual_middle + owned_rows(jnp.sum(gates[:, :, None] * routed, axis=1))
    qkv_back, proj_back, router_back = qkv_full, proj_full, router_full
    attention_gain_gradient, expert_gain_gradient = attention_gain, expert_gain
    dout = group_rows(cotangent.astype(bf16))
    dout_f = dout.astype(f32)
    gate_of_slot = jnp.zeros((experts * CAP,), f32).at[slot].set(gates.reshape(-1))
    slot_grad = (
        jnp.where(filled[:, None] > 0, gate_of_slot[:, None] * dout_f[token_of_slot], 0.0)
        .astype(bf16)
        .reshape(experts, CAP, width)
    )
    gate_grad = jnp.sum(dout_f[:, None, :] * routed, axis=-1)
    owner_g = to_owners(slot_grad)
    owner_hgrad = jnp.dot(owner_g, own_out, preferred_element_type=f32)
    owner_pgrad = jax.vjp(gelu_exact, owner_pre)[1](owner_hgrad)[0].astype(bf16)
    owner_back = jnp.einsum("cf,df->cd", owner_pgrad, own_in, preferred_element_type=f32)
    slot_in_grad = to_groups(owner_back, experts, CAP)
    in_local = jnp.einsum("cd,cf->df", owner_x, owner_pgrad, preferred_element_type=f32)
    out_local = jnp.einsum("cd,cf->df", owner_g, owner_hidden, preferred_element_type=f32)
    in_grad = weight_home(in_local, experts, holders)
    out_grad = weight_home(out_local, experts, holders)
    choice_grad = jnp.sum(picked.astype(f32) * gate_grad[:, :, None], axis=1)
    logit_grad = probs * (choice_grad - jnp.sum(probs * choice_grad, axis=-1, keepdims=True))
    router_part = jnp.einsum("td,te->de", tokens_m.astype(f32), logit_grad, precision=TOP)
    routed_in = slot_in_grad.reshape(experts * CAP, width)[slot].reshape(group, 2, width)
    token_gradient = jnp.sum(routed_in, axis=1) + jnp.einsum(
        "te,de->td", logit_grad, router_back.astype(f32), precision=TOP
    )
    expert_norm_backward, expert_gain_partial, expert_shift_partial = norm_backward(
        owned_rows(token_gradient),
        expert_standardized,
        expert_inverse_deviation,
        expert_gain_gradient,
    )
    middle_grad = cotangent + expert_norm_backward
    mid_rows = group_rows(middle_grad.astype(bf16))
    proj_part = jnp.einsum("th,td->hd", context, mid_rows, preferred_element_type=f32)
    context_grad = jnp.einsum("td,hd->th", mid_rows, proj_back, preferred_element_type=f32).astype(
        bf16
    )
    query_grad, key_grad, value_grad = attend_back(
        proj[0], proj[1], proj[2], lse, context_grad, images
    )
    stacked = jnp.stack([query_grad, key_grad, value_grad])
    qkv_part = jnp.einsum("td,ith->idh", tokens_a, stacked, preferred_element_type=f32)
    attention_input_gradient = owned_rows(
        jnp.einsum("ith,idh->td", stacked, qkv_back, preferred_element_type=f32)
    )
    attention_norm_backward, attention_gain_partial, attention_shift_partial = norm_backward(
        attention_input_gradient,
        attention_standardized,
        attention_inverse_deviation,
        attention_gain_gradient,
    )
    input_grad = middle_grad + attention_norm_backward
    qkv_grad, proj_grad, router_grad, norm_grads = reduce_dense(
        qkv_part,
        proj_part,
        router_part,
        [attention_gain_partial, attention_shift_partial, expert_gain_partial, expert_shift_partial],
    )
    return (
        outputs,
        input_grad,
        norm_grads[0],
        norm_grads[1],
        qkv_grad,
        proj_grad,
        norm_grads[2],
        norm_grads[3],
        router_grad,
        in_grad,
        out_grad,
    )


def solution(mesh):
    fsdp = mesh.shape["fsdp"]
    sub = Mesh(
        mesh.devices.reshape(EXPERTS, fsdp // EXPERTS, mesh.shape["tp"]), ("fa", "fb", "tp")
    )
    return jax.shard_map(
        per_device,
        mesh=sub,
        in_specs=(
            P(("fa", "fb", "tp"), None),
            P(("fa", "fb"), None),
            P(("fa", "fb")),
            P(("fa", "fb")),
            P(None, ("fa", "fb"), "tp"),
            P("tp", ("fa", "fb")),
            P(("fa", "fb")),
            P(("fa", "fb")),
            P(("fa", "fb"), None),
            P(("fa", "fb"), None, "tp"),
            P(("fa", "fb"), None, "tp"),
            P(("fa", "fb", "tp"), None),
        ),
        out_specs=(
            P(("fa", "fb", "tp"), None),
            P(("fa", "fb", "tp"), None),
            P(("fa", "fb")),
            P(("fa", "fb")),
            P(None, ("fa", "fb"), "tp"),
            P("tp", ("fa", "fb")),
            P(("fa", "fb")),
            P(("fa", "fb")),
            P(("fa", "fb"), None),
            P(("fa", "fb"), None, "tp"),
            P(("fa", "fb"), None, "tp"),
        ),
        check_vma=False,
    )
```
